32 devices in a mesh: segment: 4 (over y, core), expert: 8 (over z, x).
Axes of the slice: x: 2, y: 2, z: 4, core: 2. Of those that a mesh axis runs over, the one named last changes fastest.
Arguments:
- state: bfloat16 [4, 64, 2048], P('segment', 'expert'), may hold values from -24 to 24
- routes: int32 [4, 4, 64, 2], P(None, 'segment', 'expert'), may hold values from 0 to 3, all different within a row; in each aligned block of 8 rows (0 to 7, 8 to 15, ..., all dimensions but the last counted through in order) at most 6 rows name the same one
- gates: float32 [4, 4, 64, 2], P(None, 'segment', 'expert'), may hold values from 0.2 to 1
- norm_gain: float32 [2, 4, 2048], P(None, 'segment'), may hold values from 0.25 to 1.75
- w_gate: bfloat16 [2, 4, 5120, 2048], P(None, 'segment', 'expert'), may hold values from -0.125 to 0.125
- w_up: bfloat16 [2, 4, 5120, 2048], P(None, 'segment', 'expert'), may hold values from -0.125 to 0.125
- w_down: bfloat16 [2, 4, 5120, 2048], P(None, 'segment', 'expert'), may hold values from -0.15625 to 0.15625
- spare_gate: bfloat16 [2, 4, 1280, 2048], P(None, 'segment', 'expert'), may hold values from -0.125 to 0.125
- spare_up: bfloat16 [2, 4, 1280, 2048], P(None, 'segment', 'expert'), may hold values from -0.125 to 0.125
- spare_down: bfloat16 [2, 4, 1280, 2048], P(None, 'segment', 'expert'), may hold values from -0.15625 to 0.15625
Outputs:
- final: bfloat16 [4, 64, 2048], P('segment', 'expert')
The draws below stay inside these ranges and needn't reach their ends.
Inputs may be any that keep to these rules, and one draw needn't show every extreme that they name: `routes`: each row names 2 different experts. Within the 8 rows of one device at one tick (aligned blocks), no expert is named by more than 6 rows, and some blocks reach 6.
All inputs are finite; a program needn't handle non-finite values.
Results may differ from the reference program's by a relative error of at most 0.012.
Values may be sent and summed in bfloat16 or wider, within the bound.
No kernel may reach another device: no remote copies, remote signals or barrier semaphores. Data moves between devices by JAX's collectives and lax.ppermute only.
A program may use at most 64 MiB of HBM per device.

```python
import math
import jax
import jax.numpy as jnp
import numpy as np
from jax import lax

D = 2048
FE = 1280
EXPERTS = 4
TOPK = 2
TICKS = 4
TOK_DEV = 8
MOST = 6
CAP = 4
SEGMENTS = 4
TOKENS = 64
N_SEGMENT = 4
N_EXPERT = 8


def draw_state(key, part):
    base_key, column_key, row_key = jax.random.split(jax.random.fold_in(key, 11), 3)
    shape = (N_SEGMENT, TOKENS, D)
    base = jax.random.normal(base_key, shape, jnp.float32)
    columns = jnp.exp(jax.random.uniform(column_key, (D,), jnp.float32, math.log(0.3), math.log(3.0)))
    rows = jnp.exp(jax.random.uniform(row_key, (N_SEGMENT, TOKENS, 1), jnp.float32, math.log(0.5), math.log(2.0)))
    values = base * columns * rows
    return jnp.clip(values, -24.0, 24.0).astype(jnp.bfloat16)


def block_levels(rng, extent, cuts, smallest, high):
    factor_of = 1.0
    for dim, shards_of in cuts:
        steps = jax.random.uniform(jax.random.fold_in(jax.random.fold_in(rng, 6), dim), (shards_of,), jnp.float32, smallest / len(cuts), high / len(cuts))
        factor_of = factor_of * jnp.repeat(jnp.exp(steps), extent[dim] // shards_of).reshape((-1,) + (1,) * (len(extent) - 1 - dim))
    return factor_of


def deal_out(own_key, own, number, rows, number_of, top, limit, skew):
    ranking = jax.random.permutation(own_key, number_of)
    crowded, ordinary = portions_of(number_of, rows * top, limit, skew, True), portions_of(number_of, rows * top, limit, skew, False)
    places = jnp.arange(number_of)

    def named(tallies, rotation):
        used = int((tallies > 0).sum())
        fixed = max(1, used // 4)
        passed = fixed + (places - fixed + rotation * (used - fixed)) % max(1, number_of - fixed)
        return jnp.zeros((number_of,), jnp.int32).at[ranking[jnp.where(places < fixed, places, passed)]].set(jnp.asarray(tallies, jnp.int32))

    tallies = jnp.where(number % 4 == 0, named(crowded, number // 4), named(ordinary, number - number // 4 - 1))
    mixed = jax.random.permutation(jax.random.fold_in(own, 3), number_of)
    donor, sink = mixed[0:number_of // 2 * 2:2], mixed[1:number_of // 2 * 2:2]
    slack = jnp.minimum(tallies[donor] - 1, limit - tallies[sink]) // 2
    slack = jnp.where((donor == ranking[0]) | (sink == ranking[0]) | (tallies[sink] == 0), 0, jnp.maximum(slack, 0))
    passed = jax.random.randint(jax.random.fold_in(own, 4), (number_of // 2,), 0, 1 << 20) % (slack + 1)
    tallies = tallies.at[donor].add(-passed).at[sink].add(passed)
    items = jnp.searchsorted(jnp.cumsum(tallies), jnp.arange(rows * top), side="right").astype(jnp.int32)
    table = items.reshape(top, rows).T
    table = table[jax.random.permutation(jax.random.fold_in(own, 1), rows)]
    rotation = jax.random.randint(jax.random.fold_in(own, 2), (rows, 1), 0, top)
    return jnp.take_along_axis(table, (jnp.arange(top)[None, :] + rotation) % top, axis=1)


def portions_of(amount, total, reach, lean, full):
    loads = [(1 << 20) // math.isqrt(standing ** lean) + 1 for standing in range(1, amount + 1)]
    largest = reach if full else min(reach, max(-(-total // amount), total * loads[0] // sum(loads)))
    least = 1 if total - largest >= amount - 1 else 0
    counts, spare = [largest] + [least] * (amount - 1), total - largest - least * (amount - 1)
    while spare > 0:
        free = [i for i in range(1, amount) if counts[i] < largest] or [i for i in range(1, amount) if counts[i] < reach]
        whole, remaining = sum([loads[i] for i in free]), spare
        for i in free:
            extra = min(reach - counts[i], max(1, remaining * loads[i] // whole), spare)
            counts[i] = counts[i] + extra
            spare = spare - extra
    return np.array(counts)


def centred(key, extent, width, most, cuts=(), kind=jnp.bfloat16):
    values = jax.random.normal(key, extent, jnp.float32) * width
    if len(cuts) > 0:
        values = block_levels(key, extent, cuts, -0.22, 0.18) * values
    return jnp.clip(values, min=-most, max=most).astype(kind)


def setup_inputs(seed: int = 0) -> dict:
    key_of = jax.random.split(jax.random.key(seed), 11)
    state = draw_state(jax.random.fold_in(key_of[10], 71), 0)
    routes_keys = jax.random.split(jax.random.fold_in(key_of[1], 1), TICKS * SEGMENTS * TOKENS // TOK_DEV)
    routes_turns = jax.random.permutation(jax.random.fold_in(key_of[1], 3), TICKS * SEGMENTS * TOKENS // TOK_DEV)
    routes = jax.vmap(lambda own, number: deal_out(jax.random.fold_in(key_of[1], 2), own, number, TOK_DEV, EXPERTS, TOPK, MOST, 2))(routes_keys, routes_turns).reshape((TICKS, SEGMENTS, TOKENS, TOPK))
    gates = jnp.clip(jnp.exp(math.log(1.0) - 1.609438 * jax.random.uniform(key_of[2], (TICKS, SEGMENTS, TOKENS, TOPK), jnp.float32) ** block_levels(key_of[2], (TICKS, SEGMENTS, TOKENS, TOPK), ((1, 4), (2, 8)), -0.2, 0.2)), 0.2, 1.0)
    norm_gain = jnp.clip(1.0 + 0.15 * jax.random.normal(key_of[3], (2, SEGMENTS, D), jnp.float32), 0.25, 1.75)
    w_gate = centred(key_of[4], (2, SEGMENTS, EXPERTS * FE, D), D ** -0.5, 0.125, ((1, 4), (2, 8)))
    w_up = centred(key_of[5], (2, SEGMENTS, EXPERTS * FE, D), D ** -0.5, 0.125, ((1, 4), (2, 8)))
    w_down = centred(key_of[6], (2, SEGMENTS, EXPERTS * FE, D), FE ** -0.5, 0.15625, ((1, 4), (2, 8)))
    spare_gate = centred(key_of[7], (2, SEGMENTS, FE, D), D ** -0.5, 0.125, ((1, 4), (2, 8)))
    spare_up = centred(key_of[8], (2, SEGMENTS, FE, D), D ** -0.5, 0.125, ((1, 4), (2, 8)))
    spare_down = centred(key_of[9], (2, SEGMENTS, FE, D), FE ** -0.5, 0.15625, ((1, 4), (2, 8)))
    return dict(state=state, routes=routes, gates=gates, norm_gain=norm_gain, w_gate=w_gate, w_up=w_up, w_down=w_down, spare_gate=spare_gate, spare_up=spare_up, spare_down=spare_down)


EPSILON = 1e-06

def rms_normed(rows, norm_scale):
    values = rows.astype(jnp.float32)
    row_scale = lax.rsqrt(lax.optimization_barrier(jnp.mean(values * values, axis=-1, keepdims=True)) + EPSILON)
    return (values * row_scale * norm_scale).astype(jnp.bfloat16)

def expert_output(normed, gate_rows, up_rows, down_rows, split_count):
    row_count = normed.shape[0]
    hidden_part = gate_rows.shape[0] // split_count
    gate_pre = jnp.dot(normed, gate_rows.astype(jnp.float32).T, precision=lax.Precision.HIGHEST)
    up_pre = jnp.dot(normed, up_rows.astype(jnp.float32).T, precision=lax.Precision.HIGHEST)
    hidden = lax.optimization_barrier((jax.nn.silu(gate_pre) * up_pre).astype(jnp.bfloat16)).astype(jnp.float32)
    pieces = hidden.reshape(row_count, split_count, hidden_part)
    down_pieces = down_rows.astype(jnp.float32).reshape(split_count, hidden_part, D)
    partial_value = jnp.einsum('tph,phd->tpd', pieces, down_pieces, precision=lax.Precision.HIGHEST)
    partial_value = lax.optimization_barrier(partial_value.astype(jnp.bfloat16)).astype(jnp.float32)
    return lax.optimization_barrier(jnp.sum(partial_value, axis=1))

def moe_layer(current, chosen, weights, norm_scale, gate_all, up_all, down_all, spare_g, spare_u, spare_d):
    normed = rms_normed(current, norm_scale).astype(jnp.float32)
    split_count = N_EXPERT // EXPERTS
    labels = jnp.arange(EXPERTS, dtype=jnp.int32)
    member = jnp.any(chosen[:, :, None] == labels[None, None, :], axis=1)
    taken = member.astype(jnp.int32).reshape(-1, TOK_DEV, EXPERTS)
    position = (jnp.cumsum(taken, axis=1, dtype=jnp.int32) - taken).reshape(-1, EXPERTS)
    combined = jnp.zeros(current.shape, jnp.float32)
    spill = jnp.zeros((current.shape[0],), jnp.float32)
    for expert_idx in range(EXPERTS):
        low = expert_idx * FE
        output = expert_output(normed, gate_all[low:low + FE], up_all[low:low + FE], down_all[low:low + FE], split_count)
        whole = lax.optimization_barrier(jnp.sum(jnp.where(chosen == expert_idx, weights, jnp.float32(0.0)), axis=1))
        inside = position[:, expert_idx] < CAP
        share = jnp.where(inside, whole, jnp.float32(0.0))
        spill = spill + jnp.where(inside, jnp.float32(0.0), whole)
        combined = combined + share[:, None] * output
    spare_out = expert_output(normed, spare_g, spare_u, spare_d, N_EXPERT)
    combined = combined + spill[:, None] * spare_out
    return (current.astype(jnp.float32) + combined).astype(jnp.bfloat16)

def select_layer(table, group_idx, segment_idx):
    inner = lax.dynamic_index_in_dim(table, group_idx, 0, keepdims=False)
    return lax.dynamic_index_in_dim(inner, segment_idx, 0, keepdims=False)

def reference(state, routes, gates, norm_gain, w_gate, w_up, w_down, spare_gate, spare_up, spare_down):
    current = state
    for tick_idx in range(TICKS):

        def one_segment(segment_idx):
            start_segment = (segment_idx - tick_idx) % N_SEGMENT
            first_group = jnp.where((start_segment % 2 == 1) & (start_segment + TICKS <= N_SEGMENT), 1, 0)
            group_idx = (first_group + jnp.where(start_segment + tick_idx >= N_SEGMENT, 1, 0)).astype(jnp.int32)
            holder = ((segment_idx + 1) % N_SEGMENT).astype(jnp.int32)
            return moe_layer(current[segment_idx], routes[tick_idx, segment_idx], gates[tick_idx, segment_idx], select_layer(norm_gain, group_idx, segment_idx), select_layer(w_gate, group_idx, segment_idx), select_layer(w_up, group_idx, segment_idx), select_layer(w_down, group_idx, segment_idx), select_layer(spare_gate, group_idx, holder), select_layer(spare_up, group_idx, holder), select_layer(spare_down, group_idx, holder))
        updated = lax.map(one_segment, jnp.arange(N_SEGMENT, dtype=jnp.int32))
        if tick_idx + 1 < TICKS:
            current = jnp.roll(updated, 1, axis=0)
        else:
            current = updated
    return current
```

```python
import functools

import jax
import jax.numpy as jnp
from jax import lax
from jax.experimental import pallas as pl
from jax.experimental.pallas import tpu as pltpu
from jax.sharding import PartitionSpec as P

EXPERTS = 4
TICKS = 4
CAP = 4
LANES = 128


EPSILON = 1e-06


def from_behind(value, axis, steps):
    count = lax.axis_size(axis)
    pairs = [(source, (source + steps) % count) for source in range(count)]
    return lax.ppermute(value, axis, pairs)


def group_of(section, tick_idx, segments):
    start_segment = (section - tick_idx) % segments
    first_group = jnp.where((start_segment % 2 == 1) & (start_segment + TICKS <= segments), 1, 0)
    return (first_group + jnp.where(start_segment + tick_idx >= segments, 1, 0)).astype(jnp.int32)


def groups_at(tick_idx, segments):
    found = set()
    for section in range(segments):
        start = (section - tick_idx) % segments
        first = 1 if start % 2 == 1 and start + TICKS <= segments else 0
        found.add(first + (1 if start + tick_idx >= segments else 0))
    return found


def coefficients(routes, gates):
    labels = jnp.arange(EXPERTS, dtype=jnp.int32)
    matches = routes[..., None] == labels
    routed = jnp.sum(jnp.where(matches, gates[..., None], jnp.float32(0.0)), axis=2)
    member = jnp.any(matches, axis=2)
    rows = routes.shape[1]
    earlier = jnp.arange(rows)[None, :] < jnp.arange(rows)[:, None]
    position = jnp.sum(jnp.where(earlier[None, :, :, None] & member[:, None, :, :], 1, 0), axis=2)
    inside = member & (position < CAP)
    share = jnp.where(inside, routed, jnp.float32(0.0))
    spill = jnp.sum(jnp.where(inside, jnp.float32(0.0), routed), axis=2, keepdims=True)
    table = jnp.concatenate([share, spill], axis=2)
    table = jnp.transpose(table, (1, 0, 2)).reshape(rows, -1)
    high = lax.reduce_precision(table, 8, 7)
    low = table - high
    both = jnp.concatenate([high, low], axis=1).astype(jnp.bfloat16)
    return jnp.pad(both, ((0, 0), (0, LANES - both.shape[1])))


def layer_kernel(
    scalars, x_ref, table_ref, gain_ref, gate_ref, up_ref, down_ref, sg_ref, su_ref, sd_ref, out_ref,
    *, tick_idx, slices, slices_out, tok_dev, with_residual
):
    group, expert, member, spare_group = scalars[0], scalars[1], scalars[2], scalars[3]
    if slices == 1:
        x = x_ref[...]
    else:
        x = jnp.concatenate([x_ref[i] for i in range(slices)], axis=1)
    values = x.astype(jnp.float32)
    row_scale = lax.rsqrt(jnp.mean(values * values, axis=-1, keepdims=True) + EPSILON)
    normed = (values * row_scale * gain_ref[group]).astype(jnp.bfloat16)
    table = table_ref[...].astype(jnp.float32)
    lane = lax.broadcasted_iota(jnp.int32, table.shape, 1)
    width = TICKS * (EXPERTS + 1)

    def column(at):
        return jnp.sum(jnp.where((lane == at) | (lane == at + width), table, 0.0), axis=1, keepdims=True)

    share = column(tick_idx * (EXPERTS + 1) + expert)
    spill = column(tick_idx * (EXPERTS + 1) + EXPERTS)
    contract = (((1,), (1,)), ((), ()))

    def served(gate, up, down):
        gate_pre = lax.dot_general(normed, gate, contract, preferred_element_type=jnp.float32)
        up_pre = lax.dot_general(normed, up, contract, preferred_element_type=jnp.float32)
        hidden = (gate_pre / (1.0 + jnp.exp(-gate_pre)) * up_pre).astype(jnp.bfloat16)
        return jnp.dot(hidden, down, preferred_element_type=jnp.float32)

    total = share * served(gate_ref[group], up_ref[group], down_ref[group])
    total = total + spill * served(sg_ref[spare_group], su_ref[spare_group], sd_ref[spare_group])
    if with_residual:
        row = lax.broadcasted_iota(jnp.int32, (x.shape[0], 1), 0)
        total = total + jnp.where(row // tok_dev == member, values, 0.0)
    total = total.astype(jnp.bfloat16)
    if slices_out == 1:
        out_ref[...] = total
    else:
        part = total.shape[1] // slices_out
        for i in range(slices_out):
            out_ref[i] = total[:, i * part:(i + 1) * part]


def run_layer(scalars, x, table, gain, weights, spares, *, tick_idx, slices_out, tok_dev, with_residual):
    slices = 1 if x.ndim == 2 else x.shape[0]
    rows = table.shape[0]
    width = gain.shape[-1]
    out = (rows, width) if slices_out == 1 else (slices_out, rows, width // slices_out)
    whole = pl.BlockSpec(memory_space=pltpu.VMEM)
    hidden = weights[0].shape[1] + spares[0].shape[1]
    return pl.pallas_call(
        functools.partial(
            layer_kernel, tick_idx=tick_idx, slices=slices, slices_out=slices_out, tok_dev=tok_dev,
            with_residual=with_residual,
        ),
        out_shape=jax.ShapeDtypeStruct(out, jnp.bfloat16),
        in_specs=[pl.BlockSpec(memory_space=pltpu.SMEM)] + [whole] * 9,
        out_specs=whole,
        compiler_params=pltpu.CompilerParams(vmem_limit_bytes=16 * 1024 * 1024),
        cost_estimate=pl.CostEstimate(
            flops=6 * rows * hidden * width, bytes_accessed=6 * hidden * width, transcendentals=rows * hidden
        ),
        name="layer",
    )(scalars, x, table, gain, *weights, *spares)


def on_device(
    state, routes, gates, norm_gain, w_gate, w_up, w_down, spare_gate, spare_up, spare_down
):
    segments = lax.axis_size("segment")
    segment_idx = lax.axis_index("segment")
    members = lax.axis_size("expert")
    member_idx = lax.axis_index("expert")
    split_count = members // EXPERTS
    tok_dev = state.shape[1]
    width = state.shape[2]
    rows = members * tok_dev
    part = width // segments
    everyone = ("segment", "expert")

    spare_stack = [spare_gate[:, 0], spare_up[:, 0], spare_down[:, 0]]
    first = [[from_behind(one[0], "segment", -1) for one in spare_stack]]

    sent = jnp.concatenate([state[0], coefficients(routes[:, 0], gates[:, 0])], axis=1)
    sent = jnp.broadcast_to(sent[None], (members,) + sent.shape)
    arrived = lax.all_to_all(sent, "expert", split_axis=0, concat_axis=0, tiled=True)
    arrived = arrived.reshape(rows, -1)
    x = arrived[:, :width]
    table = arrived[:, width:]

    weights = [w_gate[:, 0], w_up[:, 0], w_down[:, 0]]
    gain = norm_gain
    held = None
    second = None
    for tick_idx in range(TICKS):
        needed = groups_at(tick_idx, segments)
        if second is None and needed != {0}:
            second = [from_behind(one[1], "segment", -1) for one in spare_stack]
        group_idx = group_of(segment_idx, tick_idx, segments)
        if second is None:
            spares = [one[None] for one in first[0]]
            spare_at = jnp.int32(0)
        else:
            spares = [jnp.stack([one, two]) for one, two in zip(first[0], second)]
            spare_at = group_idx
        scalars = jnp.stack(
            [group_idx, (member_idx // split_count).astype(jnp.int32), member_idx.astype(jnp.int32), spare_at]
        )
        last = tick_idx + 1 == TICKS
        partial_sum = run_layer(
            scalars, x, table, gain, weights, spares, tick_idx=tick_idx,
            slices_out=1 if last else segments, tok_dev=tok_dev, with_residual=tick_idx == 0,
        )
        if last:
            returned = lax.all_to_all(
                partial_sum.reshape(members, tok_dev, width), "expert", split_axis=0, concat_axis=0, tiled=True
            )
            mine = x.reshape(segments, members, tok_dev, part)
            mine = lax.dynamic_index_in_dim(mine, member_idx, 1, keepdims=False)
            mine = jnp.transpose(mine, (1, 0, 2)).reshape(tok_dev, width)
            total = jnp.sum(returned.astype(jnp.float32), axis=0) + mine.astype(jnp.float32)
            return total.astype(jnp.bfloat16)[None]
        returned = lax.all_to_all(
            partial_sum.reshape(segments * members, tok_dev, part), everyone, split_axis=0, concat_axis=0, tiled=True
        )
        total = jnp.sum(returned.reshape(segments, members, tok_dev, part).astype(jnp.float32), axis=1)
        if held is not None:
            total = total + held.astype(jnp.float32)
        held = jnp.roll(total.astype(jnp.bfloat16), 1, axis=0)
        sent = jnp.broadcast_to(held[:, None], (segments, members, tok_dev, part))
        x = lax.all_to_all(
            sent.reshape(segments * members, tok_dev, part), everyone, split_axis=0, concat_axis=0, tiled=True
        ).reshape(segments, rows, part)


def solution(mesh):
    return jax.shard_map(
        on_device,
        mesh=mesh,
        in_specs=(
            P("segment", "expert", None),
            P(None, "segment", "expert", None),
            P(None, "segment", "expert", None),
            P(None, "segment", None),
            P(None, "segment", "expert", None),
            P(None, "segment", "expert", None),
            P(None, "segment", "expert", None),
            P(None, "segment", "expert", None),
            P(None, "segment", "expert", None),
            P(None, "segment", "expert", None),
        ),
        out_specs=P("segment", "expert", None),
        check_vma=False,
    )
```

```python
import functools

import jax
import jax.numpy as jnp
from jax import lax
from jax.experimental import pallas as pl
from jax.experimental.pallas import tpu as pltpu
from jax.sharding import PartitionSpec as P

EXPERTS = 4
TICKS = 4
CAP = 4
LANES = 128
BOTH = ("segment", "expert")


EPSILON = 1e-06


def moved(value, flip, steps):
    segments, members = lax.axis_size("segment"), lax.axis_size("expert")
    pairs = [
        (section * members + member, (section + steps) % segments * members + (member ^ flip))
        for section in range(segments)
        for member in range(members)
    ]
    return lax.ppermute(value, BOTH, pairs)


def group_of(section, tick_idx, segments):
    start_segment = (section - tick_idx) % segments
    first_group = jnp.where((start_segment % 2 == 1) & (start_segment + TICKS <= segments), 1, 0)
    return (first_group + jnp.where(start_segment + tick_idx >= segments, 1, 0)).astype(jnp.int32)


def groups_at(tick_idx, segments):
    found = set()
    for section in range(segments):
        start = (section - tick_idx) % segments
        first = 1 if start % 2 == 1 and start + TICKS <= segments else 0
        found.add(first + (1 if start + tick_idx >= segments else 0))
    return found


def coefficients(routes, gates):
    labels = jnp.arange(EXPERTS, dtype=jnp.int32)
    matches = routes[..., None] == labels
    routed = jnp.sum(jnp.where(matches, gates[..., None], jnp.float32(0.0)), axis=2)
    member = jnp.any(matches, axis=2)
    rows = routes.shape[1]
    earlier = jnp.arange(rows)[None, :] < jnp.arange(rows)[:, None]
    position = jnp.sum(jnp.where(earlier[None, :, :, None] & member[:, None, :, :], 1, 0), axis=2)
    inside = member & (position < CAP)
    share = jnp.where(inside, routed, jnp.float32(0.0))
    spill = jnp.sum(jnp.where(inside, jnp.float32(0.0), routed), axis=2, keepdims=True)
    table = jnp.concatenate([share, spill], axis=2)
    table = jnp.transpose(table, (1, 0, 2)).reshape(rows, -1)
    high = lax.reduce_precision(table, 8, 7)
    low = table - high
    both = jnp.concatenate([high, low], axis=1).astype(jnp.bfloat16)
    return jnp.pad(both, ((0, 0), (0, LANES - both.shape[1])))


def layer_kernel(scalars, *refs, tick_idx, blocks, spare_count, tok_dev):
    x_refs, refs = refs[:blocks], refs[blocks:]
    table_ref, gain_ref, gate_ref, up_ref, down_ref = refs[:5]
    spare_refs, refs = refs[5:5 + spare_count], refs[5 + spare_count:]
    out_refs, (total_ref,) = refs[:blocks], refs[blocks:]
    group, expert = scalars[0], scalars[1]
    x = jnp.concatenate([x_ref[...] for x_ref in x_refs], axis=0)
    values = x.astype(jnp.float32)
    row_scale = lax.rsqrt(jnp.mean(values * values, axis=-1, keepdims=True) + EPSILON)
    normed = (values * row_scale * gain_ref[group]).astype(jnp.bfloat16)
    table = table_ref[...].astype(jnp.float32)
    lane = lax.broadcasted_iota(jnp.int32, table.shape, 1)
    width = TICKS * (EXPERTS + 1)

    def column(at):
        return jnp.sum(jnp.where((lane == at) | (lane == at + width), table, 0.0), axis=1, keepdims=True)

    share = column(tick_idx * (EXPERTS + 1) + expert)
    spill = column(tick_idx * (EXPERTS + 1) + EXPERTS)
    contract = (((1,), (1,)), ((), ()))

    def served(gate, up, down):
        gate_pre = lax.dot_general(normed, gate, contract, preferred_element_type=jnp.float32)
        up_pre = lax.dot_general(normed, up, contract, preferred_element_type=jnp.float32)
        hidden = (gate_pre / (1.0 + jnp.exp(-gate_pre)) * up_pre).astype(jnp.bfloat16)
        return jnp.dot(hidden, down, preferred_element_type=jnp.float32)

    total_ref[...] = share * served(gate_ref[group], up_ref[group], down_ref[group])
    for at, spare_ref in enumerate(spare_refs):

        def add(spare_ref=spare_ref):
            total_ref[...] += spill * served(spare_ref[0], spare_ref[1], spare_ref[2])

        if spare_count == 1:
            add()
        else:
            pl.when(group == at)(add)
    per = 2 * tok_dev
    first = total_ref[0:per, :]
    row = lax.broadcasted_iota(jnp.int32, (per, 1), 0)
    out_refs[0][...] = first + jnp.where(row < tok_dev, values[0:per], 0.0)
    for i in range(1, blocks):
        out_refs[i][...] = total_ref[i * per:(i + 1) * per, :].astype(jnp.bfloat16)


def run_layer(scalars, x_blocks, table, gain, weights, spares, *, tick_idx, tok_dev):
    blocks = len(x_blocks)
    rows = table.shape[0]
    width = gain.shape[-1]
    per = rows // blocks
    whole = pl.BlockSpec(memory_space=pltpu.VMEM)
    hidden = weights[0].shape[1] + spares[0].shape[1]
    return pl.pallas_call(
        functools.partial(
            layer_kernel, tick_idx=tick_idx, blocks=blocks, spare_count=len(spares), tok_dev=tok_dev
        ),
        out_shape=[jax.ShapeDtypeStruct((per, width), jnp.float32)]
        + [jax.ShapeDtypeStruct((per, width), jnp.bfloat16)] * (blocks - 1),
        in_specs=[pl.BlockSpec(memory_space=pltpu.SMEM)] + [whole] * (blocks + 5 + len(spares)),
        out_specs=[whole] * blocks,
        scratch_shapes=[pltpu.VMEM((rows, width), jnp.float32)],
        compiler_params=pltpu.CompilerParams(vmem_limit_bytes=16 * 1024 * 1024),
        cost_estimate=pl.CostEstimate(
            flops=6 * rows * hidden * width, bytes_accessed=6 * hidden * width, transcendentals=rows * hidden
        ),
        name="layer",
    )(scalars, *x_blocks, table, gain, *weights, *spares)


def pick_kernel(gate_ref, up_ref, down_ref, out_ref, sems, *, group):
    copies = [
        pltpu.make_async_copy(ref.at[group], out_ref.at[i], sems.at[i])
        for i, ref in enumerate((gate_ref, up_ref, down_ref))
    ]
    for copy in copies:
        copy.start()
    for copy in copies:
        copy.wait()


def picked(spares, group):
    return pl.pallas_call(
        functools.partial(pick_kernel, group=group),
        out_shape=jax.ShapeDtypeStruct((3,) + spares[0].shape[1:], spares[0].dtype),
        in_specs=[pl.BlockSpec(memory_space=pl.ANY)] * 3,
        out_specs=pl.BlockSpec(memory_space=pltpu.VMEM),
        scratch_shapes=[pltpu.SemaphoreType.DMA((3,))],
        name="pick",
    )(*spares)


def widest_first(outer):
    return range(outer - 1, 0, -1)


def added(values):
    total = values[0].astype(jnp.float32)
    for value in values[1:]:
        total = total + value.astype(jnp.float32)
    return total


def on_device(
    state, routes, gates, norm_gain, w_gate, w_up, w_down, spare_gate, spare_up, spare_down
):
    segments = lax.axis_size("segment")
    segment_idx = lax.axis_index("segment")
    members = lax.axis_size("expert")
    member_idx = lax.axis_index("expert")
    split_count = members // EXPERTS
    outer = members // 2
    assert outer & (outer - 1) == 0
    tok_dev = state.shape[1]
    width = state.shape[2]

    def spread(value):
        got = {j: moved(value, 2 * j, 0) for j in widest_first(outer)}
        return [value] + [got[j] for j in range(1, outer)]

    weights = [w_gate[:, 0], w_up[:, 0], w_down[:, 0]]
    spare_all = [spare_gate[:, 0], spare_up[:, 0], spare_down[:, 0]]
    spares = [moved(picked(spare_all, 0), 0, -1)]

    own = jnp.concatenate([state[0], coefficients(routes[:, 0], gates[:, 0])], axis=1)
    pair = jnp.concatenate([own, moved(own, 1, 0)], axis=0)
    arrived = spread(pair)
    x_blocks = [one[:, :width] for one in arrived]
    table = jnp.concatenate([one[:, width:] for one in arrived], axis=0)

    early = own
    for tick_idx in range(TICKS):
        group_idx = group_of(segment_idx, tick_idx, segments)
        if len(spares) == 1 and groups_at(tick_idx, segments) != {0}:
            spares.append(moved(picked(lax.optimization_barrier((*spare_all, early))[:3], 1), 0, -1))
        early = x_blocks[0]
        scalars = jnp.stack([group_idx, (member_idx // split_count).astype(jnp.int32)])
        parts = run_layer(
            scalars, x_blocks, table, norm_gain, weights, spares, tick_idx=tick_idx, tok_dev=tok_dev
        )
        got = [moved(parts[j], 2 * j, 0) for j in widest_first(outer)]
        total = added([parts[0]] + got)
        if tick_idx + 1 == TICKS:
            other = moved(total[tok_dev:].astype(jnp.bfloat16), 1, 0)
            return added([total[:tok_dev], other]).astype(jnp.bfloat16)[None]
        total = total.astype(jnp.bfloat16)
        across = moved(total, 1, 1)
        along = moved(total, 0, 1)
        across = jnp.concatenate([across[tok_dev:], across[:tok_dev]], axis=0)
        x_blocks = spread(added([along, across]).astype(jnp.bfloat16))


def solution(mesh):
    return jax.shard_map(
        on_device,
        mesh=mesh,
        in_specs=(
            P("segment", "expert", None),
            P(None, "segment", "expert", None),
            P(None, "segment", "expert", None),
            P(None, "segment", None),
            P(None, "segment", "expert", None),
            P(None, "segment", "expert", None),
            P(None, "segment", "expert", None),
            P(None, "segment", "expert", None),
            P(None, "segment", "expert", None),
            P(None, "segment", "expert", None),
        ),
        out_specs=P("segment", "expert", None),
        check_vma=False,
    )
```

```python
import functools

import jax
import jax.numpy as jnp
from jax import lax
from jax.experimental import pallas as pl
from jax.experimental.pallas import tpu as pltpu
from jax.sharding import PartitionSpec as P

EXPERTS = 4
TICKS = 4
CAP = 4
LANES = 128
BOTH = ("segment", "expert")


EPSILON = 1e-06


def moved(value, flip, steps):
    segments, members = lax.axis_size("segment"), lax.axis_size("expert")
    pairs = [
        (section * members + member, (section + steps) % segments * members + (member ^ flip))
        for section in range(segments)
        for member in range(members)
    ]
    return lax.ppermute(value, BOTH, pairs)


def group_of(section, tick_idx, segments):
    start_segment = (section - tick_idx) % segments
    first_group = jnp.where((start_segment % 2 == 1) & (start_segment + TICKS <= segments), 1, 0)
    return (first_group + jnp.where(start_segment + tick_idx >= segments, 1, 0)).astype(jnp.int32)


def groups_at(tick_idx, segments):
    found = set()
    for section in range(segments):
        start = (section - tick_idx) % segments
        first = 1 if start % 2 == 1 and start + TICKS <= segments else 0
        found.add(first + (1 if start + tick_idx >= segments else 0))
    return found


WHOLE = pl.BlockSpec(memory_space=pltpu.VMEM)


def small(kernel, out_shape, *values):
    return pl.pallas_call(
        kernel,
        out_shape=out_shape,
        in_specs=[WHOLE] * len(values),
        out_specs=WHOLE,
        compiler_params=pltpu.CompilerParams(vmem_limit_bytes=2 * 1024 * 1024),
    )(*values)


def prepare_kernel(state_ref, routes_ref, gates_ref, out_ref):
    rows, width = state_ref.shape
    lane = lax.broadcasted_iota(jnp.int32, (rows, LANES), 1)
    columns = EXPERTS + 1
    routed = jnp.zeros((rows, LANES), jnp.float32)
    member = jnp.zeros((rows, LANES), jnp.float32)
    square = (rows, rows)
    diagonal = lax.broadcasted_iota(jnp.int32, square, 0) == lax.broadcasted_iota(jnp.int32, square, 1)

    def upright(line):
        return jnp.sum(jnp.where(diagonal, line, jnp.zeros_like(line)), axis=1, keepdims=True)

    for tick_idx in range(TICKS):
        for choice in range(routes_ref.shape[1]):
            named = lane == upright(routes_ref[tick_idx, choice:choice + 1, :]) + tick_idx * columns
            routed = routed + jnp.where(named, upright(gates_ref[tick_idx, choice:choice + 1, :]), 0.0)
            member = member + jnp.where(named, 1.0, 0.0)
    row = lax.broadcasted_iota(jnp.int32, (rows, LANES), 0)
    position = jnp.zeros((rows, LANES), jnp.float32)
    for earlier in range(rows - 1):
        position = position + jnp.where(row > earlier, member[earlier:earlier + 1, :], 0.0)
    inside = position < CAP
    table = jnp.where(inside, routed, 0.0)
    over = jnp.where(inside, 0.0, routed)
    for tick_idx in range(TICKS):
        low = tick_idx * columns
        spill = jnp.sum(jnp.where((lane >= low) & (lane < low + EXPERTS), over, 0.0), axis=1, keepdims=True)
        table = jnp.where(lane == low + EXPERTS, spill, table)
    high = table.astype(jnp.bfloat16).astype(jnp.float32)
    both = high + pltpu.roll(table - high, TICKS * columns, 1)
    out_ref[:, :width] = state_ref[...]
    out_ref[:, width:] = both.astype(jnp.bfloat16)


def join_kernel(first_ref, second_ref, out_ref):
    out_ref[...] = jnp.concatenate([first_ref[...], second_ref[...]], axis=0)


def layer_kernel(*refs, tick_idx, blocks, spare_count, tok_dev, width):
    x_refs, first_refs, refs = refs[:blocks], refs[blocks:2 * blocks], refs[2 * blocks:]
    gain_ref, gate_ref, up_ref, down_ref = refs[:4]
    spare_refs, refs = refs[4:4 + spare_count], refs[4 + spare_count:]
    out_refs, (total_ref,) = refs[:blocks], refs[blocks:]
    segments, members = lax.axis_size("segment"), lax.axis_size("expert")
    group = group_of(lax.axis_index("segment"), tick_idx, segments)
    expert = lax.axis_index("expert") // (members // EXPERTS)
    x = jnp.concatenate([x_ref[:, :width] for x_ref in x_refs], axis=0)
    values = x.astype(jnp.float32)
    row_scale = lax.rsqrt(jnp.mean(values * values, axis=-1, keepdims=True) + EPSILON)
    normed = (values * row_scale * gain_ref[group]).astype(jnp.bfloat16)
    table = jnp.concatenate([ref[:, width:] for ref in first_refs], axis=0).astype(jnp.float32)
    lane = lax.broadcasted_iota(jnp.int32, table.shape, 1)
    columns = TICKS * (EXPERTS + 1)

    def column(at):
        return jnp.sum(jnp.where((lane == at) | (lane == at + columns), table, 0.0), axis=1, keepdims=True)

    share = column(tick_idx * (EXPERTS + 1) + expert)
    spill = column(tick_idx * (EXPERTS + 1) + EXPERTS)
    contract = (((1,), (1,)), ((), ()))

    def served(gate, up, down):
        gate_pre = lax.dot_general(normed, gate, contract, preferred_element_type=jnp.float32)
        up_pre = lax.dot_general(normed, up, contract, preferred_element_type=jnp.float32)
        hidden = (gate_pre / (1.0 + jnp.exp(-gate_pre)) * up_pre).astype(jnp.bfloat16)
        return jnp.dot(hidden, down, preferred_element_type=jnp.float32)

    total_ref[...] = share * served(gate_ref[group], up_ref[group], down_ref[group])
    for at, spare_ref in enumerate(spare_refs):

        def add(spare_ref=spare_ref):
            total_ref[...] += spill * served(spare_ref[0], spare_ref[1], spare_ref[2])

        if spare_count == 1:
            add()
        else:
            pl.when(group == at)(add)
    per = 2 * tok_dev
    first = total_ref[0:per, :]
    row = lax.broadcasted_iota(jnp.int32, (per, 1), 0)
    out_refs[0][...] = first + jnp.where(row < tok_dev, values[0:per], 0.0)
    for i in range(1, blocks):
        out_refs[i][...] = total_ref[i * per:(i + 1) * per, :].astype(jnp.bfloat16)


def resident(values):
    return [pltpu.with_memory_space_constraint(value, pltpu.VMEM) for value in values]


def run_layer(x_blocks, first_blocks, gain, weights, spares, *, tick_idx, tok_dev):
    blocks = len(x_blocks)
    width = gain.shape[-1]
    per = 2 * tok_dev
    rows = per * blocks
    hidden = weights[0].shape[1] + spares[0].shape[1]
    return pl.pallas_call(
        functools.partial(
            layer_kernel, tick_idx=tick_idx, blocks=blocks, spare_count=len(spares), tok_dev=tok_dev, width=width
        ),
        out_shape=[jax.ShapeDtypeStruct((per, width), jnp.float32)]
        + [jax.ShapeDtypeStruct((per, width), jnp.bfloat16)] * (blocks - 1),
        in_specs=[WHOLE] * (2 * blocks + 4 + len(spares)),
        out_specs=[WHOLE] * blocks,
        scratch_shapes=[pltpu.VMEM((rows, width), jnp.float32)],
        compiler_params=pltpu.CompilerParams(vmem_limit_bytes=12 * 1024 * 1024),
        cost_estimate=pl.CostEstimate(
            flops=6 * rows * hidden * width, bytes_accessed=6 * hidden * width, transcendentals=rows * hidden
        ),
        name="layer",
    )(*x_blocks, *first_blocks, gain, *resident(weights), *resident(spares))


def sum_kernel(*refs, swap):
    total = refs[0][...].astype(jnp.float32)
    half = total.shape[0] // 2
    for ref in refs[1:-1]:
        value = ref[...].astype(jnp.float32)
        total = total + (jnp.concatenate([value[half:], value[:half]], axis=0) if swap else value)
    refs[-1][...] = total.astype(jnp.bfloat16)


def summed(values, swap=False):
    shape = jax.ShapeDtypeStruct(values[0].shape, jnp.bfloat16)
    return small(functools.partial(sum_kernel, swap=swap), shape, *values)


def fill_kernel(*refs, group):
    count = len(refs) // 2
    ins, outs, sems = refs[:count], refs[count:2 * count], refs[2 * count]
    copies = [
        pltpu.make_async_copy(one if group is None else one.at[group], out, sems.at[i])
        for i, (one, out) in enumerate(zip(ins, outs))
    ]
    for copy in copies:
        copy.start()
    for copy in copies:
        copy.wait()


def filled(values, group=None):
    shapes = [value.shape if group is None else value.shape[1:] for value in values]
    return pl.pallas_call(
        functools.partial(fill_kernel, group=group),
        out_shape=[pltpu.VMEM(shape, value.dtype) for shape, value in zip(shapes, values)],
        in_specs=[pl.BlockSpec(memory_space=pltpu.HBM)] * len(values),
        out_specs=[WHOLE] * len(values),
        scratch_shapes=[pltpu.SemaphoreType.DMA((len(values),))],
        compiler_params=pltpu.CompilerParams(vmem_limit_bytes=1024 * 1024),
        name="fill",
    )(*[pltpu.with_memory_space_constraint(value, pltpu.HBM) for value in values])


def stack_kernel(gate_ref, up_ref, down_ref, out_ref, sems, *, group):
    copies = [
        pltpu.make_async_copy(ref.at[group], out_ref.at[i], sems.at[i])
        for i, ref in enumerate((gate_ref, up_ref, down_ref))
    ]
    for copy in copies:
        copy.start()
    for copy in copies:
        copy.wait()


def stacked(spares, group):
    return pl.pallas_call(
        functools.partial(stack_kernel, group=group),
        out_shape=pltpu.VMEM((3,) + spares[0].shape[1:], spares[0].dtype),
        in_specs=[pl.BlockSpec(memory_space=pltpu.HBM)] * 3,
        out_specs=WHOLE,
        scratch_shapes=[pltpu.SemaphoreType.DMA((3,))],
        compiler_params=pltpu.CompilerParams(vmem_limit_bytes=6 * 1024 * 1024),
        name="stack",
    )(*[pltpu.with_memory_space_constraint(value, pltpu.HBM) for value in spares])


def widest_first(outer):
    return range(outer - 1, 0, -1)


def added(values):
    total = values[0].astype(jnp.float32)
    for value in values[1:]:
        total = total + value.astype(jnp.float32)
    return total


def on_device(
    state, routes, gates, norm_gain, w_gate, w_up, w_down, spare_gate, spare_up, spare_down
):
    segments = lax.axis_size("segment")
    members = lax.axis_size("expert")
    outer = members // 2
    assert outer & (outer - 1) == 0
    tok_dev = state.shape[1]

    def spread(value):
        got = {j: moved(value, 2 * j, 0) for j in widest_first(outer)}
        return [value] + [got[j] for j in range(1, outer)]

    weights = [w_gate[:, 0], w_up[:, 0], w_down[:, 0]]
    spare_all = [spare_gate[:, 0], spare_up[:, 0], spare_down[:, 0]]
    sent, state, routes, gates = lax.optimization_barrier((stacked(spare_all, 0), state, routes, gates))
    spares = [moved(sent, 0, -1)]
    shape = (tok_dev, state.shape[2] + LANES)
    own = small(
        prepare_kernel, jax.ShapeDtypeStruct(shape, state.dtype), state[0],
        jnp.transpose(routes[:, 0], (0, 2, 1)), jnp.transpose(gates[:, 0], (0, 2, 1)),
    )
    other = moved(own, 1, 0)
    pair = small(join_kernel, jax.ShapeDtypeStruct((2 * tok_dev, shape[1]), state.dtype), own, other)
    arrived = spread(pair)
    weights = filled(weights)
    x_blocks = arrived
    late = stacked(lax.optimization_barrier((*spare_all, arrived[1]))[:3], 1)
    for tick_idx in range(TICKS):
        needed = groups_at(tick_idx, segments)
        if tick_idx == 0 and needed != {0}:
            spares.append(moved(late, 0, -1))
        parts = run_layer(x_blocks, arrived, norm_gain, weights, spares, tick_idx=tick_idx, tok_dev=tok_dev)
        got = [moved(parts[j], 2 * j, 0) for j in widest_first(outer)]
        if len(spares) == 1:
            late, _ = lax.optimization_barrier((late, parts[0]))
            spares.append(moved(late, 0, -1))
        if tick_idx + 1 == TICKS:
            total = added([parts[0]] + got)
            other = moved(total[tok_dev:].astype(jnp.bfloat16), 1, 0)
            return added([total[:tok_dev], other]).astype(jnp.bfloat16)[None]
        total = summed([parts[0]] + got)
        across = moved(total, 1, 1)
        along = moved(total, 0, 1)
        x_blocks = spread(summed([along, across], swap=True))


def solution(mesh):
    return jax.shard_map(
        on_device,
        mesh=mesh,
        in_specs=(
            P("segment", "expert", None),
            P(None, "segment", "expert", None),
            P(None, "segment", "expert", None),
            P(None, "segment", None),
            P(None, "segment", "expert", None),
            P(None, "segment", "expert", None),
            P(None, "segment", "expert", None),
            P(None, "segment", "expert", None),
            P(None, "segment", "expert", None),
            P(None, "segment", "expert", None),
        ),
        out_specs=P("segment", "expert", None),
        check_vma=False,
    )
```

```python
import functools

import jax
import jax.numpy as jnp
from jax import lax
from jax.experimental import pallas as pl
from jax.experimental.pallas import tpu as pltpu
from jax.sharding import PartitionSpec as P

EXPERTS = 4
TICKS = 4
CAP = 4
LANES = 128
BOTH = ("segment", "expert")


EPSILON = 1e-06


def moved(value, flip, steps):
    segments, members = lax.axis_size("segment"), lax.axis_size("expert")
    pairs = [
        (section * members + member, (section + steps) % segments * members + (member ^ flip))
        for section in range(segments)
        for member in range(members)
    ]
    return lax.ppermute(value, BOTH, pairs)


def group_of(section, tick_idx, segments):
    start_segment = (section - tick_idx) % segments
    first_group = jnp.where((start_segment % 2 == 1) & (start_segment + TICKS <= segments), 1, 0)
    return (first_group + jnp.where(start_segment + tick_idx >= segments, 1, 0)).astype(jnp.int32)


def groups_at(tick_idx, segments):
    found = set()
    for section in range(segments):
        start = (section - tick_idx) % segments
        first = 1 if start % 2 == 1 and start + TICKS <= segments else 0
        found.add(first + (1 if start + tick_idx >= segments else 0))
    return found


WHOLE = pl.BlockSpec(memory_space=pltpu.VMEM)


def small(kernel, out_shape, *values):
    return pl.pallas_call(
        kernel,
        out_shape=out_shape,
        in_specs=[WHOLE] * len(values),
        out_specs=WHOLE,
        compiler_params=pltpu.CompilerParams(vmem_limit_bytes=2 * 1024 * 1024),
    )(*values)


def prepare_kernel(state_ref, routes_ref, gates_ref, out_ref):
    rows, width = state_ref.shape
    lane = lax.broadcasted_iota(jnp.int32, (rows, LANES), 1)
    columns = EXPERTS + 1
    routed = jnp.zeros((rows, LANES), jnp.float32)
    member = jnp.zeros((rows, LANES), jnp.float32)
    square = (rows, rows)
    diagonal = lax.broadcasted_iota(jnp.int32, square, 0) == lax.broadcasted_iota(jnp.int32, square, 1)

    def upright(line):
        return jnp.sum(jnp.where(diagonal, line, jnp.zeros_like(line)), axis=1, keepdims=True)

    for tick_idx in range(TICKS):
        for choice in range(routes_ref.shape[1]):
            named = lane == upright(routes_ref[tick_idx, choice:choice + 1, :]) + tick_idx * columns
            routed = routed + jnp.where(named, upright(gates_ref[tick_idx, choice:choice + 1, :]), 0.0)
            member = member + jnp.where(named, 1.0, 0.0)
    row = lax.broadcasted_iota(jnp.int32, (rows, LANES), 0)
    position = jnp.zeros((rows, LANES), jnp.float32)
    for earlier in range(rows - 1):
        position = position + jnp.where(row > earlier, member[earlier:earlier + 1, :], 0.0)
    inside = position < CAP
    table = jnp.where(inside, routed, 0.0)
    over = jnp.where(inside, 0.0, routed)
    for tick_idx in range(TICKS):
        low = tick_idx * columns
        spill = jnp.sum(jnp.where((lane >= low) & (lane < low + EXPERTS), over, 0.0), axis=1, keepdims=True)
        table = jnp.where(lane == low + EXPERTS, spill, table)
    high = table.astype(jnp.bfloat16).astype(jnp.float32)
    both = high + pltpu.roll(table - high, TICKS * columns, 1)
    out_ref[:, :width] = state_ref[...]
    out_ref[:, width:] = both.astype(jnp.bfloat16)


def join_kernel(first_ref, second_ref, out_ref):
    out_ref[...] = jnp.concatenate([first_ref[...], second_ref[...]], axis=0)


def served(normed, gate, up, down):
    contract = (((1,), (1,)), ((), ()))
    gate_pre = lax.dot_general(normed, gate, contract, preferred_element_type=jnp.float32)
    up_pre = lax.dot_general(normed, up, contract, preferred_element_type=jnp.float32)
    hidden = (gate_pre / (1.0 + jnp.exp(-gate_pre)) * up_pre).astype(jnp.bfloat16)
    return jnp.dot(hidden, down, preferred_element_type=jnp.float32)


def layer_kernel(*refs, tick_idx, blocks, spare_counts, tok_dev, width, carried, ends):
    x_refs, first_refs, refs = refs[:blocks], refs[blocks:2 * blocks], refs[2 * blocks:]
    gain_ref, refs = refs[0], refs[1:]
    if carried:
        carried_ref, refs = refs[0], refs[1:]
    else:
        (gate_ref, up_ref, down_ref), refs = refs[:3], refs[3:]
    spare_refs = []
    for count in spare_counts:
        spare_refs.append(refs[:count] if count > 1 else [refs[0].at[i] for i in range(refs[0].shape[0])])
        refs = refs[count:]
    segments, members = lax.axis_size("segment"), lax.axis_size("expert")
    group = group_of(lax.axis_index("segment"), tick_idx, segments)
    expert = lax.axis_index("expert") // (members // EXPERTS)
    x = jnp.concatenate([x_ref[:, :width] for x_ref in x_refs], axis=0)
    values = x.astype(jnp.float32)
    row_scale = lax.rsqrt(jnp.mean(values * values, axis=-1, keepdims=True) + EPSILON)
    normed = (values * row_scale * gain_ref[group]).astype(jnp.bfloat16)
    table = jnp.concatenate([ref[:, width:] for ref in first_refs], axis=0).astype(jnp.float32)
    lane = lax.broadcasted_iota(jnp.int32, table.shape, 1)
    columns = TICKS * (EXPERTS + 1)

    def column(at):
        return jnp.sum(jnp.where((lane == at) | (lane == at + columns), table, 0.0), axis=1, keepdims=True)

    total_ref = refs[0] if not ends else refs[-1]
    if carried:
        total_ref[...] = carried_ref[...]
    else:
        share = column(tick_idx * (EXPERTS + 1) + expert)
        total_ref[...] = share * served(normed, gate_ref[group], up_ref[group], down_ref[group])
    for at, spare_ref in enumerate(spare_refs):

        def add(spare_ref=spare_ref):
            spill = column(tick_idx * (EXPERTS + 1) + EXPERTS)
            total_ref[...] += spill * served(normed, *[ref[...] for ref in spare_ref])

        if len(spare_refs) == 1:
            add()
        else:
            pl.when(group == at)(add)
    if not ends:
        return
    out_refs = refs[:blocks]
    per = 2 * tok_dev
    row = lax.broadcasted_iota(jnp.int32, (per, 1), 0)
    out_refs[0][...] = total_ref[0:per, :] + jnp.where(row < tok_dev, values[0:per], 0.0)
    for i in range(1, blocks):
        out_refs[i][...] = total_ref[i * per:(i + 1) * per, :].astype(jnp.bfloat16)


def resident(values):
    return [pltpu.with_memory_space_constraint(value, pltpu.VMEM) for value in values]


def run_layer(x_blocks, first_blocks, gain, weights, spares, *, tick_idx, tok_dev, carried=None, ends=True):
    blocks = len(x_blocks)
    width = gain.shape[-1]
    per = 2 * tok_dev
    rows = per * blocks
    values = [*x_blocks, *first_blocks, gain]
    values += [carried] if carried is not None else resident(weights)
    for spare in spares:
        values += resident(spare)
    hidden = (0 if carried is not None else weights[0].shape[1]) + (spares[0][0].shape[0] if spares else 0)
    whole = jax.ShapeDtypeStruct((rows, width), jnp.float32)
    parts = [jax.ShapeDtypeStruct((per, width), jnp.float32)]
    parts += [jax.ShapeDtypeStruct((per, width), jnp.bfloat16)] * (blocks - 1)
    return pl.pallas_call(
        functools.partial(
            layer_kernel, tick_idx=tick_idx, blocks=blocks, spare_counts=[len(spare) for spare in spares],
            tok_dev=tok_dev, width=width, carried=carried is not None, ends=ends,
        ),
        out_shape=parts if ends else whole,
        in_specs=[WHOLE] * len(values),
        out_specs=[WHOLE] * blocks if ends else WHOLE,
        scratch_shapes=[pltpu.VMEM((rows, width), jnp.float32)] if ends else [],
        compiler_params=pltpu.CompilerParams(vmem_limit_bytes=12 * 1024 * 1024),
        cost_estimate=pl.CostEstimate(
            flops=6 * rows * hidden * width, bytes_accessed=6 * hidden * width, transcendentals=rows * hidden
        ),
        name="layer",
    )(*values)


def sum_kernel(*refs, swap):
    total = refs[0][...].astype(jnp.float32)
    half = total.shape[0] // 2
    for ref in refs[1:-1]:
        value = ref[...].astype(jnp.float32)
        total = total + (jnp.concatenate([value[half:], value[:half]], axis=0) if swap else value)
    refs[-1][...] = total.astype(jnp.bfloat16)


def summed(values, swap=False):
    shape = jax.ShapeDtypeStruct(values[0].shape, jnp.bfloat16)
    return small(functools.partial(sum_kernel, swap=swap), shape, *values)


def fill_kernel(*refs, group):
    count = len(refs) // 2
    ins, outs, sems = refs[:count], refs[count:2 * count], refs[2 * count]
    copies = [
        pltpu.make_async_copy(one if group is None else one.at[group], out, sems.at[i])
        for i, (one, out) in enumerate(zip(ins, outs))
    ]
    for copy in copies:
        copy.start()
    for copy in copies:
        copy.wait()


def filled(values, group=None):
    shapes = [value.shape if group is None else value.shape[1:] for value in values]
    return pl.pallas_call(
        functools.partial(fill_kernel, group=group),
        out_shape=[pltpu.VMEM(shape, value.dtype) for shape, value in zip(shapes, values)],
        in_specs=[pl.BlockSpec(memory_space=pltpu.HBM)] * len(values),
        out_specs=[WHOLE] * len(values),
        scratch_shapes=[pltpu.SemaphoreType.DMA((len(values),))],
        compiler_params=pltpu.CompilerParams(vmem_limit_bytes=1024 * 1024),
        name="fill",
    )(*[pltpu.with_memory_space_constraint(value, pltpu.HBM) for value in values])


def stack_kernel(*refs, group):
    ins, out, sems = refs[:-2], refs[-2], refs[-1]
    copies = [pltpu.make_async_copy(one.at[group], out.at[i], sems.at[i]) for i, one in enumerate(ins)]
    for copy in copies:
        copy.start()
    for copy in copies:
        copy.wait()


def stacked(values, group):
    shape = (len(values),) + values[0].shape[1:]
    return pl.pallas_call(
        functools.partial(stack_kernel, group=group),
        out_shape=pltpu.VMEM(shape, values[0].dtype),
        in_specs=[pl.BlockSpec(memory_space=pltpu.HBM)] * len(values),
        out_specs=WHOLE,
        scratch_shapes=[pltpu.SemaphoreType.DMA((len(values),))],
        compiler_params=pltpu.CompilerParams(vmem_limit_bytes=6 * 1024 * 1024),
        name="stack",
    )(*[pltpu.with_memory_space_constraint(value, pltpu.HBM) for value in values])


def widest_first(outer):
    return range(outer - 1, 0, -1)


def added(values):
    total = values[0].astype(jnp.float32)
    for value in values[1:]:
        total = total + value.astype(jnp.float32)
    return total


def on_device(
    state, routes, gates, norm_gain, w_gate, w_up, w_down, spare_gate, spare_up, spare_down
):
    segments = lax.axis_size("segment")
    members = lax.axis_size("expert")
    outer = members // 2
    assert outer & (outer - 1) == 0
    tok_dev = state.shape[1]

    def spread(value):
        got = {j: moved(value, 2 * j, 0) for j in widest_first(outer)}
        return [value] + [got[j] for j in range(1, outer)]

    weights = [w_gate[:, 0], w_up[:, 0], w_down[:, 0]]
    spare_all = [spare_gate[:, 0], spare_up[:, 0], spare_down[:, 0]]

    def fetched(values):
        return [moved(value, 0, -1) for value in values]

    head = filled(spare_all[:1], 0)
    head, rest, state, routes, gates = lax.optimization_barrier((head, spare_all[1:], state, routes, gates))
    spares = [fetched(head + filled(rest, 0))]
    shape = (tok_dev, state.shape[2] + LANES)
    own = small(
        prepare_kernel, jax.ShapeDtypeStruct(shape, state.dtype), state[0],
        jnp.transpose(routes[:, 0], (0, 2, 1)), jnp.transpose(gates[:, 0], (0, 2, 1)),
    )
    other = moved(own, 1, 0)
    pair = small(join_kernel, jax.ShapeDtypeStruct((2 * tok_dev, shape[1]), state.dtype), own, other)
    arrived = spread(pair)
    weights = filled(weights)
    late = stacked(lax.optimization_barrier((*spare_all, arrived[1]))[:3], 1)
    before = run_layer(
        arrived, arrived, norm_gain, weights, [], tick_idx=0, tok_dev=tok_dev, ends=False
    )
    late = moved(late, 0, -1)
    spares.append([late])

    x_blocks = arrived
    for tick_idx in range(TICKS):
        used = sorted(groups_at(tick_idx, segments))
        assert used in ([0], [0, 1])
        parts = run_layer(
            x_blocks, arrived, norm_gain, weights, spares[:len(used)], tick_idx=tick_idx, tok_dev=tok_dev,
            carried=before if tick_idx == 0 else None,
        )
        got = [moved(parts[j], 2 * j, 0) for j in widest_first(outer)]
        if tick_idx + 1 == TICKS:
            total = added([parts[0]] + got)
            other = moved(total[tok_dev:].astype(jnp.bfloat16), 1, 0)
            return added([total[:tok_dev], other]).astype(jnp.bfloat16)[None]
        total = summed([parts[0]] + got)
        across = moved(total, 1, 1)
        along = moved(total, 0, 1)
        x_blocks = spread(summed([along, across], swap=True))


def solution(mesh):
    return jax.shard_map(
        on_device,
        mesh=mesh,
        in_specs=(
            P("segment", "expert", None),
            P(None, "segment", "expert", None),
            P(None, "segment", "expert", None),
            P(None, "segment", None),
            P(None, "segment", "expert", None),
            P(None, "segment", "expert", None),
            P(None, "segment", "expert", None),
            P(None, "segment", "expert", None),
            P(None, "segment", "expert", None),
            P(None, "segment", "expert", None),
        ),
        out_specs=P("segment", "expert", None),
        check_vma=False,
    )
```

```python
import functools

import jax
import jax.numpy as jnp
from jax import lax
from jax.experimental import pallas as pl
from jax.experimental.pallas import tpu as pltpu
from jax.sharding import PartitionSpec as P

EXPERTS = 4
TICKS = 4
CAP = 4
LANES = 128
BOTH = ("segment", "expert")


EPSILON = 1e-06


def moved(value, flip, steps):
    segments, members = lax.axis_size("segment"), lax.axis_size("expert")
    pairs = [
        (section * members + member, (section + steps) % segments * members + (member ^ flip))
        for section in range(segments)
        for member in range(members)
    ]
    return lax.ppermute(value, BOTH, pairs)


def group_of(section, tick_idx, segments):
    start_segment = (section - tick_idx) % segments
    first_group = jnp.where((start_segment % 2 == 1) & (start_segment + TICKS <= segments), 1, 0)
    return (first_group + jnp.where(start_segment + tick_idx >= segments, 1, 0)).astype(jnp.int32)


def groups_at(tick_idx, segments):
    found = set()
    for section in range(segments):
        start = (section - tick_idx) % segments
        first = 1 if start % 2 == 1 and start + TICKS <= segments else 0
        found.add(first + (1 if start + tick_idx >= segments else 0))
    return found


WHOLE = pl.BlockSpec(memory_space=pltpu.VMEM)


def small(kernel, out_shape, *values):
    return pl.pallas_call(
        kernel,
        out_shape=out_shape,
        in_specs=[WHOLE] * len(values),
        out_specs=WHOLE,
        compiler_params=pltpu.CompilerParams(vmem_limit_bytes=2 * 1024 * 1024),
    )(*values)


def prepare_kernel(state_ref, routes_ref, gates_ref, out_ref):
    rows, width = state_ref.shape
    lane = lax.broadcasted_iota(jnp.int32, (rows, LANES), 1)
    columns = EXPERTS + 1
    routed = jnp.zeros((rows, LANES), jnp.float32)
    member = jnp.zeros((rows, LANES), jnp.float32)
    square = (rows, rows)
    diagonal = lax.broadcasted_iota(jnp.int32, square, 0) == lax.broadcasted_iota(jnp.int32, square, 1)

    def upright(line):
        return jnp.sum(jnp.where(diagonal, line, jnp.zeros_like(line)), axis=1, keepdims=True)

    for tick_idx in range(TICKS):
        for choice in range(routes_ref.shape[1]):
            named = lane == upright(routes_ref[tick_idx, choice:choice + 1, :]) + tick_idx * columns
            routed = routed + jnp.where(named, upright(gates_ref[tick_idx, choice:choice + 1, :]), 0.0)
            member = member + jnp.where(named, 1.0, 0.0)
    row = lax.broadcasted_iota(jnp.int32, (rows, LANES), 0)
    position = jnp.zeros((rows, LANES), jnp.float32)
    for earlier in range(rows - 1):
        position = position + jnp.where(row > earlier, member[earlier:earlier + 1, :], 0.0)
    inside = position < CAP
    table = jnp.where(inside, routed, 0.0)
    over = jnp.where(inside, 0.0, routed)
    for tick_idx in range(TICKS):
        low = tick_idx * columns
        spill = jnp.sum(jnp.where((lane >= low) & (lane < low + EXPERTS), over, 0.0), axis=1, keepdims=True)
        table = jnp.where(lane == low + EXPERTS, spill, table)
    high = table.astype(jnp.bfloat16).astype(jnp.float32)
    both = high + pltpu.roll(table - high, TICKS * columns, 1)
    out_ref[:, :width] = state_ref[...]
    out_ref[:, width:] = both.astype(jnp.bfloat16)


def join_kernel(first_ref, second_ref, out_ref):
    out_ref[...] = jnp.concatenate([first_ref[...], second_ref[...]], axis=0)


def served(normed, gate, up, down, turned):
    contract = (((1,), (0 if turned else 1,)), ((), ()))
    gate_pre = lax.dot_general(normed, gate, contract, preferred_element_type=jnp.float32)
    up_pre = lax.dot_general(normed, up, contract, preferred_element_type=jnp.float32)
    hidden = (gate_pre / (1.0 + jnp.exp(-gate_pre)) * up_pre).astype(jnp.bfloat16)
    return jnp.dot(hidden, down, preferred_element_type=jnp.float32)


def either(second, bodies):
    if len(bodies) == 1:
        bodies[0]()
    elif bodies:
        pl.when(jnp.logical_not(second))(bodies[0])
        pl.when(second)(bodies[1])


def layer_kernel(*refs, tick_idx, blocks, slot_count, spare_counts, tok_dev, width, carried, ends):
    x_refs, first_refs, refs = refs[:blocks], refs[blocks:2 * blocks], refs[2 * blocks:]
    gain_ref, refs = refs[0], refs[1:]
    if carried:
        carried_ref, refs = refs[0], refs[1:]
    else:
        slots, refs = [refs[3 * i:3 * i + 3] for i in range(slot_count)], refs[3 * slot_count:]
    spare_refs = []
    for count in spare_counts:
        spare_refs.append(refs[:count] if count > 1 else [refs[0].at[i] for i in range(refs[0].shape[0])])
        refs = refs[count:]
    segments, members = lax.axis_size("segment"), lax.axis_size("expert")
    group = group_of(lax.axis_index("segment"), tick_idx, segments)
    expert = lax.axis_index("expert") // (members // EXPERTS)
    x = jnp.concatenate([x_ref[:, :width] for x_ref in x_refs], axis=0)
    values = x.astype(jnp.float32)
    row_scale = lax.rsqrt(jnp.mean(values * values, axis=-1, keepdims=True) + EPSILON)
    normed = (values * row_scale * gain_ref[group]).astype(jnp.bfloat16)
    table = jnp.concatenate([ref[:, width:] for ref in first_refs], axis=0).astype(jnp.float32)
    lane = lax.broadcasted_iota(jnp.int32, table.shape, 1)
    columns = TICKS * (EXPERTS + 1)

    def column(at):
        return jnp.sum(jnp.where((lane == at) | (lane == at + columns), table, 0.0), axis=1, keepdims=True)

    total_ref = refs[0] if not ends else refs[-1]
    if carried:
        total_ref[...] = carried_ref[...]
    else:

        def put(slot):
            share = column(tick_idx * (EXPERTS + 1) + expert)
            total_ref[...] = share * served(normed, *[ref[...] for ref in slot], True)

        home = group_of(lax.axis_index("segment"), 0, segments)
        either(group != home, [functools.partial(put, slot) for slot in slots])

    def add(spare_ref):
        spill = column(tick_idx * (EXPERTS + 1) + EXPERTS)
        total_ref[...] += spill * served(normed, *[ref[...] for ref in spare_ref], False)

    either(group == 1, [functools.partial(add, spare_ref) for spare_ref in spare_refs])
    if not ends:
        return
    out_refs = refs[:blocks]
    per = 2 * tok_dev
    row = lax.broadcasted_iota(jnp.int32, (per, 1), 0)
    out_refs[0][...] = total_ref[0:per, :] + jnp.where(row < tok_dev, values[0:per], 0.0)
    for i in range(1, blocks):
        out_refs[i][...] = total_ref[i * per:(i + 1) * per, :].astype(jnp.bfloat16)


def resident(values):
    return [pltpu.with_memory_space_constraint(value, pltpu.VMEM) for value in values]


def run_layer(x_blocks, first_blocks, gain, weights, spares, *, tick_idx, tok_dev, carried=None, ends=True):
    blocks = len(x_blocks)
    width = gain.shape[-1]
    per = 2 * tok_dev
    rows = per * blocks
    values = [*x_blocks, *first_blocks, gain]
    values += [carried] if carried is not None else resident([one for slot in weights for one in slot])
    for spare in spares:
        values += resident(spare)
    hidden = (0 if carried is not None else weights[0][2].shape[0]) + (spares[0][0].shape[0] if spares else 0)
    whole = jax.ShapeDtypeStruct((rows, width), jnp.float32)
    parts = [jax.ShapeDtypeStruct((per, width), jnp.float32)]
    parts += [jax.ShapeDtypeStruct((per, width), jnp.bfloat16)] * (blocks - 1)
    return pl.pallas_call(
        functools.partial(
            layer_kernel, tick_idx=tick_idx, blocks=blocks, slot_count=len(weights), spare_counts=[len(spare) for spare in spares],
            tok_dev=tok_dev, width=width, carried=carried is not None, ends=ends,
        ),
        out_shape=parts if ends else whole,
        in_specs=[WHOLE] * len(values),
        out_specs=[WHOLE] * blocks if ends else WHOLE,
        scratch_shapes=[pltpu.VMEM((rows, width), jnp.float32)] if ends else [],
        compiler_params=pltpu.CompilerParams(vmem_limit_bytes=12 * 1024 * 1024),
        cost_estimate=pl.CostEstimate(
            flops=6 * rows * hidden * width, bytes_accessed=6 * hidden * width, transcendentals=rows * hidden
        ),
        name="layer",
    )(*values)


def sum_kernel(*refs, swap):
    total = refs[0][...].astype(jnp.float32)
    half = total.shape[0] // 2
    for ref in refs[1:-1]:
        value = ref[...].astype(jnp.float32)
        total = total + (jnp.concatenate([value[half:], value[:half]], axis=0) if swap else value)
    refs[-1][...] = total.astype(jnp.bfloat16)


def summed(values, swap=False):
    shape = jax.ShapeDtypeStruct(values[0].shape, jnp.bfloat16)
    return small(functools.partial(sum_kernel, swap=swap), shape, *values)


def fill_kernel(*refs, group):
    count = len(refs) // 2
    ins, outs, sems = refs[:count], refs[count:2 * count], refs[2 * count]
    copies = [
        pltpu.make_async_copy(one if group is None else one.at[group], out, sems.at[i])
        for i, (one, out) in enumerate(zip(ins, outs))
    ]
    for copy in copies:
        copy.start()
    for copy in copies:
        copy.wait()


def filled(values, group=None):
    shapes = [value.shape if group is None else value.shape[1:] for value in values]
    return pl.pallas_call(
        functools.partial(fill_kernel, group=group),
        out_shape=[pltpu.VMEM(shape, value.dtype) for shape, value in zip(shapes, values)],
        in_specs=[pl.BlockSpec(memory_space=pltpu.HBM)] * len(values),
        out_specs=[WHOLE] * len(values),
        scratch_shapes=[pltpu.SemaphoreType.DMA((len(values),))],
        compiler_params=pltpu.CompilerParams(vmem_limit_bytes=1024 * 1024),
        name="fill",
    )(*[pltpu.with_memory_space_constraint(value, pltpu.HBM) for value in values])


def load_kernel(*refs, turned, other):
    count = len(turned)
    ins, outs, (held, sems, straight) = refs[:count], refs[count:2 * count], refs[2 * count:]
    group = group_of(lax.axis_index("segment"), 0, lax.axis_size("segment"))
    group = 1 - group if other else group
    depth, block = held.shape[:2]
    work = [
        (ins[i], outs[i], low) for i in range(count) if turned[i] for low in range(0, ins[i].shape[1], block)
    ]

    def copy_of(at):
        source, _, low = work[at]
        return pltpu.make_async_copy(source.at[group, pl.ds(low, block), :], held.at[at % depth], sems.at[at % depth])

    for at in range(min(depth - 1, len(work))):
        copy_of(at).start()
    direct = [
        pltpu.make_async_copy(ins[i].at[group], outs[i], straight.at[i]) for i in range(count) if not turned[i]
    ]
    for copy in direct:
        copy.start()
    for at, (_, out, low) in enumerate(work):
        if at + depth - 1 < len(work):
            copy_of(at + depth - 1).start()
        copy_of(at).wait()
        out[:, low:low + block] = held[at % depth].T
    for copy in direct:
        copy.wait()


def loaded(values, turned, other):
    hidden, width = values[0].shape[1:]
    block = LANES if hidden % LANES == 0 else hidden
    return pl.pallas_call(
        functools.partial(load_kernel, turned=turned, other=other),
        out_shape=[
            pltpu.VMEM((width, hidden) if flip else (hidden, width), value.dtype)
            for value, flip in zip(values, turned)
        ],
        in_specs=[pl.BlockSpec(memory_space=pltpu.HBM)] * len(values),
        out_specs=[WHOLE] * len(values),
        scratch_shapes=[
            pltpu.VMEM((4, block, width), values[0].dtype),
            pltpu.SemaphoreType.DMA((4,)),
            pltpu.SemaphoreType.DMA((len(values),)),
        ],
        compiler_params=pltpu.CompilerParams(vmem_limit_bytes=6 * 1024 * 1024),
        name="load",
    )(*[pltpu.with_memory_space_constraint(value, pltpu.HBM) for value in values])


def stack_kernel(*refs, group):
    ins, out, sems = refs[:-2], refs[-2], refs[-1]
    copies = [pltpu.make_async_copy(one.at[group], out.at[i], sems.at[i]) for i, one in enumerate(ins)]
    for copy in copies:
        copy.start()
    for copy in copies:
        copy.wait()


def stacked(values, group):
    shape = (len(values),) + values[0].shape[1:]
    return pl.pallas_call(
        functools.partial(stack_kernel, group=group),
        out_shape=pltpu.VMEM(shape, values[0].dtype),
        in_specs=[pl.BlockSpec(memory_space=pltpu.HBM)] * len(values),
        out_specs=WHOLE,
        scratch_shapes=[pltpu.SemaphoreType.DMA((len(values),))],
        compiler_params=pltpu.CompilerParams(vmem_limit_bytes=6 * 1024 * 1024),
        name="stack",
    )(*[pltpu.with_memory_space_constraint(value, pltpu.HBM) for value in values])


def widest_first(outer):
    return range(outer - 1, 0, -1)


def added(values):
    total = values[0].astype(jnp.float32)
    for value in values[1:]:
        total = total + value.astype(jnp.float32)
    return total


def on_device(
    state, routes, gates, norm_gain, w_gate, w_up, w_down, spare_gate, spare_up, spare_down
):
    segments = lax.axis_size("segment")
    members = lax.axis_size("expert")
    outer = members // 2
    assert outer & (outer - 1) == 0
    tok_dev = state.shape[1]

    def spread(value):
        got = {j: moved(value, 2 * j, 0) for j in widest_first(outer)}
        return [value] + [got[j] for j in range(1, outer)]

    weights = [w_gate[:, 0], w_up[:, 0], w_down[:, 0]]
    spare_all = [spare_gate[:, 0], spare_up[:, 0], spare_down[:, 0]]

    def fetched(values):
        return [moved(value, 0, -1) for value in values]

    head = filled(spare_all[:1], 0)
    head, rest, state, routes, gates = lax.optimization_barrier((head, spare_all[1:], state, routes, gates))
    spares = [fetched(head + filled(rest, 0))]
    shape = (tok_dev, state.shape[2] + LANES)
    own = small(
        prepare_kernel, jax.ShapeDtypeStruct(shape, state.dtype), state[0],
        jnp.transpose(routes[:, 0], (0, 2, 1)), jnp.transpose(gates[:, 0], (0, 2, 1)),
    )
    other = moved(own, 1, 0)
    pair = small(join_kernel, jax.ShapeDtypeStruct((2 * tok_dev, shape[1]), state.dtype), own, other)
    arrived = spread(pair)
    slots = [loaded(weights, (True, True, False), False)]
    late = stacked(lax.optimization_barrier((*spare_all, arrived[1]))[:3], 1)
    before = run_layer(
        arrived, arrived, norm_gain, slots, [], tick_idx=0, tok_dev=tok_dev, ends=False
    )
    late = moved(late, 0, -1)
    spares.append([late])

    x_blocks = arrived
    for tick_idx in range(TICKS):
        used = sorted(groups_at(tick_idx, segments))
        assert used in ([0], [0, 1])
        parts = run_layer(
            x_blocks, arrived, norm_gain, slots, spares[:len(used)], tick_idx=tick_idx, tok_dev=tok_dev,
            carried=before if tick_idx == 0 else None,
        )
        got = [moved(parts[j], 2 * j, 0) for j in widest_first(outer)]
        if tick_idx == 0:
            tied = lax.optimization_barrier((*weights, parts[0]))[:3]
            gate = loaded(tied[:1], (True,), True)
        if tick_idx + 1 == TICKS:
            total = added([parts[0]] + got)
            other = moved(total[tok_dev:].astype(jnp.bfloat16), 1, 0)
            return added([total[:tok_dev], other]).astype(jnp.bfloat16)[None]
        total = summed([parts[0]] + got)
        across = moved(total, 1, 1)
        along = moved(total, 0, 1)
        if tick_idx == 0:
            tied = lax.optimization_barrier((*weights, total))[:3]
            slots.append(gate + loaded(tied[1:], (True, False), True))
        x_blocks = spread(summed([along, across], swap=True))


def solution(mesh):
    return jax.shard_map(
        on_device,
        mesh=mesh,
        in_specs=(
            P("segment", "expert", None),
            P(None, "segment", "expert", None),
            P(None, "segment", "expert", None),
            P(None, "segment", None),
            P(None, "segment", "expert", None),
            P(None, "segment", "expert", None),
            P(None, "segment", "expert", None),
            P(None, "segment", "expert", None),
            P(None, "segment", "expert", None),
            P(None, "segment", "expert", None),
        ),
        out_specs=P("segment", "expert", None),
        check_vma=False,
    )
```

```python
import functools

import jax
import jax.numpy as jnp
from jax import lax
from jax.experimental import pallas as pl
from jax.experimental.pallas import tpu as pltpu
from jax.sharding import PartitionSpec as P

EXPERTS = 4
TICKS = 4
CAP = 4
LANES = 128
BOTH = ("segment", "expert")


EPSILON = 1e-06


def moved(value, flip, steps):
    segments, members = lax.axis_size("segment"), lax.axis_size("expert")
    pairs = [
        (section * members + member, (section + steps) % segments * members + (member ^ flip))
        for section in range(segments)
        for member in range(members)
    ]
    return lax.ppermute(value, BOTH, pairs)


def group_of(section, tick_idx, segments):
    start_segment = (section - tick_idx) % segments
    first_group = jnp.where((start_segment % 2 == 1) & (start_segment + TICKS <= segments), 1, 0)
    return (first_group + jnp.where(start_segment + tick_idx >= segments, 1, 0)).astype(jnp.int32)


def later_users(tick_idx, segments):
    found = set()
    for section in range(segments):
        start = (section - tick_idx) % segments
        first = 1 if start % 2 == 1 and start + TICKS <= segments else 0
        if first + (1 if start + tick_idx >= segments else 0) == 1:
            found.add(section)
    return found


def swapped(value, users):
    segments, members = lax.axis_size("segment"), lax.axis_size("expert")
    partner = {section: section for section in range(segments)}
    for section in users:
        behind = (section + 1) % segments
        assert behind not in users
        partner[section], partner[behind] = behind, section
    pairs = [
        (section * members + member, partner[section] * members + member)
        for section in range(segments)
        for member in range(members)
    ]
    return lax.ppermute(value, BOTH, pairs)


WHOLE = pl.BlockSpec(memory_space=pltpu.VMEM)


def small(kernel, out_shape, *values):
    return pl.pallas_call(
        kernel,
        out_shape=out_shape,
        in_specs=[WHOLE] * len(values),
        out_specs=WHOLE,
        compiler_params=pltpu.CompilerParams(vmem_limit_bytes=2 * 1024 * 1024),
    )(*values)


def prepare_kernel(state_ref, routes_ref, gates_ref, out_ref):
    rows, width = state_ref.shape
    lane = lax.broadcasted_iota(jnp.int32, (rows, LANES), 1)
    columns = EXPERTS + 1
    routed = jnp.zeros((rows, LANES), jnp.float32)
    member = jnp.zeros((rows, LANES), jnp.float32)
    square = (rows, rows)
    diagonal = lax.broadcasted_iota(jnp.int32, square, 0) == lax.broadcasted_iota(jnp.int32, square, 1)

    def upright(line):
        return jnp.sum(jnp.where(diagonal, line, jnp.zeros_like(line)), axis=1, keepdims=True)

    for tick_idx in range(TICKS):
        for choice in range(routes_ref.shape[1]):
            named = lane == upright(routes_ref[tick_idx, choice:choice + 1, :]) + tick_idx * columns
            routed = routed + jnp.where(named, upright(gates_ref[tick_idx, choice:choice + 1, :]), 0.0)
            member = member + jnp.where(named, 1.0, 0.0)
    row = lax.broadcasted_iota(jnp.int32, (rows, LANES), 0)
    position = jnp.zeros((rows, LANES), jnp.float32)
    for earlier in range(rows - 1):
        position = position + jnp.where(row > earlier, member[earlier:earlier + 1, :], 0.0)
    inside = position < CAP
    table = jnp.where(inside, routed, 0.0)
    over = jnp.where(inside, 0.0, routed)
    for tick_idx in range(TICKS):
        low = tick_idx * columns
        spill = jnp.sum(jnp.where((lane >= low) & (lane < low + EXPERTS), over, 0.0), axis=1, keepdims=True)
        table = jnp.where(lane == low + EXPERTS, spill, table)
    high = table.astype(jnp.bfloat16).astype(jnp.float32)
    both = high + pltpu.roll(table - high, TICKS * columns, 1)
    out_ref[:, :width] = state_ref[...]
    out_ref[:, width:] = both.astype(jnp.bfloat16)


def join_kernel(first_ref, second_ref, out_ref):
    out_ref[...] = jnp.concatenate([first_ref[...], second_ref[...]], axis=0)


def served(normed, gate, up, down, turned):
    contract = (((1,), (0 if turned else 1,)), ((), ()))
    gate_pre = lax.dot_general(normed, gate, contract, preferred_element_type=jnp.float32)
    up_pre = lax.dot_general(normed, up, contract, preferred_element_type=jnp.float32)
    hidden = (gate_pre / (1.0 + jnp.exp(-gate_pre)) * up_pre).astype(jnp.bfloat16)
    return jnp.dot(hidden, down, preferred_element_type=jnp.float32)


def either(second, bodies):
    if len(bodies) == 1:
        bodies[0]()
    elif bodies:
        pl.when(jnp.logical_not(second))(bodies[0])
        pl.when(second)(bodies[1])


def layer_kernel(*refs, tick_idx, blocks, slot_count, spare_counts, tok_dev, width, carried, ends):
    x_refs, first_refs, refs = refs[:blocks], refs[blocks:2 * blocks], refs[2 * blocks:]
    gain_ref, refs = refs[0], refs[1:]
    if carried:
        carried_ref, refs = refs[0], refs[1:]
    else:
        slots, refs = [refs[3 * i:3 * i + 3] for i in range(slot_count)], refs[3 * slot_count:]
    spare_refs = []
    for count in spare_counts:
        spare_refs.append(refs[:count] if count > 1 else [refs[0].at[i] for i in range(refs[0].shape[0])])
        refs = refs[count:]
    segments, members = lax.axis_size("segment"), lax.axis_size("expert")
    group = group_of(lax.axis_index("segment"), tick_idx, segments)
    expert = lax.axis_index("expert") // (members // EXPERTS)
    x = jnp.concatenate([x_ref[:, :width] for x_ref in x_refs], axis=0)
    values = x.astype(jnp.float32)
    row_scale = lax.rsqrt(jnp.mean(values * values, axis=-1, keepdims=True) + EPSILON)
    normed = (values * row_scale * gain_ref[group]).astype(jnp.bfloat16)
    table = jnp.concatenate([ref[:, width:] for ref in first_refs], axis=0).astype(jnp.float32)
    lane = lax.broadcasted_iota(jnp.int32, table.shape, 1)
    columns = TICKS * (EXPERTS + 1)

    def column(at):
        return jnp.sum(jnp.where((lane == at) | (lane == at + columns), table, 0.0), axis=1, keepdims=True)

    total_ref = refs[0] if not ends else refs[-1]
    if carried:
        total_ref[...] = carried_ref[...]
    else:

        def put(slot):
            share = column(tick_idx * (EXPERTS + 1) + expert)
            total_ref[...] = share * served(normed, *[ref[...] for ref in slot], True)

        home = group_of(lax.axis_index("segment"), 0, segments)
        either(group != home, [functools.partial(put, slot) for slot in slots])

    def add(spare_ref):
        spill = column(tick_idx * (EXPERTS + 1) + EXPERTS)
        total_ref[...] += spill * served(normed, *[ref[...] for ref in spare_ref], False)

    either(group == 1, [functools.partial(add, spare_ref) for spare_ref in spare_refs])
    if not ends:
        return
    out_refs = refs[:blocks]
    per = 2 * tok_dev
    row = lax.broadcasted_iota(jnp.int32, (per, 1), 0)
    out_refs[0][...] = total_ref[0:per, :] + jnp.where(row < tok_dev, values[0:per], 0.0)
    for i in range(1, blocks):
        out_refs[i][...] = total_ref[i * per:(i + 1) * per, :].astype(jnp.bfloat16)


def resident(values):
    return [pltpu.with_memory_space_constraint(value, pltpu.VMEM) for value in values]


def run_layer(x_blocks, first_blocks, gain, weights, spares, *, tick_idx, tok_dev, carried=None, ends=True):
    blocks = len(x_blocks)
    width = gain.shape[-1]
    per = 2 * tok_dev
    rows = per * blocks
    values = [*x_blocks, *first_blocks, gain]
    values += [carried] if carried is not None else resident([one for slot in weights for one in slot])
    for spare in spares:
        values += resident(spare)
    hidden = (0 if carried is not None else weights[0][2].shape[0]) + (spares[0][0].shape[0] if spares else 0)
    whole = jax.ShapeDtypeStruct((rows, width), jnp.float32)
    parts = [jax.ShapeDtypeStruct((per, width), jnp.float32)]
    parts += [jax.ShapeDtypeStruct((per, width), jnp.bfloat16)] * (blocks - 1)
    return pl.pallas_call(
        functools.partial(
            layer_kernel, tick_idx=tick_idx, blocks=blocks, slot_count=len(weights), spare_counts=[len(spare) for spare in spares],
            tok_dev=tok_dev, width=width, carried=carried is not None, ends=ends,
        ),
        out_shape=parts if ends else whole,
        in_specs=[WHOLE] * len(values),
        out_specs=[WHOLE] * blocks if ends else WHOLE,
        scratch_shapes=[pltpu.VMEM((rows, width), jnp.float32)] if ends else [],
        compiler_params=pltpu.CompilerParams(vmem_limit_bytes=12 * 1024 * 1024),
        cost_estimate=pl.CostEstimate(
            flops=6 * rows * hidden * width, bytes_accessed=6 * hidden * width, transcendentals=rows * hidden
        ),
        name="layer",
    )(*values)


def sum_kernel(*refs, swap):
    total = refs[0][...].astype(jnp.float32)
    half = total.shape[0] // 2
    for ref in refs[1:-1]:
        value = ref[...].astype(jnp.float32)
        total = total + (jnp.concatenate([value[half:], value[:half]], axis=0) if swap else value)
    refs[-1][...] = total.astype(jnp.bfloat16)


def summed(values, swap=False):
    shape = jax.ShapeDtypeStruct(values[0].shape, jnp.bfloat16)
    return small(functools.partial(sum_kernel, swap=swap), shape, *values)


def fill_kernel(*refs, group):
    count = len(refs) // 2
    ins, outs, sems = refs[:count], refs[count:2 * count], refs[2 * count]
    copies = [
        pltpu.make_async_copy(one if group is None else one.at[group], out, sems.at[i])
        for i, (one, out) in enumerate(zip(ins, outs))
    ]
    for copy in copies:
        copy.start()
    for copy in copies:
        copy.wait()


def filled(values, group=None):
    shapes = [value.shape if group is None else value.shape[1:] for value in values]
    return pl.pallas_call(
        functools.partial(fill_kernel, group=group),
        out_shape=[pltpu.VMEM(shape, value.dtype) for shape, value in zip(shapes, values)],
        in_specs=[pl.BlockSpec(memory_space=pltpu.HBM)] * len(values),
        out_specs=[WHOLE] * len(values),
        scratch_shapes=[pltpu.SemaphoreType.DMA((len(values),))],
        compiler_params=pltpu.CompilerParams(vmem_limit_bytes=1024 * 1024),
        name="fill",
    )(*[pltpu.with_memory_space_constraint(value, pltpu.HBM) for value in values])


def load_kernel(*refs, turned, other):
    count = len(turned)
    ins, outs, (held, sems, straight) = refs[:count], refs[count:2 * count], refs[2 * count:]
    group = group_of(lax.axis_index("segment"), 0, lax.axis_size("segment"))
    group = 1 - group if other else group
    depth, block = held.shape[:2]
    work = [
        (ins[i], outs[i], low) for i in range(count) if turned[i] for low in range(0, ins[i].shape[1], block)
    ]

    def copy_of(at):
        source, _, low = work[at]
        return pltpu.make_async_copy(source.at[group, pl.ds(low, block), :], held.at[at % depth], sems.at[at % depth])

    for at in range(min(depth - 1, len(work))):
        copy_of(at).start()
    direct = [
        pltpu.make_async_copy(ins[i].at[group], outs[i], straight.at[i]) for i in range(count) if not turned[i]
    ]
    for copy in direct:
        copy.start()
    for at, (_, out, low) in enumerate(work):
        if at + depth - 1 < len(work):
            copy_of(at + depth - 1).start()
        copy_of(at).wait()
        out[:, low:low + block] = held[at % depth].T
    for copy in direct:
        copy.wait()


def loaded(values, turned, other):
    hidden, width = values[0].shape[1:]
    block = LANES if hidden % LANES == 0 else hidden
    return pl.pallas_call(
        functools.partial(load_kernel, turned=turned, other=other),
        out_shape=[
            pltpu.VMEM((width, hidden) if flip else (hidden, width), value.dtype)
            for value, flip in zip(values, turned)
        ],
        in_specs=[pl.BlockSpec(memory_space=pltpu.HBM)] * len(values),
        out_specs=[WHOLE] * len(values),
        scratch_shapes=[
            pltpu.VMEM((4, block, width), values[0].dtype),
            pltpu.SemaphoreType.DMA((4,)),
            pltpu.SemaphoreType.DMA((len(values),)),
        ],
        compiler_params=pltpu.CompilerParams(vmem_limit_bytes=6 * 1024 * 1024),
        name="load",
    )(*[pltpu.with_memory_space_constraint(value, pltpu.HBM) for value in values])


def stack_kernel(*refs, group):
    ins, out, sems = refs[:-2], refs[-2], refs[-1]
    copies = [pltpu.make_async_copy(one.at[group], out.at[i], sems.at[i]) for i, one in enumerate(ins)]
    for copy in copies:
        copy.start()
    for copy in copies:
        copy.wait()


def stacked(values, group):
    shape = (len(values),) + values[0].shape[1:]
    return pl.pallas_call(
        functools.partial(stack_kernel, group=group),
        out_shape=pltpu.VMEM(shape, values[0].dtype),
        in_specs=[pl.BlockSpec(memory_space=pltpu.HBM)] * len(values),
        out_specs=WHOLE,
        scratch_shapes=[pltpu.SemaphoreType.DMA((len(values),))],
        compiler_params=pltpu.CompilerParams(vmem_limit_bytes=6 * 1024 * 1024),
        name="stack",
    )(*[pltpu.with_memory_space_constraint(value, pltpu.HBM) for value in values])


def widest_first(outer):
    return range(outer - 1, 0, -1)


def added(values):
    total = values[0].astype(jnp.float32)
    for value in values[1:]:
        total = total + value.astype(jnp.float32)
    return total


def on_device(
    state, routes, gates, norm_gain, w_gate, w_up, w_down, spare_gate, spare_up, spare_down
):
    segments = lax.axis_size("segment")
    segments, members = lax.axis_size("segment"), lax.axis_size("expert")
    outer = members // 2
    assert outer & (outer - 1) == 0
    tok_dev = state.shape[1]

    def spread(value):
        got = {j: moved(value, 2 * j, 0) for j in widest_first(outer)}
        return [value] + [got[j] for j in range(1, outer)]

    weights = [w_gate[:, 0], w_up[:, 0], w_down[:, 0]]
    spare_all = [spare_gate[:, 0], spare_up[:, 0], spare_down[:, 0]]

    def fetched(values):
        return [moved(value, 0, -1) for value in values]

    head = filled(spare_all[:1], 0)
    head, rest, state, routes, gates = lax.optimization_barrier((head, spare_all[1:], state, routes, gates))
    spares = [fetched(head + filled(rest, 0))]
    shape = (tok_dev, state.shape[2] + LANES)
    own = small(
        prepare_kernel, jax.ShapeDtypeStruct(shape, state.dtype), state[0],
        jnp.transpose(routes[:, 0], (0, 2, 1)), jnp.transpose(gates[:, 0], (0, 2, 1)),
    )
    other = moved(own, 1, 0)
    pair = small(join_kernel, jax.ShapeDtypeStruct((2 * tok_dev, shape[1]), state.dtype), own, other)
    arrived = spread(pair)
    slots = [loaded(weights, (True, True, False), False)]
    late = stacked(lax.optimization_barrier((*spare_all, arrived[1]))[:3], 1)
    before = run_layer(
        arrived, arrived, norm_gain, slots, [], tick_idx=0, tok_dev=tok_dev, ends=False
    )

    users = [later_users(tick_idx, segments) for tick_idx in range(TICKS)]
    opening = min([tick_idx for tick_idx in range(TICKS) if users[tick_idx]], default=TICKS)
    near = [swapped(late, users[opening])] if opening < TICKS else []

    x_blocks = arrived
    for tick_idx in range(TICKS):
        used = [spares[0]]
        if users[tick_idx]:
            used.append(near if users[tick_idx] <= users[opening] else far)
        parts = run_layer(
            x_blocks, arrived, norm_gain, slots, used, tick_idx=tick_idx, tok_dev=tok_dev,
            carried=before if tick_idx == 0 else None,
        )
        got = [moved(parts[j], 2 * j, 0) for j in widest_first(outer)]
        if tick_idx == 0:
            far = [moved(lax.optimization_barrier((late, parts[0]))[0], 0, -1)]
            tied = lax.optimization_barrier((*weights, parts[0]))[:3]
            gate = loaded(tied[:1], (True,), True)
        if tick_idx + 1 == TICKS:
            total = added([parts[0]] + got)
            other = moved(total[tok_dev:].astype(jnp.bfloat16), 1, 0)
            return added([total[:tok_dev], other]).astype(jnp.bfloat16)[None]
        total = summed([parts[0]] + got)
        across = moved(total, 1, 1)
        along = moved(total, 0, 1)
        if tick_idx == 0:
            tied = lax.optimization_barrier((*weights, total))[:3]
            slots.append(gate + loaded(tied[1:], (True, False), True))
        x_blocks = spread(summed([along, across], swap=True))


def solution(mesh):
    return jax.shard_map(
        on_device,
        mesh=mesh,
        in_specs=(
            P("segment", "expert", None),
            P(None, "segment", "expert", None),
            P(None, "segment", "expert", None),
            P(None, "segment", None),
            P(None, "segment", "expert", None),
            P(None, "segment", "expert", None),
            P(None, "segment", "expert", None),
            P(None, "segment", "expert", None),
            P(None, "segment", "expert", None),
            P(None, "segment", "expert", None),
        ),
        out_specs=P("segment", "expert", None),
        check_vma=False,
    )
```

```python
import functools

import jax
import jax.numpy as jnp
from jax import lax
from jax.experimental import pallas as pl
from jax.experimental.pallas import tpu as pltpu
from jax.sharding import PartitionSpec as P

EXPERTS = 4
TICKS = 4
CAP = 4
LANES = 128
BOTH = ("segment", "expert")


EPSILON = 1e-06


def moved(value, flip, steps):
    segments, members = lax.axis_size("segment"), lax.axis_size("expert")
    pairs = [
        (section * members + member, (section + steps) % segments * members + (member ^ flip))
        for section in range(segments)
        for member in range(members)
    ]
    return lax.ppermute(value, BOTH, pairs)


def group_of(section, tick_idx, segments):
    start_segment = (section - tick_idx) % segments
    first_group = jnp.where((start_segment % 2 == 1) & (start_segment + TICKS <= segments), 1, 0)
    return (first_group + jnp.where(start_segment + tick_idx >= segments, 1, 0)).astype(jnp.int32)


def later_users(tick_idx, segments):
    found = set()
    for section in range(segments):
        start = (section - tick_idx) % segments
        first = 1 if start % 2 == 1 and start + TICKS <= segments else 0
        if first + (1 if start + tick_idx >= segments else 0) == 1:
            found.add(section)
    return found


def swapped(value, users):
    segments, members = lax.axis_size("segment"), lax.axis_size("expert")
    partner = {section: section for section in range(segments)}
    for section in users:
        behind = (section + 1) % segments
        assert behind not in users
        partner[section], partner[behind] = behind, section
    pairs = [
        (section * members + member, partner[section] * members + member)
        for section in range(segments)
        for member in range(members)
    ]
    return lax.ppermute(value, BOTH, pairs)


WHOLE = pl.BlockSpec(memory_space=pltpu.VMEM)


def small(kernel, out_shape, *values):
    return pl.pallas_call(
        kernel,
        out_shape=out_shape,
        in_specs=[WHOLE] * len(values),
        out_specs=WHOLE,
        compiler_params=pltpu.CompilerParams(vmem_limit_bytes=2 * 1024 * 1024),
    )(*values)


def prepare_kernel(state_ref, routes_ref, gates_ref, out_ref):
    rows, width = state_ref.shape
    lane = lax.broadcasted_iota(jnp.int32, (rows, LANES), 1)
    columns = EXPERTS + 1
    routed = jnp.zeros((rows, LANES), jnp.float32)
    member = jnp.zeros((rows, LANES), jnp.float32)
    square = (rows, rows)
    diagonal = lax.broadcasted_iota(jnp.int32, square, 0) == lax.broadcasted_iota(jnp.int32, square, 1)

    def upright(line):
        return jnp.sum(jnp.where(diagonal, line, jnp.zeros_like(line)), axis=1, keepdims=True)

    for tick_idx in range(TICKS):
        for choice in range(routes_ref.shape[1]):
            named = lane == upright(routes_ref[tick_idx, choice:choice + 1, :]) + tick_idx * columns
            routed = routed + jnp.where(named, upright(gates_ref[tick_idx, choice:choice + 1, :]), 0.0)
            member = member + jnp.where(named, 1.0, 0.0)
    row = lax.broadcasted_iota(jnp.int32, (rows, LANES), 0)
    position = jnp.zeros((rows, LANES), jnp.float32)
    for earlier in range(rows - 1):
        position = position + jnp.where(row > earlier, member[earlier:earlier + 1, :], 0.0)
    inside = position < CAP
    table = jnp.where(inside, routed, 0.0)
    over = jnp.where(inside, 0.0, routed)
    for tick_idx in range(TICKS):
        low = tick_idx * columns
        spill = jnp.sum(jnp.where((lane >= low) & (lane < low + EXPERTS), over, 0.0), axis=1, keepdims=True)
        table = jnp.where(lane == low + EXPERTS, spill, table)
    high = table.astype(jnp.bfloat16).astype(jnp.float32)
    both = high + pltpu.roll(table - high, TICKS * columns, 1)
    out_ref[:, :width] = state_ref[...]
    out_ref[:, width:] = both.astype(jnp.bfloat16)


def join_kernel(first_ref, second_ref, out_ref):
    out_ref[...] = jnp.concatenate([first_ref[...], second_ref[...]], axis=0)


def served(normed, gate, up, down, turned):
    contract = (((1,), (0 if turned else 1,)), ((), ()))
    gate_pre = lax.dot_general(normed, gate, contract, preferred_element_type=jnp.float32)
    up_pre = lax.dot_general(normed, up, contract, preferred_element_type=jnp.float32)
    hidden = (gate_pre / (1.0 + jnp.exp(-gate_pre)) * up_pre).astype(jnp.bfloat16)
    return jnp.dot(hidden, down, preferred_element_type=jnp.float32)


def either(second, bodies):
    if len(bodies) == 1:
        bodies[0]()
    elif bodies:
        pl.when(jnp.logical_not(second))(bodies[0])
        pl.when(second)(bodies[1])


def layer_kernel(*refs, tick_idx, blocks, slot_count, spare_counts, tok_dev, width, carried, ends, lead):
    x_refs, first_refs, refs = refs[:blocks], refs[blocks:2 * blocks], refs[2 * blocks:]
    gain_ref, refs = refs[0], refs[1:]
    if carried:
        carried_ref, refs = refs[0], refs[1:]
    else:
        slots, refs = [refs[3 * i:3 * i + 3] for i in range(slot_count)], refs[3 * slot_count:]
    spare_refs = []
    for count in spare_counts:
        spare_refs.append(refs[:count] if count > 1 else [refs[0].at[i] for i in range(refs[0].shape[0])])
        refs = refs[count:]
    segments, members = lax.axis_size("segment"), lax.axis_size("expert")
    group = group_of(lax.axis_index("segment"), tick_idx, segments)
    expert = lax.axis_index("expert") // (members // EXPERTS)
    x = jnp.concatenate([x_ref[:, :width] for x_ref in x_refs], axis=0)
    values = x.astype(jnp.float32)
    row_scale = lax.rsqrt(jnp.mean(values * values, axis=-1, keepdims=True) + EPSILON)
    normed = (values * row_scale * gain_ref[group]).astype(jnp.bfloat16)
    table = jnp.concatenate([ref[:, width:] for ref in first_refs], axis=0).astype(jnp.float32)
    lane = lax.broadcasted_iota(jnp.int32, table.shape, 1)
    columns = TICKS * (EXPERTS + 1)

    def column(at):
        return jnp.sum(jnp.where((lane == at) | (lane == at + columns), table, 0.0), axis=1, keepdims=True)

    total_ref = refs[0] if not ends else refs[-1]
    if carried:
        total_ref[...] = carried_ref[...]
    else:

        def put(slot):
            share = column(tick_idx * (EXPERTS + 1) + expert)
            total_ref[...] = share * served(normed, *[ref[...] for ref in slot], True)

        home = group_of(lax.axis_index("segment"), 0, segments)
        either(group != home, [functools.partial(put, slot) for slot in slots])

    def add(spare_ref):
        spill = column(tick_idx * (EXPERTS + 1) + EXPERTS)
        total_ref[...] += spill * served(normed, *[ref[...] for ref in spare_ref], False)

    either(group == 1, [functools.partial(add, spare_ref) for spare_ref in spare_refs])
    if not ends:
        return
    out_refs = refs[:blocks]
    per = 2 * tok_dev
    row = lax.broadcasted_iota(jnp.int32, (per, 1), 0)
    for i in range(blocks):
        part = total_ref[i * per:(i + 1) * per, :]
        if lead and i == 0:
            part = part + jnp.where(row < tok_dev, values[0:per], 0.0)
        out_refs[i][...] = part.astype(out_refs[i].dtype)


def resident(values):
    return [pltpu.with_memory_space_constraint(value, pltpu.VMEM) for value in values]


def run_layer(x_blocks, first_blocks, gain, weights, spares, *, tick_idx, tok_dev, carried=None, ends=True, lead=True):
    blocks = len(x_blocks)
    width = gain.shape[-1]
    per = 2 * tok_dev
    rows = per * blocks
    values = [*x_blocks, *first_blocks, gain]
    values += [carried] if carried is not None else resident([one for slot in weights for one in slot])
    for spare in spares:
        values += resident(spare)
    hidden = (0 if carried is not None else weights[0][2].shape[0]) + (spares[0][0].shape[0] if spares else 0)
    whole = jax.ShapeDtypeStruct((rows, width), jnp.float32)
    parts = [
        jax.ShapeDtypeStruct((per, width), jnp.float32 if lead and i == 0 else jnp.bfloat16) for i in range(blocks)
    ]
    return pl.pallas_call(
        functools.partial(
            layer_kernel, tick_idx=tick_idx, blocks=blocks, slot_count=len(weights), spare_counts=[len(spare) for spare in spares],
            tok_dev=tok_dev, width=width, carried=carried is not None, ends=ends, lead=lead,
        ),
        out_shape=parts if ends else whole,
        in_specs=[WHOLE] * len(values),
        out_specs=[WHOLE] * blocks if ends else WHOLE,
        scratch_shapes=[pltpu.VMEM((rows, width), jnp.float32)] if ends else [],
        compiler_params=pltpu.CompilerParams(vmem_limit_bytes=12 * 1024 * 1024),
        cost_estimate=pl.CostEstimate(
            flops=6 * rows * hidden * width, bytes_accessed=6 * hidden * width, transcendentals=rows * hidden
        ),
        name="layer",
    )(*values)


def sum_kernel(*refs, swap):
    total = refs[0][...].astype(jnp.float32)
    half = total.shape[0] // 2
    for ref in refs[1:-1]:
        value = ref[...].astype(jnp.float32)
        total = total + (jnp.concatenate([value[half:], value[:half]], axis=0) if swap else value)
    refs[-1][...] = total.astype(jnp.bfloat16)


def summed(values, swap=False):
    shape = jax.ShapeDtypeStruct(values[0].shape, jnp.bfloat16)
    return small(functools.partial(sum_kernel, swap=swap), shape, *values)


def fill_kernel(*refs, group):
    count = len(refs) // 2
    ins, outs, sems = refs[:count], refs[count:2 * count], refs[2 * count]
    copies = [
        pltpu.make_async_copy(one if group is None else one.at[group], out, sems.at[i])
        for i, (one, out) in enumerate(zip(ins, outs))
    ]
    for copy in copies:
        copy.start()
    for copy in copies:
        copy.wait()


def filled(values, group=None):
    shapes = [value.shape if group is None else value.shape[1:] for value in values]
    return pl.pallas_call(
        functools.partial(fill_kernel, group=group),
        out_shape=[pltpu.VMEM(shape, value.dtype) for shape, value in zip(shapes, values)],
        in_specs=[pl.BlockSpec(memory_space=pltpu.HBM)] * len(values),
        out_specs=[WHOLE] * len(values),
        scratch_shapes=[pltpu.SemaphoreType.DMA((len(values),))],
        compiler_params=pltpu.CompilerParams(vmem_limit_bytes=1024 * 1024),
        name="fill",
    )(*[pltpu.with_memory_space_constraint(value, pltpu.HBM) for value in values])


def load_kernel(*refs, turned, other):
    count = len(turned)
    ins, outs, (held, sems, straight) = refs[:count], refs[count:2 * count], refs[2 * count:]
    group = group_of(lax.axis_index("segment"), 0, lax.axis_size("segment"))
    group = 1 - group if other else group
    depth, block = held.shape[:2]
    work = [
        (ins[i], outs[i], low) for i in range(count) if turned[i] for low in range(0, ins[i].shape[1], block)
    ]

    def copy_of(at):
        source, _, low = work[at]
        return pltpu.make_async_copy(source.at[group, pl.ds(low, block), :], held.at[at % depth], sems.at[at % depth])

    for at in range(min(depth - 1, len(work))):
        copy_of(at).start()
    direct = [
        pltpu.make_async_copy(ins[i].at[group], outs[i], straight.at[i]) for i in range(count) if not turned[i]
    ]
    for copy in direct:
        copy.start()
    for at, (_, out, low) in enumerate(work):
        if at + depth - 1 < len(work):
            copy_of(at + depth - 1).start()
        copy_of(at).wait()
        out[:, low:low + block] = held[at % depth].T
    for copy in direct:
        copy.wait()


def loaded(values, turned, other):
    hidden, width = values[0].shape[1:]
    block = LANES if hidden % LANES == 0 else hidden
    return pl.pallas_call(
        functools.partial(load_kernel, turned=turned, other=other),
        out_shape=[
            pltpu.VMEM((width, hidden) if flip else (hidden, width), value.dtype)
            for value, flip in zip(values, turned)
        ],
        in_specs=[pl.BlockSpec(memory_space=pltpu.HBM)] * len(values),
        out_specs=[WHOLE] * len(values),
        scratch_shapes=[
            pltpu.VMEM((4, block, width), values[0].dtype),
            pltpu.SemaphoreType.DMA((4,)),
            pltpu.SemaphoreType.DMA((len(values),)),
        ],
        compiler_params=pltpu.CompilerParams(vmem_limit_bytes=6 * 1024 * 1024),
        name="load",
    )(*[pltpu.with_memory_space_constraint(value, pltpu.HBM) for value in values])


def stack_kernel(*refs, group):
    ins, out, sems = refs[:-2], refs[-2], refs[-1]
    copies = [pltpu.make_async_copy(one.at[group], out.at[i], sems.at[i]) for i, one in enumerate(ins)]
    for copy in copies:
        copy.start()
    for copy in copies:
        copy.wait()


def stacked(values, group):
    shape = (len(values),) + values[0].shape[1:]
    return pl.pallas_call(
        functools.partial(stack_kernel, group=group),
        out_shape=pltpu.VMEM(shape, values[0].dtype),
        in_specs=[pl.BlockSpec(memory_space=pltpu.HBM)] * len(values),
        out_specs=WHOLE,
        scratch_shapes=[pltpu.SemaphoreType.DMA((len(values),))],
        compiler_params=pltpu.CompilerParams(vmem_limit_bytes=6 * 1024 * 1024),
        name="stack",
    )(*[pltpu.with_memory_space_constraint(value, pltpu.HBM) for value in values])


def widest_first(outer):
    return range(outer - 1, 0, -1)


def added(values):
    total = values[0].astype(jnp.float32)
    for value in values[1:]:
        total = total + value.astype(jnp.float32)
    return total


def on_device(
    state, routes, gates, norm_gain, w_gate, w_up, w_down, spare_gate, spare_up, spare_down
):
    segments = lax.axis_size("segment")
    segments, members = lax.axis_size("segment"), lax.axis_size("expert")
    outer = members // 2
    assert outer & (outer - 1) == 0
    tok_dev = state.shape[1]

    def spread(value):
        got = {j: moved(value, 2 * j, 0) for j in widest_first(outer)}
        return [value] + [got[j] for j in range(1, outer)]

    weights = [w_gate[:, 0], w_up[:, 0], w_down[:, 0]]
    spare_all = [spare_gate[:, 0], spare_up[:, 0], spare_down[:, 0]]

    def fetched(values):
        return [moved(value, 0, -1) for value in values]

    users = [later_users(tick_idx, segments) for tick_idx in range(TICKS)]
    opening = min([tick_idx for tick_idx in range(TICKS) if users[tick_idx]], default=TICKS)
    last = outer // 2
    here = [j for j in range(outer) if j != last]
    head = filled(spare_all[:1], 0)
    head, rest, state, routes, gates = lax.optimization_barrier((head, spare_all[1:], state, routes, gates))
    spares = fetched(head + filled(rest, 0))
    shape = (tok_dev, state.shape[2] + LANES)
    own = small(
        prepare_kernel, jax.ShapeDtypeStruct(shape, state.dtype), state[0],
        jnp.transpose(routes[:, 0], (0, 2, 1)), jnp.transpose(gates[:, 0], (0, 2, 1)),
    )
    other = moved(own, 1, 0)
    pair = small(join_kernel, jax.ShapeDtypeStruct((2 * tok_dev, shape[1]), state.dtype), own, other)
    arrived = spread(pair)
    slots = [loaded(weights, (True, True, False), False)]
    late = stacked(lax.optimization_barrier((*spare_all, arrived[1]))[:3], 1)
    near = [swapped(late, users[opening])] if opening < TICKS else []
    before = run_layer(
        arrived, arrived, norm_gain, slots, [], tick_idx=0, tok_dev=tok_dev, ends=False
    )

    x_blocks = arrived
    for tick_idx in range(TICKS):
        if tick_idx > 0:
            x_blocks = spread(total)
        used = [spares]
        if users[tick_idx]:
            used.append(near if users[tick_idx] <= users[opening] else far)
        layer = functools.partial(run_layer, tick_idx=tick_idx, tok_dev=tok_dev)
        if tick_idx == 0:
            parts = layer(x_blocks, arrived, norm_gain, slots, used, carried=before)
        else:
            most = layer(
                [x_blocks[j] for j in here], [arrived[j] for j in here], norm_gain, slots, used
            )
            rest = layer(x_blocks[last:last + 1], arrived[last:last + 1], norm_gain, slots, used, lead=False)
            parts = most[:last] + rest + most[last:]
        got = [moved(parts[j], 2 * j, 0) for j in widest_first(outer)]
        if tick_idx == 0:
            far = [moved(lax.optimization_barrier((late, parts[0]))[0], 0, -1)]
            tied = lax.optimization_barrier((*weights, parts[0]))[:3]
            gate = loaded(tied[:1], (True,), True)
        if tick_idx + 1 == TICKS:
            total = added([parts[0]] + got)
            other = moved(total[tok_dev:].astype(jnp.bfloat16), 1, 0)
            return added([total[:tok_dev], other]).astype(jnp.bfloat16)[None]
        total = summed([parts[0]] + got)
        across = moved(total, 1, 1)
        along = moved(total, 0, 1)
        if tick_idx == 0:
            tied = lax.optimization_barrier((*weights, total))[:3]
            slots.append(gate + loaded(tied[1:], (True, False), True))
        total = summed([along, across], swap=True)


def solution(mesh):
    return jax.shard_map(
        on_device,
        mesh=mesh,
        in_specs=(
            P("segment", "expert", None),
            P(None, "segment", "expert", None),
            P(None, "segment", "expert", None),
            P(None, "segment", None),
            P(None, "segment", "expert", None),
            P(None, "segment", "expert", None),
            P(None, "segment", "expert", None),
            P(None, "segment", "expert", None),
            P(None, "segment", "expert", None),
            P(None, "segment", "expert", None),
        ),
        out_specs=P("segment", "expert", None),
        check_vma=False,
    )
```

```python
import functools

import jax
import jax.numpy as jnp
from jax import lax
from jax.experimental import pallas as pl
from jax.experimental.pallas import tpu as pltpu
from jax.sharding import PartitionSpec as P

EXPERTS = 4
TICKS = 4
CAP = 4
LANES = 128
BOTH = ("segment", "expert")


EPSILON = 1e-06


def moved(value, flip, steps):
    segments, members = lax.axis_size("segment"), lax.axis_size("expert")
    pairs = [
        (section * members + member, (section + steps) % segments * members + (member ^ flip))
        for section in range(segments)
        for member in range(members)
    ]
    return lax.ppermute(value, BOTH, pairs)


def group_of(section, tick_idx, segments):
    start_segment = (section - tick_idx) % segments
    first_group = jnp.where((start_segment % 2 == 1) & (start_segment + TICKS <= segments), 1, 0)
    return (first_group + jnp.where(start_segment + tick_idx >= segments, 1, 0)).astype(jnp.int32)


def later_users(tick_idx, segments):
    found = set()
    for section in range(segments):
        start = (section - tick_idx) % segments
        first = 1 if start % 2 == 1 and start + TICKS <= segments else 0
        if first + (1 if start + tick_idx >= segments else 0) == 1:
            found.add(section)
    return found


def swapped(value, users):
    segments, members = lax.axis_size("segment"), lax.axis_size("expert")
    partner = {section: section for section in range(segments)}
    for section in users:
        behind = (section + 1) % segments
        assert behind not in users
        partner[section], partner[behind] = behind, section
    pairs = [
        (section * members + member, partner[section] * members + member)
        for section in range(segments)
        for member in range(members)
    ]
    return lax.ppermute(value, BOTH, pairs)


WHOLE = pl.BlockSpec(memory_space=pltpu.VMEM)


def small(kernel, out_shape, *values):
    return pl.pallas_call(
        kernel,
        out_shape=out_shape,
        in_specs=[WHOLE] * len(values),
        out_specs=[WHOLE] * len(out_shape) if isinstance(out_shape, list) else WHOLE,
        compiler_params=pltpu.CompilerParams(vmem_limit_bytes=2 * 1024 * 1024),
    )(*values)


def normed_rows(values, gain_ref, tick_idx):
    group = group_of(lax.axis_index("segment"), tick_idx, lax.axis_size("segment"))
    row_scale = lax.rsqrt(jnp.mean(values * values, axis=-1, keepdims=True) + EPSILON)
    return (values * row_scale * gain_ref[group]).astype(jnp.bfloat16)


def prepare_kernel(state_ref, routes_ref, gates_ref, gain_ref, out_ref):
    rows, width = state_ref.shape
    lane = lax.broadcasted_iota(jnp.int32, (rows, LANES), 1)
    columns = EXPERTS + 1
    routed = jnp.zeros((rows, LANES), jnp.float32)
    member = jnp.zeros((rows, LANES), jnp.float32)
    square = (rows, rows)
    diagonal = lax.broadcasted_iota(jnp.int32, square, 0) == lax.broadcasted_iota(jnp.int32, square, 1)

    def upright(line):
        return jnp.sum(jnp.where(diagonal, line, jnp.zeros_like(line)), axis=1, keepdims=True)

    for tick_idx in range(TICKS):
        for choice in range(routes_ref.shape[1]):
            named = lane == upright(routes_ref[tick_idx, choice:choice + 1, :]) + tick_idx * columns
            routed = routed + jnp.where(named, upright(gates_ref[tick_idx, choice:choice + 1, :]), 0.0)
            member = member + jnp.where(named, 1.0, 0.0)
    row = lax.broadcasted_iota(jnp.int32, (rows, LANES), 0)
    position = jnp.zeros((rows, LANES), jnp.float32)
    for earlier in range(rows - 1):
        position = position + jnp.where(row > earlier, member[earlier:earlier + 1, :], 0.0)
    inside = position < CAP
    table = jnp.where(inside, routed, 0.0)
    over = jnp.where(inside, 0.0, routed)
    for tick_idx in range(TICKS):
        low = tick_idx * columns
        spill = jnp.sum(jnp.where((lane >= low) & (lane < low + EXPERTS), over, 0.0), axis=1, keepdims=True)
        table = jnp.where(lane == low + EXPERTS, spill, table)
    high = table.astype(jnp.bfloat16).astype(jnp.float32)
    both = high + pltpu.roll(table - high, TICKS * columns, 1)
    out_ref[:, :width] = normed_rows(state_ref[...].astype(jnp.float32), gain_ref, 0)
    out_ref[:, width:] = both.astype(jnp.bfloat16)


def join_kernel(first_ref, second_ref, out_ref):
    out_ref[...] = jnp.concatenate([first_ref[...], second_ref[...]], axis=0)


def served(normed, gate, up, down, turned):
    contract = (((1,), (0 if turned else 1,)), ((), ()))
    gate_pre = lax.dot_general(normed, gate, contract, preferred_element_type=jnp.float32)
    up_pre = lax.dot_general(normed, up, contract, preferred_element_type=jnp.float32)
    hidden = (gate_pre / (1.0 + jnp.exp(-gate_pre)) * up_pre).astype(jnp.bfloat16)
    return jnp.dot(hidden, down, preferred_element_type=jnp.float32)


def either(second, bodies):
    if len(bodies) == 1:
        bodies[0]()
    elif bodies:
        pl.when(jnp.logical_not(second))(bodies[0])
        pl.when(second)(bodies[1])


def layer_kernel(*refs, tick_idx, blocks, layer_counts, tok_dev, width, carried, ends):
    row_refs, table_refs, refs = refs[:blocks], refs[blocks:2 * blocks], refs[2 * blocks:]
    own_ref, refs = refs[0], refs[1:]
    if carried:
        carried_ref, refs = refs[0], refs[1:]
    choices = []
    for slot_count, spare_count in layer_counts:
        slot, spare, refs = refs[:slot_count], refs[slot_count:slot_count + spare_count], refs[slot_count + spare_count:]
        choices.append((slot, [spare[0].at[i] for i in range(3)] if spare_count == 1 else spare))
    segments, members = lax.axis_size("segment"), lax.axis_size("expert")
    group = group_of(lax.axis_index("segment"), tick_idx, segments)
    expert = lax.axis_index("expert") // (members // EXPERTS)
    normed = jnp.concatenate([ref[:, :width] for ref in row_refs], axis=0)
    table = jnp.concatenate([ref[:, width:] for ref in table_refs], axis=0).astype(jnp.float32)
    lane = lax.broadcasted_iota(jnp.int32, table.shape, 1)
    columns = TICKS * (EXPERTS + 1)

    def column(at):
        return jnp.sum(jnp.where((lane == at) | (lane == at + columns), table, 0.0), axis=1, keepdims=True)

    share = column(tick_idx * (EXPERTS + 1) + expert)
    spill = column(tick_idx * (EXPERTS + 1) + EXPERTS)
    per = 2 * tok_dev

    def run(slot, spare):
        total = carried_ref[...] if carried else share * served(normed, *[ref[...] for ref in slot], True)
        if spare:
            total = total + spill * served(normed, *[ref[...] for ref in spare], False)
        if not ends:
            refs[0][...] = total
            return
        own = jnp.concatenate([own_ref[...].astype(jnp.float32), jnp.zeros((tok_dev, width), jnp.float32)], axis=0)
        refs[0][...] = total[0:per] + own
        for i in range(1, blocks):
            refs[i][...] = total[i * per:(i + 1) * per].astype(jnp.bfloat16)

    either(group == 1, [functools.partial(run, *choice) for choice in choices])


def resident(values):
    return [pltpu.with_memory_space_constraint(value, pltpu.VMEM) for value in values]


def run_layer(rows, tables, own, layers, *, tick_idx, tok_dev, carried=None, ends=True):
    blocks = len(rows)
    width = own.shape[-1]
    per = 2 * tok_dev
    values = [*rows, *tables, own]
    if carried is not None:
        values.append(carried)
    for slot, spare in layers:
        values += resident([*slot, *spare])
    slot, spare = layers[0]
    hidden = (slot[2].shape[0] if slot else 0) + (spare[-1].shape[-2] if spare else 0)
    whole = jax.ShapeDtypeStruct((per * blocks, width), jnp.float32)
    parts = [jax.ShapeDtypeStruct((per, width), jnp.float32)]
    parts += [jax.ShapeDtypeStruct((per, width), jnp.bfloat16)] * (blocks - 1)
    return pl.pallas_call(
        functools.partial(
            layer_kernel, tick_idx=tick_idx, blocks=blocks, tok_dev=tok_dev, width=width, ends=ends,
            layer_counts=[(len(slot), len(spare)) for slot, spare in layers], carried=carried is not None,
        ),
        out_shape=parts if ends else whole,
        in_specs=[WHOLE] * len(values),
        out_specs=[WHOLE] * blocks if ends else WHOLE,
        compiler_params=pltpu.CompilerParams(vmem_limit_bytes=12 * 1024 * 1024),
        cost_estimate=pl.CostEstimate(
            flops=6 * per * blocks * hidden * width, bytes_accessed=6 * hidden * width,
            transcendentals=per * blocks * hidden,
        ),
        name="layer",
    )(*values)


def sum_kernel(*refs):
    refs[-1][...] = added([ref[...] for ref in refs[:-1]]).astype(jnp.bfloat16)


def summed(values):
    shape = jax.ShapeDtypeStruct(values[0].shape, jnp.bfloat16)
    return small(sum_kernel, shape, *values)


def arrive_kernel(along_ref, across_ref, gain_ref, own_ref, normed_ref, *, tick_idx):
    across = across_ref[...].astype(jnp.float32)
    half = across.shape[0] // 2
    total = along_ref[...].astype(jnp.float32) + jnp.concatenate([across[half:], across[:half]], axis=0)
    total = total.astype(jnp.bfloat16)
    own_ref[...] = total[:half]
    normed_ref[...] = normed_rows(total.astype(jnp.float32), gain_ref, tick_idx)


def arriving(along, across, gain, tick_idx):
    rows, width = along.shape
    shapes = [jax.ShapeDtypeStruct((count, width), jnp.bfloat16) for count in (rows // 2, rows)]
    return small(functools.partial(arrive_kernel, tick_idx=tick_idx), shapes, along, across, gain)


def fill_kernel(*refs, group):
    count = len(refs) // 2
    ins, outs, sems = refs[:count], refs[count:2 * count], refs[2 * count]
    copies = [
        pltpu.make_async_copy(one if group is None else one.at[group], out, sems.at[i])
        for i, (one, out) in enumerate(zip(ins, outs))
    ]
    for copy in copies:
        copy.start()
    for copy in copies:
        copy.wait()


def filled(values, group=None):
    shapes = [value.shape if group is None else value.shape[1:] for value in values]
    return pl.pallas_call(
        functools.partial(fill_kernel, group=group),
        out_shape=[pltpu.VMEM(shape, value.dtype) for shape, value in zip(shapes, values)],
        in_specs=[pl.BlockSpec(memory_space=pltpu.HBM)] * len(values),
        out_specs=[WHOLE] * len(values),
        scratch_shapes=[pltpu.SemaphoreType.DMA((len(values),))],
        compiler_params=pltpu.CompilerParams(vmem_limit_bytes=1024 * 1024),
        name="fill",
    )(*[pltpu.with_memory_space_constraint(value, pltpu.HBM) for value in values])


def load_kernel(*refs, turned, group):
    count = len(turned)
    ins, outs, (held, sems, straight) = refs[:count], refs[count:2 * count], refs[2 * count:]
    depth, block = held.shape[:2]
    work = [
        (ins[i], outs[i], low) for i in range(count) if turned[i] for low in range(0, ins[i].shape[1], block)
    ]

    def copy_of(at):
        source, _, low = work[at]
        return pltpu.make_async_copy(source.at[group, pl.ds(low, block), :], held.at[at % depth], sems.at[at % depth])

    for at in range(min(depth - 1, len(work))):
        copy_of(at).start()
    direct = [
        pltpu.make_async_copy(ins[i].at[group], outs[i], straight.at[i]) for i in range(count) if not turned[i]
    ]
    for copy in direct:
        copy.start()
    for at, (_, out, low) in enumerate(work):
        if at + depth - 1 < len(work):
            copy_of(at + depth - 1).start()
        copy_of(at).wait()
        out[:, low:low + block] = held[at % depth].T
    for copy in direct:
        copy.wait()


def loaded(values, turned, group):
    hidden, width = values[0].shape[1:]
    block = LANES if hidden % LANES == 0 else hidden
    return pl.pallas_call(
        functools.partial(load_kernel, turned=turned, group=group),
        out_shape=[
            pltpu.VMEM((width, hidden) if flip else (hidden, width), value.dtype)
            for value, flip in zip(values, turned)
        ],
        in_specs=[pl.BlockSpec(memory_space=pltpu.HBM)] * len(values),
        out_specs=[WHOLE] * len(values),
        scratch_shapes=[
            pltpu.VMEM((4, block, width), values[0].dtype),
            pltpu.SemaphoreType.DMA((4,)),
            pltpu.SemaphoreType.DMA((len(values),)),
        ],
        compiler_params=pltpu.CompilerParams(vmem_limit_bytes=6 * 1024 * 1024),
        name="load",
    )(*[pltpu.with_memory_space_constraint(value, pltpu.HBM) for value in values])


def stack_kernel(*refs, group):
    ins, out, sems = refs[:-2], refs[-2], refs[-1]
    copies = [pltpu.make_async_copy(one.at[group], out.at[i], sems.at[i]) for i, one in enumerate(ins)]
    for copy in copies:
        copy.start()
    for copy in copies:
        copy.wait()


def stacked(values, group):
    shape = (len(values),) + values[0].shape[1:]
    return pl.pallas_call(
        functools.partial(stack_kernel, group=group),
        out_shape=pltpu.VMEM(shape, values[0].dtype),
        in_specs=[pl.BlockSpec(memory_space=pltpu.HBM)] * len(values),
        out_specs=WHOLE,
        scratch_shapes=[pltpu.SemaphoreType.DMA((len(values),))],
        compiler_params=pltpu.CompilerParams(vmem_limit_bytes=6 * 1024 * 1024),
        name="stack",
    )(*[pltpu.with_memory_space_constraint(value, pltpu.HBM) for value in values])


def widest_first(outer):
    return range(outer - 1, 0, -1)


def added(values):
    total = values[0].astype(jnp.float32)
    for value in values[1:]:
        total = total + value.astype(jnp.float32)
    return total


def on_device(
    state, routes, gates, norm_gain, w_gate, w_up, w_down, spare_gate, spare_up, spare_down
):
    segments = lax.axis_size("segment")
    segments, members = lax.axis_size("segment"), lax.axis_size("expert")
    outer = members // 2
    assert outer & (outer - 1) == 0
    tok_dev = state.shape[1]

    def spread(value):
        got = {j: moved(value, 2 * j, 0) for j in widest_first(outer)}
        return [value] + [got[j] for j in range(1, outer)]

    weights = [w_gate[:, 0], w_up[:, 0], w_down[:, 0]]
    spare_all = [spare_gate[:, 0], spare_up[:, 0], spare_down[:, 0]]

    def fetched(values):
        return [moved(value, 0, -1) for value in values]

    head = filled(spare_all[:1], 0)
    head, rest, state, routes, gates = lax.optimization_barrier((head, spare_all[1:], state, routes, gates))
    spares = [fetched(head + filled(rest, 0))]
    shape = (tok_dev, state.shape[2] + LANES)
    own = small(
        prepare_kernel, jax.ShapeDtypeStruct(shape, state.dtype), state[0],
        jnp.transpose(routes[:, 0], (0, 2, 1)), jnp.transpose(gates[:, 0], (0, 2, 1)), norm_gain,
    )
    other = moved(own, 1, 0)
    pair = small(join_kernel, jax.ShapeDtypeStruct((2 * tok_dev, shape[1]), state.dtype), own, other)
    arrived = spread(pair)
    users = [later_users(tick_idx, segments) for tick_idx in range(TICKS)]
    opening = min([tick_idx for tick_idx in range(TICKS) if users[tick_idx]], default=TICKS)
    slots = [loaded(weights, (True, True, False), 0)]
    if users[0]:
        slots.append(loaded(weights, (True, True, False), 1))
    late = stacked(lax.optimization_barrier((*spare_all, arrived[1]))[:3], 1)
    near = [swapped(late, users[opening])] if opening < TICKS else []
    own = state[0]
    before = run_layer(arrived, arrived, own, [(slot, []) for slot in slots], tick_idx=0, tok_dev=tok_dev, ends=False)

    rows = arrived
    for tick_idx in range(TICKS):
        layers = [(slots[0], spares[0])]
        if users[tick_idx]:
            layers.append((slots[1], near if users[tick_idx] <= users[opening] else far))
        if tick_idx == 0:
            layers = [([], spare) for _, spare in layers]
        parts = run_layer(
            rows, arrived, own, layers, tick_idx=tick_idx, tok_dev=tok_dev,
            carried=before if tick_idx == 0 else None,
        )
        got = [moved(parts[j], 2 * j, 0) for j in widest_first(outer)]
        if tick_idx == 0 and not users[0]:
            tied = lax.optimization_barrier((*weights, parts[0]))[:3]
            gate = loaded(tied[:1], (True,), 1)
        if tick_idx + 1 == TICKS:
            total = added([parts[0]] + got)
            other = moved(total[tok_dev:].astype(jnp.bfloat16), 1, 0)
            return added([total[:tok_dev], other]).astype(jnp.bfloat16)[None]
        total = summed([parts[0]] + got)
        across = moved(total, 1, 1)
        along = moved(total, 0, 1)
        if tick_idx == 0:
            far = [moved(lax.optimization_barrier((late, total))[0], 0, -1)]
            if not users[0]:
                tied = lax.optimization_barrier((*weights, total))[:3]
                slots.append(gate + loaded(tied[1:], (True, False), 1))
        own, normed = arriving(along, across, norm_gain, tick_idx + 1)
        rows = spread(normed)


def solution(mesh):
    return jax.shard_map(
        on_device,
        mesh=mesh,
        in_specs=(
            P("segment", "expert", None),
            P(None, "segment", "expert", None),
            P(None, "segment", "expert", None),
            P(None, "segment", None),
            P(None, "segment", "expert", None),
            P(None, "segment", "expert", None),
            P(None, "segment", "expert", None),
            P(None, "segment", "expert", None),
            P(None, "segment", "expert", None),
            P(None, "segment", "expert", None),
        ),
        out_specs=P("segment", "expert", None),
        check_vma=False,
    )
```

```python
import functools

import jax
import jax.numpy as jnp
from jax import lax
from jax.experimental import pallas as pl
from jax.experimental.pallas import tpu as pltpu
from jax.sharding import PartitionSpec as P

EXPERTS = 4
TICKS = 4
CAP = 4
LANES = 128
BOTH = ("segment", "expert")


EPSILON = 1e-06


def moved(value, flip, steps):
    segments, members = lax.axis_size("segment"), lax.axis_size("expert")
    pairs = [
        (section * members + member, (section + steps) % segments * members + (member ^ flip))
        for section in range(segments)
        for member in range(members)
    ]
    return lax.ppermute(value, BOTH, pairs)


def group_of(section, tick_idx, segments):
    start_segment = (section - tick_idx) % segments
    first_group = jnp.where((start_segment % 2 == 1) & (start_segment + TICKS <= segments), 1, 0)
    return (first_group + jnp.where(start_segment + tick_idx >= segments, 1, 0)).astype(jnp.int32)


def later_users(tick_idx, segments):
    found = set()
    for section in range(segments):
        start = (section - tick_idx) % segments
        first = 1 if start % 2 == 1 and start + TICKS <= segments else 0
        if first + (1 if start + tick_idx >= segments else 0) == 1:
            found.add(section)
    return found


def swapped(value, users):
    segments, members = lax.axis_size("segment"), lax.axis_size("expert")
    partner = {section: section for section in range(segments)}
    for section in users:
        behind = (section + 1) % segments
        assert behind not in users
        partner[section], partner[behind] = behind, section
    pairs = [
        (section * members + member, partner[section] * members + member)
        for section in range(segments)
        for member in range(members)
    ]
    return lax.ppermute(value, BOTH, pairs)


WHOLE = pl.BlockSpec(memory_space=pltpu.VMEM)


def small(kernel, out_shape, *values):
    return pl.pallas_call(
        kernel,
        out_shape=out_shape,
        in_specs=[WHOLE] * len(values),
        out_specs=[WHOLE] * len(out_shape) if isinstance(out_shape, list) else WHOLE,
        compiler_params=pltpu.CompilerParams(vmem_limit_bytes=2 * 1024 * 1024),
    )(*values)


def normed_rows(values, gain_ref, tick_idx):
    group = group_of(lax.axis_index("segment"), tick_idx, lax.axis_size("segment"))
    row_scale = lax.rsqrt(jnp.mean(values * values, axis=-1, keepdims=True) + EPSILON)
    return (values * row_scale * gain_ref[group]).astype(jnp.bfloat16)


def prepare_kernel(state_ref, routes_ref, gates_ref, gain_ref, out_ref):
    rows, width = state_ref.shape
    lane = lax.broadcasted_iota(jnp.int32, (rows, LANES), 1)
    columns = EXPERTS + 1
    routed = jnp.zeros((rows, LANES), jnp.float32)
    member = jnp.zeros((rows, LANES), jnp.float32)
    square = (rows, rows)
    diagonal = lax.broadcasted_iota(jnp.int32, square, 0) == lax.broadcasted_iota(jnp.int32, square, 1)

    def upright(line):
        return jnp.sum(jnp.where(diagonal, line, jnp.zeros_like(line)), axis=1, keepdims=True)

    for tick_idx in range(TICKS):
        for choice in range(routes_ref.shape[1]):
            named = lane == upright(routes_ref[tick_idx, choice:choice + 1, :]) + tick_idx * columns
            routed = routed + jnp.where(named, upright(gates_ref[tick_idx, choice:choice + 1, :]), 0.0)
            member = member + jnp.where(named, 1.0, 0.0)
    row = lax.broadcasted_iota(jnp.int32, (rows, LANES), 0)
    position = jnp.zeros((rows, LANES), jnp.float32)
    for earlier in range(rows - 1):
        position = position + jnp.where(row > earlier, member[earlier:earlier + 1, :], 0.0)
    inside = position < CAP
    table = jnp.where(inside, routed, 0.0)
    over = jnp.where(inside, 0.0, routed)
    for tick_idx in range(TICKS):
        low = tick_idx * columns
        spill = jnp.sum(jnp.where((lane >= low) & (lane < low + EXPERTS), over, 0.0), axis=1, keepdims=True)
        table = jnp.where(lane == low + EXPERTS, spill, table)
    high = table.astype(jnp.bfloat16).astype(jnp.float32)
    both = high + pltpu.roll(table - high, TICKS * columns, 1)
    out_ref[:, :width] = normed_rows(state_ref[...].astype(jnp.float32), gain_ref, 0)
    out_ref[:, width:] = both.astype(jnp.bfloat16)


def join_kernel(first_ref, second_ref, out_ref):
    out_ref[...] = jnp.concatenate([first_ref[...], second_ref[...]], axis=0)


def served(normed, gate, up, down, turned):
    contract = (((1,), (0 if turned else 1,)), ((), ()))
    gate_pre = lax.dot_general(normed, gate, contract, preferred_element_type=jnp.float32)
    up_pre = lax.dot_general(normed, up, contract, preferred_element_type=jnp.float32)
    hidden = (gate_pre / (1.0 + jnp.exp(-gate_pre)) * up_pre).astype(jnp.bfloat16)
    return jnp.dot(hidden, down, preferred_element_type=jnp.float32)


def either(second, bodies):
    if len(bodies) == 1:
        bodies[0]()
    elif bodies:
        pl.when(jnp.logical_not(second))(bodies[0])
        pl.when(second)(bodies[1])


def layer_kernel(*refs, tick_idx, blocks, layer_counts, tok_dev, width, carried, ends):
    row_refs, table_refs, refs = refs[:blocks], refs[blocks:2 * blocks], refs[2 * blocks:]
    own_ref, refs = refs[0], refs[1:]
    if carried:
        carried_ref, refs = refs[0], refs[1:]
    choices = []
    for slot_count, spare_count in layer_counts:
        slot, spare, refs = refs[:slot_count], refs[slot_count:slot_count + spare_count], refs[slot_count + spare_count:]
        choices.append((slot, [spare[0].at[i] for i in range(3)] if spare_count == 1 else spare))
    segments, members = lax.axis_size("segment"), lax.axis_size("expert")
    group = group_of(lax.axis_index("segment"), tick_idx, segments)
    expert = lax.axis_index("expert") // (members // EXPERTS)
    normed = jnp.concatenate([ref[:, :width] for ref in row_refs], axis=0)
    table = jnp.concatenate([ref[:, width:] for ref in table_refs], axis=0).astype(jnp.float32)
    lane = lax.broadcasted_iota(jnp.int32, table.shape, 1)
    columns = TICKS * (EXPERTS + 1)

    def column(at):
        return jnp.sum(jnp.where((lane == at) | (lane == at + columns), table, 0.0), axis=1, keepdims=True)

    share = column(tick_idx * (EXPERTS + 1) + expert)
    spill = column(tick_idx * (EXPERTS + 1) + EXPERTS)
    per = 2 * tok_dev

    def run(slot, spare):
        total = carried_ref[...] if carried else share * served(normed, *[ref[...] for ref in slot], True)
        if spare:
            total = total + spill * served(normed, *[ref[...] for ref in spare], False)
        if not ends:
            refs[0][...] = total
            return
        own = jnp.concatenate([own_ref[...].astype(jnp.float32), jnp.zeros((tok_dev, width), jnp.float32)], axis=0)
        refs[0][...] = total[0:per] + own
        for i in range(1, blocks):
            refs[i][...] = total[i * per:(i + 1) * per].astype(jnp.bfloat16)

    either(group == 1, [functools.partial(run, *choice) for choice in choices])


def resident(values):
    return [pltpu.with_memory_space_constraint(value, pltpu.VMEM) for value in values]


def run_layer(rows, tables, own, layers, *, tick_idx, tok_dev, carried=None, ends=True):
    blocks = len(rows)
    width = own.shape[-1]
    per = 2 * tok_dev
    values = [*rows, *tables, own]
    if carried is not None:
        values.append(carried)
    for slot, spare in layers:
        values += resident([*slot, *spare])
    slot, spare = layers[0]
    hidden = (slot[2].shape[0] if slot else 0) + (spare[-1].shape[-2] if spare else 0)
    whole = jax.ShapeDtypeStruct((per * blocks, width), jnp.float32)
    parts = [jax.ShapeDtypeStruct((per, width), jnp.float32)]
    parts += [jax.ShapeDtypeStruct((per, width), jnp.bfloat16)] * (blocks - 1)
    return pl.pallas_call(
        functools.partial(
            layer_kernel, tick_idx=tick_idx, blocks=blocks, tok_dev=tok_dev, width=width, ends=ends,
            layer_counts=[(len(slot), len(spare)) for slot, spare in layers], carried=carried is not None,
        ),
        out_shape=parts if ends else whole,
        in_specs=[WHOLE] * len(values),
        out_specs=[WHOLE] * blocks if ends else WHOLE,
        compiler_params=pltpu.CompilerParams(vmem_limit_bytes=12 * 1024 * 1024),
        cost_estimate=pl.CostEstimate(
            flops=6 * per * blocks * hidden * width, bytes_accessed=6 * hidden * width,
            transcendentals=per * blocks * hidden,
        ),
        name="layer",
    )(*values)


def sum_kernel(*refs):
    refs[-1][...] = added([ref[...] for ref in refs[:-1]]).astype(jnp.bfloat16)


def summed(values):
    shape = jax.ShapeDtypeStruct(values[0].shape, jnp.bfloat16)
    return small(sum_kernel, shape, *values)


def arrive_kernel(along_ref, across_ref, gain_ref, own_ref, normed_ref, *, tick_idx):
    across = across_ref[...].astype(jnp.float32)
    half = across.shape[0] // 2
    total = along_ref[...].astype(jnp.float32) + jnp.concatenate([across[half:], across[:half]], axis=0)
    total = total.astype(jnp.bfloat16)
    own_ref[...] = total[:half]
    normed_ref[...] = normed_rows(total.astype(jnp.float32), gain_ref, tick_idx)


def arriving(along, across, gain, tick_idx):
    rows, width = along.shape
    shapes = [jax.ShapeDtypeStruct((count, width), jnp.bfloat16) for count in (rows // 2, rows)]
    return small(functools.partial(arrive_kernel, tick_idx=tick_idx), shapes, along, across, gain)


def fill_kernel(*refs, group):
    count = len(refs) // 2
    ins, outs, sems = refs[:count], refs[count:2 * count], refs[2 * count]
    copies = [
        pltpu.make_async_copy(one if group is None else one.at[group], out, sems.at[i])
        for i, (one, out) in enumerate(zip(ins, outs))
    ]
    for copy in copies:
        copy.start()
    for copy in copies:
        copy.wait()


def filled(values, group=None):
    shapes = [value.shape if group is None else value.shape[1:] for value in values]
    return pl.pallas_call(
        functools.partial(fill_kernel, group=group),
        out_shape=[pltpu.VMEM(shape, value.dtype) for shape, value in zip(shapes, values)],
        in_specs=[pl.BlockSpec(memory_space=pltpu.HBM)] * len(values),
        out_specs=[WHOLE] * len(values),
        scratch_shapes=[pltpu.SemaphoreType.DMA((len(values),))],
        compiler_params=pltpu.CompilerParams(vmem_limit_bytes=1024 * 1024),
        name="fill",
    )(*[pltpu.with_memory_space_constraint(value, pltpu.HBM) for value in values])


def load_kernel(*refs, turned, group):
    count = len(turned)
    ins, outs, (held, sems, straight) = refs[:count], refs[count:2 * count], refs[2 * count:]
    depth, block = held.shape[:2]
    work = [
        (ins[i], outs[i], low) for i in range(count) if turned[i] for low in range(0, ins[i].shape[1], block)
    ]

    def copy_of(at):
        source, _, low = work[at]
        return pltpu.make_async_copy(source.at[group, pl.ds(low, block), :], held.at[at % depth], sems.at[at % depth])

    for at in range(min(depth - 1, len(work))):
        copy_of(at).start()
    direct = [
        pltpu.make_async_copy(ins[i].at[group], outs[i], straight.at[i]) for i in range(count) if not turned[i]
    ]
    for copy in direct:
        copy.start()
    for at, (_, out, low) in enumerate(work):
        if at + depth - 1 < len(work):
            copy_of(at + depth - 1).start()
        copy_of(at).wait()
        out[:, low:low + block] = held[at % depth].T
    for copy in direct:
        copy.wait()


def loaded(values, turned, group):
    hidden, width = values[0].shape[1:]
    block = LANES if hidden % LANES == 0 else hidden
    return pl.pallas_call(
        functools.partial(load_kernel, turned=turned, group=group),
        out_shape=[
            pltpu.VMEM((width, hidden) if flip else (hidden, width), value.dtype)
            for value, flip in zip(values, turned)
        ],
        in_specs=[pl.BlockSpec(memory_space=pltpu.HBM)] * len(values),
        out_specs=[WHOLE] * len(values),
        scratch_shapes=[
            pltpu.VMEM((4, block, width), values[0].dtype),
            pltpu.SemaphoreType.DMA((4,)),
            pltpu.SemaphoreType.DMA((len(values),)),
        ],
        compiler_params=pltpu.CompilerParams(vmem_limit_bytes=6 * 1024 * 1024),
        name="load",
    )(*[pltpu.with_memory_space_constraint(value, pltpu.HBM) for value in values])


def stack_kernel(*refs, group):
    ins, out, sems = refs[:-2], refs[-2], refs[-1]
    copies = [pltpu.make_async_copy(one.at[group], out.at[i], sems.at[i]) for i, one in enumerate(ins)]
    for copy in copies:
        copy.start()
    for copy in copies:
        copy.wait()


def stacked(values, group):
    shape = (len(values),) + values[0].shape[1:]
    return pl.pallas_call(
        functools.partial(stack_kernel, group=group),
        out_shape=pltpu.VMEM(shape, values[0].dtype),
        in_specs=[pl.BlockSpec(memory_space=pltpu.HBM)] * len(values),
        out_specs=WHOLE,
        scratch_shapes=[pltpu.SemaphoreType.DMA((len(values),))],
        compiler_params=pltpu.CompilerParams(vmem_limit_bytes=6 * 1024 * 1024),
        name="stack",
    )(*[pltpu.with_memory_space_constraint(value, pltpu.HBM) for value in values])


def widest_first(outer):
    return list(range(outer - 1, 0, -1))


def half_first(outer):
    return [outer // 2] + [j for j in widest_first(outer) if j != outer // 2]


def added(values):
    total = values[0].astype(jnp.float32)
    for value in values[1:]:
        total = total + value.astype(jnp.float32)
    return total


def on_device(
    state, routes, gates, norm_gain, w_gate, w_up, w_down, spare_gate, spare_up, spare_down
):
    segments = lax.axis_size("segment")
    segments, members = lax.axis_size("segment"), lax.axis_size("expert")
    outer = members // 2
    assert outer & (outer - 1) == 0
    tok_dev = state.shape[1]

    def spread(value):
        got = {j: moved(value, 2 * j, 0) for j in half_first(outer)}
        return [value] + [got[j] for j in range(1, outer)]

    weights = [w_gate[:, 0], w_up[:, 0], w_down[:, 0]]
    spare_all = [spare_gate[:, 0], spare_up[:, 0], spare_down[:, 0]]

    def fetched(values):
        return [moved(value, 0, -1) for value in values]

    head = filled(spare_all[:1], 0)
    head, rest, state, routes, gates = lax.optimization_barrier((head, spare_all[1:], state, routes, gates))
    spares = [fetched(head + filled(rest, 0))]
    shape = (tok_dev, state.shape[2] + LANES)
    own = small(
        prepare_kernel, jax.ShapeDtypeStruct(shape, state.dtype), state[0],
        jnp.transpose(routes[:, 0], (0, 2, 1)), jnp.transpose(gates[:, 0], (0, 2, 1)), norm_gain,
    )
    other = moved(own, 1, 0)
    pair = small(join_kernel, jax.ShapeDtypeStruct((2 * tok_dev, shape[1]), state.dtype), own, other)
    arrived = spread(pair)
    users = [later_users(tick_idx, segments) for tick_idx in range(TICKS)]
    opening = min([tick_idx for tick_idx in range(TICKS) if users[tick_idx]], default=TICKS)
    slots = [loaded(weights, (True, True, False), 0)]
    if users[0]:
        slots.append(loaded(weights, (True, True, False), 1))
    late = stacked(lax.optimization_barrier((*spare_all, arrived[1]))[:3], 1)
    near = [swapped(late, users[opening])] if opening < TICKS else []
    own = state[0]
    before = run_layer(arrived, arrived, own, [(slot, []) for slot in slots], tick_idx=0, tok_dev=tok_dev, ends=False)

    rows = arrived
    for tick_idx in range(TICKS):
        layers = [(slots[0], spares[0])]
        if users[tick_idx]:
            layers.append((slots[1], near if users[tick_idx] <= users[opening] else far))
        if tick_idx == 0:
            layers = [([], spare) for _, spare in layers]
        parts = run_layer(
            rows, arrived, own, layers, tick_idx=tick_idx, tok_dev=tok_dev,
            carried=before if tick_idx == 0 else None,
        )
        got = [moved(parts[j], 2 * j, 0) for j in widest_first(outer)]
        if tick_idx == 0 and not users[0]:
            tied = lax.optimization_barrier((*weights, parts[0]))[:3]
            gate = loaded(tied[:1], (True,), 1)
        if tick_idx + 1 == TICKS:
            total = added([parts[0]] + got)
            other = moved(total[tok_dev:].astype(jnp.bfloat16), 1, 0)
            return added([total[:tok_dev], other]).astype(jnp.bfloat16)[None]
        total = summed([parts[0]] + got)
        across = moved(total, 1, 1)
        along = moved(total, 0, 1)
        if tick_idx == 0:
            far = [moved(lax.optimization_barrier((late, total))[0], 0, -1)]
            if not users[0]:
                tied = lax.optimization_barrier((*weights, total))[:3]
                slots.append(gate + loaded(tied[1:], (True, False), 1))
        own, normed = arriving(along, across, norm_gain, tick_idx + 1)
        rows = spread(normed)


def solution(mesh):
    return jax.shard_map(
        on_device,
        mesh=mesh,
        in_specs=(
            P("segment", "expert", None),
            P(None, "segment", "expert", None),
            P(None, "segment", "expert", None),
            P(None, "segment", None),
            P(None, "segment", "expert", None),
            P(None, "segment", "expert", None),
            P(None, "segment", "expert", None),
            P(None, "segment", "expert", None),
            P(None, "segment", "expert", None),
            P(None, "segment", "expert", None),
        ),
        out_specs=P("segment", "expert", None),
        check_vma=False,
    )
```

```python
import functools

import jax
import jax.numpy as jnp
from jax import lax
from jax.experimental import pallas as pl
from jax.experimental.pallas import tpu as pltpu
from jax.sharding import PartitionSpec as P

EXPERTS = 4
TICKS = 4
CAP = 4
LANES = 128
BOTH = ("segment", "expert")


EPSILON = 1e-06


def moved(value, flip, steps):
    segments, members = lax.axis_size("segment"), lax.axis_size("expert")
    pairs = [
        (section * members + member, (section + steps) % segments * members + (member ^ flip))
        for section in range(segments)
        for member in range(members)
    ]
    return lax.ppermute(value, BOTH, pairs)


def group_of(section, tick_idx, segments):
    start_segment = (section - tick_idx) % segments
    first_group = jnp.where((start_segment % 2 == 1) & (start_segment + TICKS <= segments), 1, 0)
    return (first_group + jnp.where(start_segment + tick_idx >= segments, 1, 0)).astype(jnp.int32)


def later_users(tick_idx, segments):
    found = set()
    for section in range(segments):
        start = (section - tick_idx) % segments
        first = 1 if start % 2 == 1 and start + TICKS <= segments else 0
        if first + (1 if start + tick_idx >= segments else 0) == 1:
            found.add(section)
    return found


def swapped(value, users):
    segments, members = lax.axis_size("segment"), lax.axis_size("expert")
    partner = {section: section for section in range(segments)}
    for section in users:
        behind = (section + 1) % segments
        assert behind not in users
        partner[section], partner[behind] = behind, section
    pairs = [
        (section * members + member, partner[section] * members + member)
        for section in range(segments)
        for member in range(members)
    ]
    return lax.ppermute(value, BOTH, pairs)


WHOLE = pl.BlockSpec(memory_space=pltpu.VMEM)


def small(kernel, out_shape, *values):
    return pl.pallas_call(
        kernel,
        out_shape=out_shape,
        in_specs=[WHOLE] * len(values),
        out_specs=[WHOLE] * len(out_shape) if isinstance(out_shape, list) else WHOLE,
        compiler_params=pltpu.CompilerParams(vmem_limit_bytes=2 * 1024 * 1024),
    )(*values)


def normed_rows(values, gain_ref, tick_idx):
    group = group_of(lax.axis_index("segment"), tick_idx, lax.axis_size("segment"))
    row_scale = lax.rsqrt(jnp.mean(values * values, axis=-1, keepdims=True) + EPSILON)
    return (values * row_scale * gain_ref[group]).astype(jnp.bfloat16)


def prepare_kernel(state_ref, routes_ref, gates_ref, gain_ref, out_ref):
    rows, width = state_ref.shape
    lane = lax.broadcasted_iota(jnp.int32, (rows, LANES), 1)
    columns = EXPERTS + 1
    routed = jnp.zeros((rows, LANES), jnp.float32)
    member = jnp.zeros((rows, LANES), jnp.float32)
    square = (rows, rows)
    diagonal = lax.broadcasted_iota(jnp.int32, square, 0) == lax.broadcasted_iota(jnp.int32, square, 1)

    def upright(line):
        return jnp.sum(jnp.where(diagonal, line, jnp.zeros_like(line)), axis=1, keepdims=True)

    for tick_idx in range(TICKS):
        for choice in range(routes_ref.shape[1]):
            named = lane == upright(routes_ref[tick_idx, choice:choice + 1, :]) + tick_idx * columns
            routed = routed + jnp.where(named, upright(gates_ref[tick_idx, choice:choice + 1, :]), 0.0)
            member = member + jnp.where(named, 1.0, 0.0)
    row = lax.broadcasted_iota(jnp.int32, (rows, LANES), 0)
    position = jnp.zeros((rows, LANES), jnp.float32)
    for earlier in range(rows - 1):
        position = position + jnp.where(row > earlier, member[earlier:earlier + 1, :], 0.0)
    inside = position < CAP
    table = jnp.where(inside, routed, 0.0)
    over = jnp.where(inside, 0.0, routed)
    for tick_idx in range(TICKS):
        low = tick_idx * columns
        spill = jnp.sum(jnp.where((lane >= low) & (lane < low + EXPERTS), over, 0.0), axis=1, keepdims=True)
        table = jnp.where(lane == low + EXPERTS, spill, table)
    high = table.astype(jnp.bfloat16).astype(jnp.float32)
    both = high + pltpu.roll(table - high, TICKS * columns, 1)
    out_ref[:, :width] = normed_rows(state_ref[...].astype(jnp.float32), gain_ref, 0)
    out_ref[:, width:] = both.astype(jnp.bfloat16)


def join_kernel(first_ref, second_ref, out_ref):
    out_ref[...] = jnp.concatenate([first_ref[...], second_ref[...]], axis=0)


def served(normed, gate, up, down, turned):
    contract = (((1,), (0 if turned else 1,)), ((), ()))
    gate_pre = lax.dot_general(normed, gate, contract, preferred_element_type=jnp.float32)
    up_pre = lax.dot_general(normed, up, contract, preferred_element_type=jnp.float32)
    hidden = (gate_pre / (1.0 + jnp.exp(-gate_pre)) * up_pre).astype(jnp.bfloat16)
    return jnp.dot(hidden, down, preferred_element_type=jnp.float32)


def either(second, bodies):
    if len(bodies) == 1:
        bodies[0]()
    elif bodies:
        pl.when(jnp.logical_not(second))(bodies[0])
        pl.when(second)(bodies[1])


def layer_kernel(*refs, tick_idx, blocks, layer_counts, tok_dev, width, carried, ends):
    row_refs, table_refs, refs = refs[:blocks], refs[blocks:2 * blocks], refs[2 * blocks:]
    own_ref, refs = refs[0], refs[1:]
    if carried:
        carried_ref, refs = refs[0], refs[1:]
    choices = []
    for slot_count, spare_count in layer_counts:
        slot, spare, refs = refs[:slot_count], refs[slot_count:slot_count + spare_count], refs[slot_count + spare_count:]
        choices.append((slot, [spare[0].at[i] for i in range(3)] if spare_count == 1 else spare))
    segments, members = lax.axis_size("segment"), lax.axis_size("expert")
    group = group_of(lax.axis_index("segment"), tick_idx, segments)
    expert = lax.axis_index("expert") // (members // EXPERTS)
    normed = jnp.concatenate([ref[:, :width] for ref in row_refs], axis=0)
    table = jnp.concatenate([ref[:, width:] for ref in table_refs], axis=0).astype(jnp.float32)
    lane = lax.broadcasted_iota(jnp.int32, table.shape, 1)
    columns = TICKS * (EXPERTS + 1)

    def column(at):
        return jnp.sum(jnp.where((lane == at) | (lane == at + columns), table, 0.0), axis=1, keepdims=True)

    share = column(tick_idx * (EXPERTS + 1) + expert)
    spill = column(tick_idx * (EXPERTS + 1) + EXPERTS)
    per = 2 * tok_dev

    def run(slot, spare):
        total = carried_ref[...] if carried else share * served(normed, *[ref[...] for ref in slot], True)
        if spare:
            total = total + spill * served(normed, *[ref[...] for ref in spare], False)
        if not ends:
            refs[0][...] = total
            return
        own = jnp.concatenate([own_ref[...].astype(jnp.float32), jnp.zeros((tok_dev, width), jnp.float32)], axis=0)
        refs[0][...] = total[0:per] + own
        for i in range(1, blocks):
            refs[i][...] = total[i * per:(i + 1) * per].astype(jnp.bfloat16)

    either(group == 1, [functools.partial(run, *choice) for choice in choices])


def resident(values):
    return [pltpu.with_memory_space_constraint(value, pltpu.VMEM) for value in values]


def run_layer(rows, tables, own, layers, *, tick_idx, tok_dev, carried=None, ends=True):
    blocks = len(rows)
    width = own.shape[-1]
    per = 2 * tok_dev
    values = [*rows, *tables, own]
    if carried is not None:
        values.append(carried)
    for slot, spare in layers:
        values += resident([*slot, *spare])
    slot, spare = layers[0]
    hidden = (slot[2].shape[0] if slot else 0) + (spare[-1].shape[-2] if spare else 0)
    whole = jax.ShapeDtypeStruct((per * blocks, width), jnp.float32)
    parts = [jax.ShapeDtypeStruct((per, width), jnp.float32)]
    parts += [jax.ShapeDtypeStruct((per, width), jnp.bfloat16)] * (blocks - 1)
    return pl.pallas_call(
        functools.partial(
            layer_kernel, tick_idx=tick_idx, blocks=blocks, tok_dev=tok_dev, width=width, ends=ends,
            layer_counts=[(len(slot), len(spare)) for slot, spare in layers], carried=carried is not None,
        ),
        out_shape=parts if ends else whole,
        in_specs=[WHOLE] * len(values),
        out_specs=[WHOLE] * blocks if ends else WHOLE,
        compiler_params=pltpu.CompilerParams(vmem_limit_bytes=12 * 1024 * 1024),
        cost_estimate=pl.CostEstimate(
            flops=6 * per * blocks * hidden * width, bytes_accessed=6 * hidden * width,
            transcendentals=per * blocks * hidden,
        ),
        name="layer",
    )(*values)


def sum_kernel(*refs):
    refs[-1][...] = added([ref[...] for ref in refs[:-1]]).astype(jnp.bfloat16)


def summed(values):
    shape = jax.ShapeDtypeStruct(values[0].shape, jnp.bfloat16)
    return small(sum_kernel, shape, *values)


def arrive_kernel(along_ref, across_ref, gain_ref, own_ref, normed_ref, *, tick_idx):
    across = across_ref[...].astype(jnp.float32)
    half = across.shape[0] // 2
    total = along_ref[...].astype(jnp.float32) + jnp.concatenate([across[half:], across[:half]], axis=0)
    total = total.astype(jnp.bfloat16)
    own_ref[...] = total[:half]
    normed_ref[...] = normed_rows(total.astype(jnp.float32), gain_ref, tick_idx)


def arriving(along, across, gain, tick_idx):
    rows, width = along.shape
    shapes = [jax.ShapeDtypeStruct((count, width), jnp.bfloat16) for count in (rows // 2, rows)]
    return small(functools.partial(arrive_kernel, tick_idx=tick_idx), shapes, along, across, gain)


def fill_kernel(*refs, group):
    count = len(refs) // 2
    ins, outs, sems = refs[:count], refs[count:2 * count], refs[2 * count]
    copies = [
        pltpu.make_async_copy(one if group is None else one.at[group], out, sems.at[i])
        for i, (one, out) in enumerate(zip(ins, outs))
    ]
    for copy in copies:
        copy.start()
    for copy in copies:
        copy.wait()


def filled(values, group=None):
    shapes = [value.shape if group is None else value.shape[1:] for value in values]
    return pl.pallas_call(
        functools.partial(fill_kernel, group=group),
        out_shape=[pltpu.VMEM(shape, value.dtype) for shape, value in zip(shapes, values)],
        in_specs=[pl.BlockSpec(memory_space=pltpu.HBM)] * len(values),
        out_specs=[WHOLE] * len(values),
        scratch_shapes=[pltpu.SemaphoreType.DMA((len(values),))],
        compiler_params=pltpu.CompilerParams(vmem_limit_bytes=1024 * 1024),
        name="fill",
    )(*[pltpu.with_memory_space_constraint(value, pltpu.HBM) for value in values])


def load_kernel(*refs, turned, group):
    count = len(turned)
    ins, outs, (held, sems, straight) = refs[:count], refs[count:2 * count], refs[2 * count:]
    depth, block = held.shape[:2]
    work = [
        (ins[i], outs[i], low) for i in range(count) if turned[i] for low in range(0, ins[i].shape[1], block)
    ]

    def copy_of(at):
        source, _, low = work[at]
        return pltpu.make_async_copy(source.at[group, pl.ds(low, block), :], held.at[at % depth], sems.at[at % depth])

    for at in range(min(depth - 1, len(work))):
        copy_of(at).start()
    direct = [
        pltpu.make_async_copy(ins[i].at[group], outs[i], straight.at[i]) for i in range(count) if not turned[i]
    ]
    for copy in direct:
        copy.start()
    for at, (_, out, low) in enumerate(work):
        if at + depth - 1 < len(work):
            copy_of(at + depth - 1).start()
        copy_of(at).wait()
        out[:, low:low + block] = held[at % depth].T
    for copy in direct:
        copy.wait()


def loaded(values, turned, group):
    hidden, width = values[0].shape[1:]
    block = LANES if hidden % LANES == 0 else hidden
    return pl.pallas_call(
        functools.partial(load_kernel, turned=turned, group=group),
        out_shape=[
            pltpu.VMEM((width, hidden) if flip else (hidden, width), value.dtype)
            for value, flip in zip(values, turned)
        ],
        in_specs=[pl.BlockSpec(memory_space=pltpu.HBM)] * len(values),
        out_specs=[WHOLE] * len(values),
        scratch_shapes=[
            pltpu.VMEM((4, block, width), values[0].dtype),
            pltpu.SemaphoreType.DMA((4,)),
            pltpu.SemaphoreType.DMA((len(values),)),
        ],
        compiler_params=pltpu.CompilerParams(vmem_limit_bytes=6 * 1024 * 1024),
        name="load",
    )(*[pltpu.with_memory_space_constraint(value, pltpu.HBM) for value in values])


def stack_kernel(*refs, group):
    ins, out, sems = refs[:-2], refs[-2], refs[-1]
    copies = [pltpu.make_async_copy(one.at[group], out.at[i], sems.at[i]) for i, one in enumerate(ins)]
    for copy in copies:
        copy.start()
    for copy in copies:
        copy.wait()


def stacked(values, group):
    shape = (len(values),) + values[0].shape[1:]
    return pl.pallas_call(
        functools.partial(stack_kernel, group=group),
        out_shape=pltpu.VMEM(shape, values[0].dtype),
        in_specs=[pl.BlockSpec(memory_space=pltpu.HBM)] * len(values),
        out_specs=WHOLE,
        scratch_shapes=[pltpu.SemaphoreType.DMA((len(values),))],
        compiler_params=pltpu.CompilerParams(vmem_limit_bytes=6 * 1024 * 1024),
        name="stack",
    )(*[pltpu.with_memory_space_constraint(value, pltpu.HBM) for value in values])


def both_first(outer):
    return [outer - 1, *range(1, outer - 1)]


def added(values):
    total = values[0].astype(jnp.float32)
    for value in values[1:]:
        total = total + value.astype(jnp.float32)
    return total


def on_device(
    state, routes, gates, norm_gain, w_gate, w_up, w_down, spare_gate, spare_up, spare_down
):
    segments = lax.axis_size("segment")
    segments, members = lax.axis_size("segment"), lax.axis_size("expert")
    outer = members // 2
    assert outer & (outer - 1) == 0
    tok_dev = state.shape[1]

    def spread(value):
        got = {j: moved(value, j, 0) for j in both_first(outer)}
        return [value] + [got[j] for j in range(1, outer)]

    weights = [w_gate[:, 0], w_up[:, 0], w_down[:, 0]]
    spare_all = [spare_gate[:, 0], spare_up[:, 0], spare_down[:, 0]]

    def fetched(values):
        return [moved(value, 0, -1) for value in values]

    head = filled(spare_all[:1], 0)
    head, rest, state, routes, gates = lax.optimization_barrier((head, spare_all[1:], state, routes, gates))
    spares = [fetched(head + filled(rest, 0))]
    shape = (tok_dev, state.shape[2] + LANES)
    own = small(
        prepare_kernel, jax.ShapeDtypeStruct(shape, state.dtype), state[0],
        jnp.transpose(routes[:, 0], (0, 2, 1)), jnp.transpose(gates[:, 0], (0, 2, 1)), norm_gain,
    )
    other = moved(own, outer, 0)
    pair = small(join_kernel, jax.ShapeDtypeStruct((2 * tok_dev, shape[1]), state.dtype), own, other)
    arrived = spread(pair)
    users = [later_users(tick_idx, segments) for tick_idx in range(TICKS)]
    opening = min([tick_idx for tick_idx in range(TICKS) if users[tick_idx]], default=TICKS)
    slots = [loaded(weights, (True, True, False), 0)]
    if users[0]:
        slots.append(loaded(weights, (True, True, False), 1))
    late = stacked(lax.optimization_barrier((*spare_all, arrived[both_first(outer)[-1]]))[:3], 1)
    near = [swapped(late, users[opening])] if opening < TICKS else []
    own = state[0]
    before = run_layer(arrived, arrived, own, [(slot, []) for slot in slots], tick_idx=0, tok_dev=tok_dev, ends=False)

    rows = arrived
    for tick_idx in range(TICKS):
        layers = [(slots[0], spares[0])]
        if users[tick_idx]:
            layers.append((slots[1], near if users[tick_idx] <= users[opening] else far))
        if tick_idx == 0:
            layers = [([], spare) for _, spare in layers]
        parts = run_layer(
            rows, arrived, own, layers, tick_idx=tick_idx, tok_dev=tok_dev,
            carried=before if tick_idx == 0 else None,
        )
        got = [moved(parts[j], j, 0) for j in both_first(outer)]
        if tick_idx == 0 and not users[0]:
            tied = lax.optimization_barrier((*weights, parts[0]))[:3]
            gate = loaded(tied[:1], (True,), 1)
        if tick_idx + 1 == TICKS:
            total = added([parts[0]] + got)
            other = moved(total[tok_dev:].astype(jnp.bfloat16), outer, 0)
            return added([total[:tok_dev], other]).astype(jnp.bfloat16)[None]
        total = summed([parts[0]] + got)
        across = moved(total, outer, 1)
        along = moved(total, 0, 1)
        if tick_idx == 0:
            far = [moved(lax.optimization_barrier((late, total))[0], 0, -1)]
            if not users[0]:
                tied = lax.optimization_barrier((*weights, total))[:3]
                slots.append(gate + loaded(tied[1:], (True, False), 1))
        own, normed = arriving(along, across, norm_gain, tick_idx + 1)
        rows = spread(normed)


def solution(mesh):
    return jax.shard_map(
        on_device,
        mesh=mesh,
        in_specs=(
            P("segment", "expert", None),
            P(None, "segment", "expert", None),
            P(None, "segment", "expert", None),
            P(None, "segment", None),
            P(None, "segment", "expert", None),
            P(None, "segment", "expert", None),
            P(None, "segment", "expert", None),
            P(None, "segment", "expert", None),
            P(None, "segment", "expert", None),
            P(None, "segment", "expert", None),
        ),
        out_specs=P("segment", "expert", None),
        check_vma=False,
    )
```

```python
import functools

import jax
import jax.numpy as jnp
from jax import lax
from jax.experimental import pallas as pl
from jax.experimental.pallas import tpu as pltpu
from jax.sharding import PartitionSpec as P

EXPERTS = 4
TICKS = 4
CAP = 4
LANES = 128
BOTH = ("segment", "expert")


EPSILON = 1e-06


def moved(value, flip, steps):
    segments, members = lax.axis_size("segment"), lax.axis_size("expert")
    pairs = [
        (section * members + member, (section + steps) % segments * members + (member ^ flip))
        for section in range(segments)
        for member in range(members)
    ]
    return lax.ppermute(value, BOTH, pairs)


def group_of(section, tick_idx, segments):
    start_segment = (section - tick_idx) % segments
    first_group = jnp.where((start_segment % 2 == 1) & (start_segment + TICKS <= segments), 1, 0)
    return (first_group + jnp.where(start_segment + tick_idx >= segments, 1, 0)).astype(jnp.int32)


def later_users(tick_idx, segments):
    found = set()
    for section in range(segments):
        start = (section - tick_idx) % segments
        first = 1 if start % 2 == 1 and start + TICKS <= segments else 0
        if first + (1 if start + tick_idx >= segments else 0) == 1:
            found.add(section)
    return found


def swapped(value, users):
    segments, members = lax.axis_size("segment"), lax.axis_size("expert")
    partner = {section: section for section in range(segments)}
    for section in users:
        behind = (section + 1) % segments
        assert behind not in users
        partner[section], partner[behind] = behind, section
    pairs = [
        (section * members + member, partner[section] * members + member)
        for section in range(segments)
        for member in range(members)
    ]
    return lax.ppermute(value, BOTH, pairs)


WHOLE = pl.BlockSpec(memory_space=pltpu.VMEM)


def small(kernel, out_shape, *values):
    return pl.pallas_call(
        kernel,
        out_shape=out_shape,
        in_specs=[WHOLE] * len(values),
        out_specs=[WHOLE] * len(out_shape) if isinstance(out_shape, list) else WHOLE,
        compiler_params=pltpu.CompilerParams(vmem_limit_bytes=2 * 1024 * 1024),
    )(*values)


def normed_rows(values, gain_ref, tick_idx):
    group = group_of(lax.axis_index("segment"), tick_idx, lax.axis_size("segment"))
    row_scale = lax.rsqrt(jnp.mean(values * values, axis=-1, keepdims=True) + EPSILON)
    return (values * row_scale * gain_ref[group]).astype(jnp.bfloat16)


def prepare_kernel(state_ref, routes_ref, gates_ref, gain_ref, out_ref):
    rows, width = state_ref.shape
    lane = lax.broadcasted_iota(jnp.int32, (rows, LANES), 1)
    columns = EXPERTS + 1
    routed = jnp.zeros((rows, LANES), jnp.float32)
    member = jnp.zeros((rows, LANES), jnp.float32)
    square = (rows, rows)
    diagonal = lax.broadcasted_iota(jnp.int32, square, 0) == lax.broadcasted_iota(jnp.int32, square, 1)

    def upright(line):
        return jnp.sum(jnp.where(diagonal, line, jnp.zeros_like(line)), axis=1, keepdims=True)

    for tick_idx in range(TICKS):
        for choice in range(routes_ref.shape[1]):
            named = lane == upright(routes_ref[tick_idx, choice:choice + 1, :]) + tick_idx * columns
            routed = routed + jnp.where(named, upright(gates_ref[tick_idx, choice:choice + 1, :]), 0.0)
            member = member + jnp.where(named, 1.0, 0.0)
    row = lax.broadcasted_iota(jnp.int32, (rows, LANES), 0)
    position = jnp.zeros((rows, LANES), jnp.float32)
    for earlier in range(rows - 1):
        position = position + jnp.where(row > earlier, member[earlier:earlier + 1, :], 0.0)
    inside = position < CAP
    table = jnp.where(inside, routed, 0.0)
    over = jnp.where(inside, 0.0, routed)
    for tick_idx in range(TICKS):
        low = tick_idx * columns
        spill = jnp.sum(jnp.where((lane >= low) & (lane < low + EXPERTS), over, 0.0), axis=1, keepdims=True)
        table = jnp.where(lane == low + EXPERTS, spill, table)
    high = table.astype(jnp.bfloat16).astype(jnp.float32)
    both = high + pltpu.roll(table - high, TICKS * columns, 1)
    out_ref[:, :width] = normed_rows(state_ref[...].astype(jnp.float32), gain_ref, 0)
    out_ref[:, width:] = both.astype(jnp.bfloat16)


def join_kernel(first_ref, second_ref, out_ref):
    out_ref[...] = jnp.concatenate([first_ref[...], second_ref[...]], axis=0)


def served(normed, gate, up, down, turned):
    contract = (((1,), (0 if turned else 1,)), ((), ()))
    gate_pre = lax.dot_general(normed, gate, contract, preferred_element_type=jnp.float32)
    up_pre = lax.dot_general(normed, up, contract, preferred_element_type=jnp.float32)
    hidden = (gate_pre / (1.0 + jnp.exp(-gate_pre)) * up_pre).astype(jnp.bfloat16)
    return jnp.dot(hidden, down, preferred_element_type=jnp.float32)


def either(second, bodies):
    if len(bodies) == 1:
        bodies[0]()
    elif bodies:
        pl.when(jnp.logical_not(second))(bodies[0])
        pl.when(second)(bodies[1])


def layer_kernel(*refs, tick_idx, blocks, layer_counts, tok_dev, width, carried, ends):
    row_refs, table_refs, refs = refs[:blocks], refs[blocks:2 * blocks], refs[2 * blocks:]
    own_ref, refs = refs[0], refs[1:]
    if carried:
        carried_ref, refs = refs[0], refs[1:]
    choices = []
    for slot_count, spare_count in layer_counts:
        slot, spare, refs = refs[:slot_count], refs[slot_count:slot_count + spare_count], refs[slot_count + spare_count:]
        choices.append((slot, [spare[0].at[i] for i in range(3)] if spare_count == 1 else spare))
    segments, members = lax.axis_size("segment"), lax.axis_size("expert")
    group = group_of(lax.axis_index("segment"), tick_idx, segments)
    expert = lax.axis_index("expert") // (members // EXPERTS)
    normed = jnp.concatenate([ref[:, :width] for ref in row_refs], axis=0)
    table = jnp.concatenate([ref[:, width:] for ref in table_refs], axis=0).astype(jnp.float32)
    lane = lax.broadcasted_iota(jnp.int32, table.shape, 1)
    columns = TICKS * (EXPERTS + 1)

    def column(at):
        return jnp.sum(jnp.where((lane == at) | (lane == at + columns), table, 0.0), axis=1, keepdims=True)

    share = column(tick_idx * (EXPERTS + 1) + expert)
    spill = column(tick_idx * (EXPERTS + 1) + EXPERTS)
    per = 2 * tok_dev

    def run(slot, spare):
        total = carried_ref[...] if carried else share * served(normed, *[ref[...] for ref in slot], True)
        if spare:
            total = total + spill * served(normed, *[ref[...] for ref in spare], False)
        if not ends:
            refs[0][...] = total
            return
        own = jnp.concatenate([own_ref[...].astype(jnp.float32), jnp.zeros((tok_dev, width), jnp.float32)], axis=0)
        refs[0][...] = total[0:per] + own
        for i in range(1, blocks):
            refs[i][...] = total[i * per:(i + 1) * per].astype(jnp.bfloat16)

    either(group == 1, [functools.partial(run, *choice) for choice in choices])


def resident(values):
    return [pltpu.with_memory_space_constraint(value, pltpu.VMEM) for value in values]


def run_layer(rows, tables, own, layers, *, tick_idx, tok_dev, carried=None, ends=True):
    blocks = len(rows)
    width = own.shape[-1]
    per = 2 * tok_dev
    values = [*rows, *tables, own]
    if carried is not None:
        values.append(carried)
    for slot, spare in layers:
        values += resident([*slot, *spare])
    slot, spare = layers[0]
    hidden = (slot[2].shape[0] if slot else 0) + (spare[-1].shape[-2] if spare else 0)
    whole = jax.ShapeDtypeStruct((per * blocks, width), jnp.float32)
    parts = [jax.ShapeDtypeStruct((per, width), jnp.float32)]
    parts += [jax.ShapeDtypeStruct((per, width), jnp.bfloat16)] * (blocks - 1)
    return pl.pallas_call(
        functools.partial(
            layer_kernel, tick_idx=tick_idx, blocks=blocks, tok_dev=tok_dev, width=width, ends=ends,
            layer_counts=[(len(slot), len(spare)) for slot, spare in layers], carried=carried is not None,
        ),
        out_shape=parts if ends else whole,
        in_specs=[WHOLE] * len(values),
        out_specs=[WHOLE] * blocks if ends else WHOLE,
        compiler_params=pltpu.CompilerParams(vmem_limit_bytes=12 * 1024 * 1024),
        cost_estimate=pl.CostEstimate(
            flops=6 * per * blocks * hidden * width, bytes_accessed=6 * hidden * width,
            transcendentals=per * blocks * hidden,
        ),
        name="layer",
    )(*values)


def sum_kernel(*refs):
    refs[-1][...] = added([ref[...] for ref in refs[:-1]]).astype(jnp.bfloat16)


def summed(values):
    shape = jax.ShapeDtypeStruct(values[0].shape, jnp.bfloat16)
    return small(sum_kernel, shape, *values)


def arrive_kernel(along_ref, across_ref, gain_ref, own_ref, normed_ref, *, tick_idx):
    across = across_ref[...].astype(jnp.float32)
    half = across.shape[0] // 2
    total = along_ref[...].astype(jnp.float32) + jnp.concatenate([across[half:], across[:half]], axis=0)
    total = total.astype(jnp.bfloat16)
    own_ref[...] = total[:half]
    normed_ref[...] = normed_rows(total.astype(jnp.float32), gain_ref, tick_idx)


def arriving(along, across, gain, tick_idx):
    rows, width = along.shape
    shapes = [jax.ShapeDtypeStruct((count, width), jnp.bfloat16) for count in (rows // 2, rows)]
    return small(functools.partial(arrive_kernel, tick_idx=tick_idx), shapes, along, across, gain)


def fill_kernel(*refs, group):
    count = len(refs) // 2
    ins, outs, sems = refs[:count], refs[count:2 * count], refs[2 * count]
    pieces = sems.shape[1]
    rows = outs[0].shape[0] // pieces
    copies = [
        pltpu.make_async_copy(one.at[group, pl.ds(at * rows, rows)], out.at[pl.ds(at * rows, rows)], sems.at[i, at])
        for i, (one, out) in enumerate(zip(ins, outs))
        for at in range(pieces)
    ]
    for copy in copies:
        copy.start()
    for copy in copies:
        copy.wait()


def filled(values, group):
    shapes = [value.shape[1:] for value in values]
    pieces = 4 if shapes[0][0] % 32 == 0 else 1
    return pl.pallas_call(
        functools.partial(fill_kernel, group=group),
        out_shape=[pltpu.VMEM(shape, value.dtype) for shape, value in zip(shapes, values)],
        in_specs=[pl.BlockSpec(memory_space=pltpu.HBM)] * len(values),
        out_specs=[WHOLE] * len(values),
        scratch_shapes=[pltpu.SemaphoreType.DMA((len(values), pieces))],
        compiler_params=pltpu.CompilerParams(vmem_limit_bytes=1024 * 1024),
        name="fill",
    )(*[pltpu.with_memory_space_constraint(value, pltpu.HBM) for value in values])


def load_kernel(*refs, turned, group):
    count = len(turned)
    ins, outs, (held, sems, straight) = refs[:count], refs[count:2 * count], refs[2 * count:]
    depth, block = held.shape[:2]
    work = [
        (ins[i], outs[i], low) for i in range(count) if turned[i] for low in range(0, ins[i].shape[1], block)
    ]

    def copy_of(at):
        source, _, low = work[at]
        return pltpu.make_async_copy(source.at[group, pl.ds(low, block), :], held.at[at % depth], sems.at[at % depth])

    for at in range(min(depth - 1, len(work))):
        copy_of(at).start()
    direct = [
        pltpu.make_async_copy(ins[i].at[group], outs[i], straight.at[i]) for i in range(count) if not turned[i]
    ]
    for copy in direct:
        copy.start()
    for at, (_, out, low) in enumerate(work):
        if at + depth - 1 < len(work):
            copy_of(at + depth - 1).start()
        copy_of(at).wait()
        out[:, low:low + block] = held[at % depth].T
    for copy in direct:
        copy.wait()


def loaded(values, turned, group):
    hidden, width = values[0].shape[1:]
    block = LANES if hidden % LANES == 0 else hidden
    return pl.pallas_call(
        functools.partial(load_kernel, turned=turned, group=group),
        out_shape=[
            pltpu.VMEM((width, hidden) if flip else (hidden, width), value.dtype)
            for value, flip in zip(values, turned)
        ],
        in_specs=[pl.BlockSpec(memory_space=pltpu.HBM)] * len(values),
        out_specs=[WHOLE] * len(values),
        scratch_shapes=[
            pltpu.VMEM((4, block, width), values[0].dtype),
            pltpu.SemaphoreType.DMA((4,)),
            pltpu.SemaphoreType.DMA((len(values),)),
        ],
        compiler_params=pltpu.CompilerParams(vmem_limit_bytes=6 * 1024 * 1024),
        name="load",
    )(*[pltpu.with_memory_space_constraint(value, pltpu.HBM) for value in values])


def both_first(outer):
    return [outer - 1, *range(1, outer - 1)]


def added(values):
    total = values[0].astype(jnp.float32)
    for value in values[1:]:
        total = total + value.astype(jnp.float32)
    return total


def on_device(
    state, routes, gates, norm_gain, w_gate, w_up, w_down, spare_gate, spare_up, spare_down
):
    segments = lax.axis_size("segment")
    segments, members = lax.axis_size("segment"), lax.axis_size("expert")
    outer = members // 2
    assert outer & (outer - 1) == 0
    tok_dev = state.shape[1]

    def spread(value):
        got = {j: moved(value, j, 0) for j in both_first(outer)}
        return [value] + [got[j] for j in range(1, outer)]

    weights = [w_gate[:, 0], w_up[:, 0], w_down[:, 0]]
    spare_all = [spare_gate[:, 0], spare_up[:, 0], spare_down[:, 0]]

    def fetched(values):
        return [moved(value, 0, -1) for value in values]

    head = filled(spare_all[:1], 0)
    head, rest, state, routes, gates = lax.optimization_barrier((head, spare_all[1:], state, routes, gates))
    spares = [fetched(head + filled(rest, 0))]
    shape = (tok_dev, state.shape[2] + LANES)
    own = small(
        prepare_kernel, jax.ShapeDtypeStruct(shape, state.dtype), state[0],
        jnp.transpose(routes[:, 0], (0, 2, 1)), jnp.transpose(gates[:, 0], (0, 2, 1)), norm_gain,
    )
    other = moved(own, outer, 0)
    pair = small(join_kernel, jax.ShapeDtypeStruct((2 * tok_dev, shape[1]), state.dtype), own, other)
    arrived = spread(pair)
    users = [later_users(tick_idx, segments) for tick_idx in range(TICKS)]
    opening = min([tick_idx for tick_idx in range(TICKS) if users[tick_idx]], default=TICKS)
    slots = [loaded(weights, (True, True, False), 0)]
    if users[0]:
        slots.append(loaded(weights, (True, True, False), 1))
    late = filled(lax.optimization_barrier((*spare_all, arrived[both_first(outer)[-1]]))[:3], 1)
    near = [swapped(one, users[opening]) for one in late] if opening < TICKS else []
    own = state[0]
    before = run_layer(arrived, arrived, own, [(slot, []) for slot in slots], tick_idx=0, tok_dev=tok_dev, ends=False)

    rows = arrived
    for tick_idx in range(TICKS):
        layers = [(slots[0], spares[0])]
        if users[tick_idx]:
            layers.append((slots[1], near if users[tick_idx] <= users[opening] else far))
        if tick_idx == 0:
            layers = [([], spare) for _, spare in layers]
        parts = run_layer(
            rows, arrived, own, layers, tick_idx=tick_idx, tok_dev=tok_dev,
            carried=before if tick_idx == 0 else None,
        )
        got = [moved(parts[j], j, 0) for j in both_first(outer)]
        if tick_idx == 0:
            far = [moved(lax.optimization_barrier((late[0], parts[0]))[0], 0, -1)]
        if tick_idx == 0 and not users[0]:
            tied = lax.optimization_barrier((*weights, parts[0]))[:3]
            gate = loaded(tied[:1], (True,), 1)
        if tick_idx + 1 == TICKS:
            total = added([parts[0]] + got)
            other = moved(total[tok_dev:].astype(jnp.bfloat16), outer, 0)
            return added([total[:tok_dev], other]).astype(jnp.bfloat16)[None]
        total = summed([parts[0]] + got)
        across = moved(total, outer, 1)
        along = moved(total, 0, 1)
        if tick_idx == 0:
            if not users[0]:
                tied = lax.optimization_barrier((*weights, total))[:3]
                slots.append(gate + loaded(tied[1:], (True, False), 1))
        own, normed = arriving(along, across, norm_gain, tick_idx + 1)
        if tick_idx == 0:
            later = lax.optimization_barrier((*late[1:], normed))[:2]
            far += [moved(one, 0, -1) for one in later]
        rows = spread(normed)


def solution(mesh):
    return jax.shard_map(
        on_device,
        mesh=mesh,
        in_specs=(
            P("segment", "expert", None),
            P(None, "segment", "expert", None),
            P(None, "segment", "expert", None),
            P(None, "segment", None),
            P(None, "segment", "expert", None),
            P(None, "segment", "expert", None),
            P(None, "segment", "expert", None),
            P(None, "segment", "expert", None),
            P(None, "segment", "expert", None),
            P(None, "segment", "expert", None),
        ),
        out_specs=P("segment", "expert", None),
        check_vma=False,
    )
```

```python
import functools

import jax
import jax.numpy as jnp
from jax import lax
from jax.experimental import pallas as pl
from jax.experimental.pallas import tpu as pltpu
from jax.sharding import PartitionSpec as P

EXPERTS = 4
TICKS = 4
CAP = 4
LANES = 128
BOTH = ("segment", "expert")


EPSILON = 1e-06


def moved(value, flip, steps):
    segments, members = lax.axis_size("segment"), lax.axis_size("expert")
    pairs = [
        (section * members + member, (section + steps) % segments * members + (member ^ flip))
        for section in range(segments)
        for member in range(members)
    ]
    return lax.ppermute(value, BOTH, pairs)


def group_of(section, tick_idx, segments):
    start_segment = (section - tick_idx) % segments
    first_group = jnp.where((start_segment % 2 == 1) & (start_segment + TICKS <= segments), 1, 0)
    return (first_group + jnp.where(start_segment + tick_idx >= segments, 1, 0)).astype(jnp.int32)


def later_users(tick_idx, segments):
    found = set()
    for section in range(segments):
        start = (section - tick_idx) % segments
        first = 1 if start % 2 == 1 and start + TICKS <= segments else 0
        if first + (1 if start + tick_idx >= segments else 0) == 1:
            found.add(section)
    return found


def swapped(value, users):
    segments, members = lax.axis_size("segment"), lax.axis_size("expert")
    partner = {section: section for section in range(segments)}
    for section in users:
        behind = (section + 1) % segments
        assert behind not in users
        partner[section], partner[behind] = behind, section
    pairs = [
        (section * members + member, partner[section] * members + member)
        for section in range(segments)
        for member in range(members)
    ]
    return lax.ppermute(value, BOTH, pairs)


WHOLE = pl.BlockSpec(memory_space=pltpu.VMEM)


def small(kernel, out_shape, *values):
    return pl.pallas_call(
        kernel,
        out_shape=out_shape,
        in_specs=[WHOLE] * len(values),
        out_specs=[WHOLE] * len(out_shape) if isinstance(out_shape, list) else WHOLE,
        compiler_params=pltpu.CompilerParams(vmem_limit_bytes=2 * 1024 * 1024),
    )(*values)


def normed_rows(values, gain_ref, tick_idx):
    group = group_of(lax.axis_index("segment"), tick_idx, lax.axis_size("segment"))
    row_scale = lax.rsqrt(jnp.mean(values * values, axis=-1, keepdims=True) + EPSILON)
    return (values * row_scale * gain_ref[group]).astype(jnp.bfloat16)


def prepare_kernel(state_ref, routes_ref, gates_ref, gain_ref, out_ref):
    rows, width = state_ref.shape
    lane = lax.broadcasted_iota(jnp.int32, (rows, LANES), 1)
    columns = EXPERTS + 1
    routed = jnp.zeros((rows, LANES), jnp.float32)
    member = jnp.zeros((rows, LANES), jnp.float32)
    square = (rows, rows)
    diagonal = lax.broadcasted_iota(jnp.int32, square, 0) == lax.broadcasted_iota(jnp.int32, square, 1)

    def upright(line):
        return jnp.sum(jnp.where(diagonal, line, jnp.zeros_like(line)), axis=1, keepdims=True)

    for tick_idx in range(TICKS):
        for choice in range(routes_ref.shape[1]):
            named = lane == upright(routes_ref[tick_idx, choice:choice + 1, :]) + tick_idx * columns
            routed = routed + jnp.where(named, upright(gates_ref[tick_idx, choice:choice + 1, :]), 0.0)
            member = member + jnp.where(named, 1.0, 0.0)
    row = lax.broadcasted_iota(jnp.int32, (rows, LANES), 0)
    position = jnp.zeros((rows, LANES), jnp.float32)
    for earlier in range(rows - 1):
        position = position + jnp.where(row > earlier, member[earlier:earlier + 1, :], 0.0)
    inside = position < CAP
    table = jnp.where(inside, routed, 0.0)
    over = jnp.where(inside, 0.0, routed)
    for tick_idx in range(TICKS):
        low = tick_idx * columns
        spill = jnp.sum(jnp.where((lane >= low) & (lane < low + EXPERTS), over, 0.0), axis=1, keepdims=True)
        table = jnp.where(lane == low + EXPERTS, spill, table)
    high = table.astype(jnp.bfloat16).astype(jnp.float32)
    both = high + pltpu.roll(table - high, TICKS * columns, 1)
    out_ref[:, :width] = normed_rows(state_ref[...].astype(jnp.float32), gain_ref, 0)
    out_ref[:, width:] = both.astype(jnp.bfloat16)


def join_kernel(first_ref, second_ref, out_ref):
    out_ref[...] = jnp.concatenate([first_ref[...], second_ref[...]], axis=0)


def served(normed, gate, up, down, turned):
    contract = (((1,), (0 if turned else 1,)), ((), ()))
    gate_pre = lax.dot_general(normed, gate, contract, preferred_element_type=jnp.float32)
    up_pre = lax.dot_general(normed, up, contract, preferred_element_type=jnp.float32)
    hidden = (gate_pre / (1.0 + jnp.exp(-gate_pre)) * up_pre).astype(jnp.bfloat16)
    return jnp.dot(hidden, down, preferred_element_type=jnp.float32)


def either(second, bodies):
    if len(bodies) == 1:
        bodies[0]()
    elif bodies:
        pl.when(jnp.logical_not(second))(bodies[0])
        pl.when(second)(bodies[1])


def layer_kernel(*refs, tick_idx, blocks, layer_counts, tok_dev, width, carried, ends):
    row_refs, table_refs, refs = refs[:blocks], refs[blocks:2 * blocks], refs[2 * blocks:]
    own_ref, refs = refs[0], refs[1:]
    if carried:
        carried_ref, refs = refs[0], refs[1:]
    choices = []
    for slot_count, spare_count in layer_counts:
        slot, spare, refs = refs[:slot_count], refs[slot_count:slot_count + spare_count], refs[slot_count + spare_count:]
        whole = []
        for ref in spare:
            whole += [ref.at[i] for i in range(ref.shape[0])] if len(ref.shape) == 3 else [ref]
        choices.append((slot, whole))
    segments, members = lax.axis_size("segment"), lax.axis_size("expert")
    group = group_of(lax.axis_index("segment"), tick_idx, segments)
    expert = lax.axis_index("expert") // (members // EXPERTS)
    normed = jnp.concatenate([ref[:, :width] for ref in row_refs], axis=0)
    table = jnp.concatenate([ref[:, width:] for ref in table_refs], axis=0).astype(jnp.float32)
    lane = lax.broadcasted_iota(jnp.int32, table.shape, 1)
    columns = TICKS * (EXPERTS + 1)

    def column(at):
        return jnp.sum(jnp.where((lane == at) | (lane == at + columns), table, 0.0), axis=1, keepdims=True)

    share = column(tick_idx * (EXPERTS + 1) + expert)
    spill = column(tick_idx * (EXPERTS + 1) + EXPERTS)
    per = 2 * tok_dev

    def run(slot, spare):
        total = carried_ref[...] if carried else share * served(normed, *[ref[...] for ref in slot], True)
        if spare:
            total = total + spill * served(normed, *[ref[...] for ref in spare], False)
        if not ends:
            refs[0][...] = total
            return
        own = jnp.concatenate([own_ref[...].astype(jnp.float32), jnp.zeros((tok_dev, width), jnp.float32)], axis=0)
        refs[0][...] = total[0:per] + own
        for i in range(1, blocks):
            refs[i][...] = total[i * per:(i + 1) * per].astype(jnp.bfloat16)

    either(group == 1, [functools.partial(run, *choice) for choice in choices])


def resident(values):
    return [pltpu.with_memory_space_constraint(value, pltpu.VMEM) for value in values]


def run_layer(rows, tables, own, layers, *, tick_idx, tok_dev, carried=None, ends=True):
    blocks = len(rows)
    width = own.shape[-1]
    per = 2 * tok_dev
    values = [*rows, *tables, own]
    if carried is not None:
        values.append(carried)
    for slot, spare in layers:
        values += resident([*slot, *spare])
    slot, spare = layers[0]
    hidden = (slot[2].shape[0] if slot else 0) + (spare[-1].shape[-2] if spare else 0)
    whole = jax.ShapeDtypeStruct((per * blocks, width), jnp.float32)
    parts = [jax.ShapeDtypeStruct((per, width), jnp.float32)]
    parts += [jax.ShapeDtypeStruct((per, width), jnp.bfloat16)] * (blocks - 1)
    return pl.pallas_call(
        functools.partial(
            layer_kernel, tick_idx=tick_idx, blocks=blocks, tok_dev=tok_dev, width=width, ends=ends,
            layer_counts=[(len(slot), len(spare)) for slot, spare in layers], carried=carried is not None,
        ),
        out_shape=parts if ends else whole,
        in_specs=[WHOLE] * len(values),
        out_specs=[WHOLE] * blocks if ends else WHOLE,
        compiler_params=pltpu.CompilerParams(vmem_limit_bytes=12 * 1024 * 1024),
        cost_estimate=pl.CostEstimate(
            flops=6 * per * blocks * hidden * width, bytes_accessed=6 * hidden * width,
            transcendentals=per * blocks * hidden,
        ),
        name="layer",
    )(*values)


def sum_kernel(*refs):
    refs[-1][...] = added([ref[...] for ref in refs[:-1]]).astype(jnp.bfloat16)


def summed(values):
    shape = jax.ShapeDtypeStruct(values[0].shape, jnp.bfloat16)
    return small(sum_kernel, shape, *values)


def arrive_kernel(along_ref, across_ref, gain_ref, own_ref, normed_ref, *, tick_idx):
    across = across_ref[...].astype(jnp.float32)
    half = across.shape[0] // 2
    total = along_ref[...].astype(jnp.float32) + jnp.concatenate([across[half:], across[:half]], axis=0)
    total = total.astype(jnp.bfloat16)
    own_ref[...] = total[:half]
    normed_ref[...] = normed_rows(total.astype(jnp.float32), gain_ref, tick_idx)


def arriving(along, across, gain, tick_idx):
    rows, width = along.shape
    shapes = [jax.ShapeDtypeStruct((count, width), jnp.bfloat16) for count in (rows // 2, rows)]
    return small(functools.partial(arrive_kernel, tick_idx=tick_idx), shapes, along, across, gain)


def fill_kernel(*refs, group):
    count = len(refs) // 2
    ins, outs, sems = refs[:count], refs[count:2 * count], refs[2 * count]
    copies = [
        pltpu.make_async_copy(one if group is None else one.at[group], out, sems.at[i])
        for i, (one, out) in enumerate(zip(ins, outs))
    ]
    for copy in copies:
        copy.start()
    for copy in copies:
        copy.wait()


def filled(values, group=None):
    shapes = [value.shape if group is None else value.shape[1:] for value in values]
    return pl.pallas_call(
        functools.partial(fill_kernel, group=group),
        out_shape=[pltpu.VMEM(shape, value.dtype) for shape, value in zip(shapes, values)],
        in_specs=[pl.BlockSpec(memory_space=pltpu.HBM)] * len(values),
        out_specs=[WHOLE] * len(values),
        scratch_shapes=[pltpu.SemaphoreType.DMA((len(values),))],
        compiler_params=pltpu.CompilerParams(vmem_limit_bytes=1024 * 1024),
        name="fill",
    )(*[pltpu.with_memory_space_constraint(value, pltpu.HBM) for value in values])


def load_kernel(*refs, turned, group):
    count = len(turned)
    ins, outs, (held, sems, straight) = refs[:count], refs[count:2 * count], refs[2 * count:]
    depth, block = held.shape[:2]
    work = [
        (ins[i], outs[i], low) for i in range(count) if turned[i] for low in range(0, ins[i].shape[1], block)
    ]

    def copy_of(at):
        source, _, low = work[at]
        return pltpu.make_async_copy(source.at[group, pl.ds(low, block), :], held.at[at % depth], sems.at[at % depth])

    for at in range(min(depth - 1, len(work))):
        copy_of(at).start()
    direct = [
        pltpu.make_async_copy(ins[i].at[group], outs[i], straight.at[i]) for i in range(count) if not turned[i]
    ]
    for copy in direct:
        copy.start()
    for at, (_, out, low) in enumerate(work):
        if at + depth - 1 < len(work):
            copy_of(at + depth - 1).start()
        copy_of(at).wait()
        out[:, low:low + block] = held[at % depth].T
    for copy in direct:
        copy.wait()


def loaded(values, turned, group):
    hidden, width = values[0].shape[1:]
    block = LANES if hidden % LANES == 0 else hidden
    return pl.pallas_call(
        functools.partial(load_kernel, turned=turned, group=group),
        out_shape=[
            pltpu.VMEM((width, hidden) if flip else (hidden, width), value.dtype)
            for value, flip in zip(values, turned)
        ],
        in_specs=[pl.BlockSpec(memory_space=pltpu.HBM)] * len(values),
        out_specs=[WHOLE] * len(values),
        scratch_shapes=[
            pltpu.VMEM((4, block, width), values[0].dtype),
            pltpu.SemaphoreType.DMA((4,)),
            pltpu.SemaphoreType.DMA((len(values),)),
        ],
        compiler_params=pltpu.CompilerParams(vmem_limit_bytes=6 * 1024 * 1024),
        name="load",
    )(*[pltpu.with_memory_space_constraint(value, pltpu.HBM) for value in values])


def stack_kernel(*refs, group):
    ins, out, sems = refs[:-2], refs[-2], refs[-1]
    copies = [pltpu.make_async_copy(one.at[group], out.at[i], sems.at[i]) for i, one in enumerate(ins)]
    for copy in copies:
        copy.start()
    for copy in copies:
        copy.wait()


def stacked(values, group):
    shape = (len(values),) + values[0].shape[1:]
    return pl.pallas_call(
        functools.partial(stack_kernel, group=group),
        out_shape=pltpu.VMEM(shape, values[0].dtype),
        in_specs=[pl.BlockSpec(memory_space=pltpu.HBM)] * len(values),
        out_specs=WHOLE,
        scratch_shapes=[pltpu.SemaphoreType.DMA((len(values),))],
        compiler_params=pltpu.CompilerParams(vmem_limit_bytes=6 * 1024 * 1024),
        name="stack",
    )(*[pltpu.with_memory_space_constraint(value, pltpu.HBM) for value in values])


def both_first(outer):
    return [outer - 1, *range(1, outer - 1)]


def added(values):
    total = values[0].astype(jnp.float32)
    for value in values[1:]:
        total = total + value.astype(jnp.float32)
    return total


def on_device(
    state, routes, gates, norm_gain, w_gate, w_up, w_down, spare_gate, spare_up, spare_down
):
    segments = lax.axis_size("segment")
    segments, members = lax.axis_size("segment"), lax.axis_size("expert")
    outer = members // 2
    assert outer & (outer - 1) == 0
    tok_dev = state.shape[1]

    def spread(value):
        got = {j: moved(value, j, 0) for j in both_first(outer)}
        return [value] + [got[j] for j in range(1, outer)]

    weights = [w_gate[:, 0], w_up[:, 0], w_down[:, 0]]
    spare_all = [spare_gate[:, 0], spare_up[:, 0], spare_down[:, 0]]

    def fetched(values):
        return [moved(value, 0, -1) for value in values]

    head = filled(spare_all[:1], 0)
    head, rest, state, routes, gates = lax.optimization_barrier((head, spare_all[1:], state, routes, gates))
    spares = [fetched(head + filled(rest, 0))]
    shape = (tok_dev, state.shape[2] + LANES)
    own = small(
        prepare_kernel, jax.ShapeDtypeStruct(shape, state.dtype), state[0],
        jnp.transpose(routes[:, 0], (0, 2, 1)), jnp.transpose(gates[:, 0], (0, 2, 1)), norm_gain,
    )
    other = moved(own, outer, 0)
    pair = small(join_kernel, jax.ShapeDtypeStruct((2 * tok_dev, shape[1]), state.dtype), own, other)
    arrived = spread(pair)
    users = [later_users(tick_idx, segments) for tick_idx in range(TICKS)]
    opening = min([tick_idx for tick_idx in range(TICKS) if users[tick_idx]], default=TICKS)
    slots = [loaded(weights, (True, True, False), 0)]
    if users[0]:
        slots.append(loaded(weights, (True, True, False), 1))
    late = stacked(lax.optimization_barrier((*spare_all, arrived[both_first(outer)[-1]]))[:3], 1)
    first_late = filled(lax.optimization_barrier((*spare_all, arrived[both_first(outer)[-1]]))[:1], 1)[0]
    near = [swapped(late, users[opening])] if opening < TICKS else []
    own = state[0]
    before = run_layer(arrived, arrived, own, [(slot, []) for slot in slots], tick_idx=0, tok_dev=tok_dev, ends=False)

    rows = arrived
    for tick_idx in range(TICKS):
        layers = [(slots[0], spares[0])]
        if users[tick_idx]:
            layers.append((slots[1], near if users[tick_idx] <= users[opening] else far))
        if tick_idx == 0:
            layers = [([], spare) for _, spare in layers]
        parts = run_layer(
            rows, arrived, own, layers, tick_idx=tick_idx, tok_dev=tok_dev,
            carried=before if tick_idx == 0 else None,
        )
        got = [moved(parts[j], j, 0) for j in both_first(outer)]
        if tick_idx == 0:
            far = [moved(lax.optimization_barrier((first_late, parts[0]))[0], 0, -1)]
            rest_late = stacked(lax.optimization_barrier((*spare_all[1:], parts[0]))[:2], 1)
        if tick_idx == 0 and not users[0]:
            tied = lax.optimization_barrier((*weights, parts[0]))[:3]
            gate = loaded(tied[:1], (True,), 1)
        if tick_idx + 1 == TICKS:
            total = added([parts[0]] + got)
            other = moved(total[tok_dev:].astype(jnp.bfloat16), outer, 0)
            return added([total[:tok_dev], other]).astype(jnp.bfloat16)[None]
        total = summed([parts[0]] + got)
        across = moved(total, outer, 1)
        along = moved(total, 0, 1)
        if tick_idx == 0:
            if not users[0]:
                tied = lax.optimization_barrier((*weights, parts[0]))[:3]
                slots.append(gate + loaded(tied[1:], (True, False), 1))
        own, normed = arriving(along, across, norm_gain, tick_idx + 1)
        if tick_idx == 0:
            far.append(moved(lax.optimization_barrier((rest_late, normed))[0], 0, -1))
        rows = spread(normed)


def solution(mesh):
    return jax.shard_map(
        on_device,
        mesh=mesh,
        in_specs=(
            P("segment", "expert", None),
            P(None, "segment", "expert", None),
            P(None, "segment", "expert", None),
            P(None, "segment", None),
            P(None, "segment", "expert", None),
            P(None, "segment", "expert", None),
            P(None, "segment", "expert", None),
            P(None, "segment", "expert", None),
            P(None, "segment", "expert", None),
            P(None, "segment", "expert", None),
        ),
        out_specs=P("segment", "expert", None),
        check_vma=False,
    )
```

```python
import functools

import jax
import jax.numpy as jnp
from jax import lax
from jax.experimental import pallas as pl
from jax.experimental.pallas import tpu as pltpu
from jax.sharding import PartitionSpec as P

EXPERTS = 4
TICKS = 4
CAP = 4
LANES = 128
BOTH = ("segment", "expert")


EPSILON = 1e-06


def moved(value, flip, steps):
    segments, members = lax.axis_size("segment"), lax.axis_size("expert")
    pairs = [
        (section * members + member, (section + steps) % segments * members + (member ^ flip))
        for section in range(segments)
        for member in range(members)
    ]
    return lax.ppermute(value, BOTH, pairs)


def group_of(section, tick_idx, segments):
    start_segment = (section - tick_idx) % segments
    first_group = jnp.where((start_segment % 2 == 1) & (start_segment + TICKS <= segments), 1, 0)
    return (first_group + jnp.where(start_segment + tick_idx >= segments, 1, 0)).astype(jnp.int32)


def later_users(tick_idx, segments):
    found = set()
    for section in range(segments):
        start = (section - tick_idx) % segments
        first = 1 if start % 2 == 1 and start + TICKS <= segments else 0
        if first + (1 if start + tick_idx >= segments else 0) == 1:
            found.add(section)
    return found


def swapped(value, users):
    segments, members = lax.axis_size("segment"), lax.axis_size("expert")
    partner = {section: section for section in range(segments)}
    for section in users:
        behind = (section + 1) % segments
        assert behind not in users
        partner[section], partner[behind] = behind, section
    pairs = [
        (section * members + member, partner[section] * members + member)
        for section in range(segments)
        for member in range(members)
    ]
    return lax.ppermute(value, BOTH, pairs)


WHOLE = pl.BlockSpec(memory_space=pltpu.VMEM)


def small(kernel, out_shape, *values):
    return pl.pallas_call(
        kernel,
        out_shape=out_shape,
        in_specs=[WHOLE] * len(values),
        out_specs=[WHOLE] * len(out_shape) if isinstance(out_shape, list) else WHOLE,
        compiler_params=pltpu.CompilerParams(vmem_limit_bytes=2 * 1024 * 1024),
    )(*values)


def normed_rows(values, gain_ref, tick_idx):
    group = group_of(lax.axis_index("segment"), tick_idx, lax.axis_size("segment"))
    row_scale = lax.rsqrt(jnp.mean(values * values, axis=-1, keepdims=True) + EPSILON)
    return (values * row_scale * gain_ref[group]).astype(jnp.bfloat16)


def prepare_kernel(state_ref, routes_ref, gates_ref, gain_ref, out_ref):
    rows, width = state_ref.shape
    lane = lax.broadcasted_iota(jnp.int32, (rows, LANES), 1)
    columns = EXPERTS + 1
    routed = jnp.zeros((rows, LANES), jnp.float32)
    member = jnp.zeros((rows, LANES), jnp.float32)
    square = (rows, rows)
    diagonal = lax.broadcasted_iota(jnp.int32, square, 0) == lax.broadcasted_iota(jnp.int32, square, 1)

    def upright(line):
        return jnp.sum(jnp.where(diagonal, line, jnp.zeros_like(line)), axis=1, keepdims=True)

    for tick_idx in range(TICKS):
        for choice in range(routes_ref.shape[1]):
            named = lane == upright(routes_ref[tick_idx, choice:choice + 1, :]) + tick_idx * columns
            routed = routed + jnp.where(named, upright(gates_ref[tick_idx, choice:choice + 1, :]), 0.0)
            member = member + jnp.where(named, 1.0, 0.0)
    row = lax.broadcasted_iota(jnp.int32, (rows, LANES), 0)
    position = jnp.zeros((rows, LANES), jnp.float32)
    for earlier in range(rows - 1):
        position = position + jnp.where(row > earlier, member[earlier:earlier + 1, :], 0.0)
    inside = position < CAP
    table = jnp.where(inside, routed, 0.0)
    over = jnp.where(inside, 0.0, routed)
    for tick_idx in range(TICKS):
        low = tick_idx * columns
        spill = jnp.sum(jnp.where((lane >= low) & (lane < low + EXPERTS), over, 0.0), axis=1, keepdims=True)
        table = jnp.where(lane == low + EXPERTS, spill, table)
    high = table.astype(jnp.bfloat16).astype(jnp.float32)
    both = high + pltpu.roll(table - high, TICKS * columns, 1)
    out_ref[:, :width] = normed_rows(state_ref[...].astype(jnp.float32), gain_ref, 0)
    out_ref[:, width:] = both.astype(jnp.bfloat16)


def join_kernel(first_ref, second_ref, out_ref):
    out_ref[...] = jnp.concatenate([first_ref[...], second_ref[...]], axis=0)


def served(normed, gate, up, down, turned):
    contract = (((1,), (0 if turned else 1,)), ((), ()))
    gate_pre = lax.dot_general(normed, gate, contract, preferred_element_type=jnp.float32)
    up_pre = lax.dot_general(normed, up, contract, preferred_element_type=jnp.float32)
    hidden = (gate_pre / (1.0 + jnp.exp(-gate_pre)) * up_pre).astype(jnp.bfloat16)
    return jnp.dot(hidden, down, preferred_element_type=jnp.float32)


def either(second, bodies):
    if len(bodies) == 1:
        bodies[0]()
    elif bodies:
        pl.when(jnp.logical_not(second))(bodies[0])
        pl.when(second)(bodies[1])


def layer_kernel(*refs, tick_idx, blocks, layer_counts, tok_dev, width, carried, ends):
    row_refs, table_refs, refs = refs[:blocks], refs[blocks:2 * blocks], refs[2 * blocks:]
    own_ref, refs = refs[0], refs[1:]
    if carried:
        carried_ref, refs = refs[0], refs[1:]
    choices = []
    for slot_count, spare_count in layer_counts:
        slot, spare, refs = refs[:slot_count], refs[slot_count:slot_count + spare_count], refs[slot_count + spare_count:]
        choices.append((slot, [spare[0].at[i] for i in range(3)] if spare_count == 1 else spare))
    segments, members = lax.axis_size("segment"), lax.axis_size("expert")
    group = group_of(lax.axis_index("segment"), tick_idx, segments)
    expert = lax.axis_index("expert") // (members // EXPERTS)
    normed = jnp.concatenate([ref[:, :width] for ref in row_refs], axis=0)
    table = jnp.concatenate([ref[:, width:] for ref in table_refs], axis=0).astype(jnp.float32)
    lane = lax.broadcasted_iota(jnp.int32, table.shape, 1)
    columns = TICKS * (EXPERTS + 1)

    def column(at):
        return jnp.sum(jnp.where((lane == at) | (lane == at + columns), table, 0.0), axis=1, keepdims=True)

    share = column(tick_idx * (EXPERTS + 1) + expert)
    spill = column(tick_idx * (EXPERTS + 1) + EXPERTS)
    per = 2 * tok_dev

    def run(slot, spare):
        total = carried_ref[...] if carried else share * served(normed, *[ref[...] for ref in slot], True)
        if spare:
            total = total + spill * served(normed, *[ref[...] for ref in spare], False)
        if not ends:
            refs[0][...] = total
            return
        own = jnp.concatenate([own_ref[...].astype(jnp.float32), jnp.zeros((tok_dev, width), jnp.float32)], axis=0)
        refs[0][...] = total[0:per] + own
        for i in range(1, blocks):
            refs[i][...] = total[i * per:(i + 1) * per].astype(jnp.bfloat16)

    either(group == 1, [functools.partial(run, *choice) for choice in choices])


def resident(values):
    return [pltpu.with_memory_space_constraint(value, pltpu.VMEM) for value in values]


def run_layer(rows, tables, own, layers, *, tick_idx, tok_dev, carried=None, ends=True):
    blocks = len(rows)
    width = own.shape[-1]
    per = 2 * tok_dev
    values = [*rows, *tables, own]
    if carried is not None:
        values.append(carried)
    for slot, spare in layers:
        values += resident([*slot, *spare])
    slot, spare = layers[0]
    hidden = (slot[2].shape[0] if slot else 0) + (spare[-1].shape[-2] if spare else 0)
    whole = jax.ShapeDtypeStruct((per * blocks, width), jnp.float32)
    parts = [jax.ShapeDtypeStruct((per, width), jnp.float32)]
    parts += [jax.ShapeDtypeStruct((per, width), jnp.bfloat16)] * (blocks - 1)
    return pl.pallas_call(
        functools.partial(
            layer_kernel, tick_idx=tick_idx, blocks=blocks, tok_dev=tok_dev, width=width, ends=ends,
            layer_counts=[(len(slot), len(spare)) for slot, spare in layers], carried=carried is not None,
        ),
        out_shape=parts if ends else whole,
        in_specs=[WHOLE] * len(values),
        out_specs=[WHOLE] * blocks if ends else WHOLE,
        compiler_params=pltpu.CompilerParams(vmem_limit_bytes=12 * 1024 * 1024),
        cost_estimate=pl.CostEstimate(
            flops=6 * per * blocks * hidden * width, bytes_accessed=6 * hidden * width,
            transcendentals=per * blocks * hidden,
        ),
        name="layer",
    )(*values)


def sum_kernel(*refs):
    refs[-1][...] = added([ref[...] for ref in refs[:-1]]).astype(jnp.bfloat16)


def summed(values):
    shape = jax.ShapeDtypeStruct(values[0].shape, jnp.bfloat16)
    return small(sum_kernel, shape, *values)


def arrive_kernel(along_ref, across_ref, gain_ref, own_ref, normed_ref, *, tick_idx):
    across = across_ref[...].astype(jnp.float32)
    half = across.shape[0] // 2
    total = along_ref[...].astype(jnp.float32) + jnp.concatenate([across[half:], across[:half]], axis=0)
    total = total.astype(jnp.bfloat16)
    own_ref[...] = total[:half]
    normed_ref[...] = normed_rows(total.astype(jnp.float32), gain_ref, tick_idx)


def arriving(along, across, gain, tick_idx):
    rows, width = along.shape
    shapes = [jax.ShapeDtypeStruct((count, width), jnp.bfloat16) for count in (rows // 2, rows)]
    return small(functools.partial(arrive_kernel, tick_idx=tick_idx), shapes, along, across, gain)


def fill_kernel(*refs, group):
    count = len(refs) // 2
    ins, outs, sems = refs[:count], refs[count:2 * count], refs[2 * count]
    copies = [
        pltpu.make_async_copy(one if group is None else one.at[group], out, sems.at[i])
        for i, (one, out) in enumerate(zip(ins, outs))
    ]
    for copy in copies:
        copy.start()
    for copy in copies:
        copy.wait()


def filled(values, group=None):
    shapes = [value.shape if group is None else value.shape[1:] for value in values]
    return pl.pallas_call(
        functools.partial(fill_kernel, group=group),
        out_shape=[pltpu.VMEM(shape, value.dtype) for shape, value in zip(shapes, values)],
        in_specs=[pl.BlockSpec(memory_space=pltpu.HBM)] * len(values),
        out_specs=[WHOLE] * len(values),
        scratch_shapes=[pltpu.SemaphoreType.DMA((len(values),))],
        compiler_params=pltpu.CompilerParams(vmem_limit_bytes=1024 * 1024),
        name="fill",
    )(*[pltpu.with_memory_space_constraint(value, pltpu.HBM) for value in values])


def load_kernel(*refs, turned, group):
    count = len(turned)
    ins, outs, (held, sems, straight) = refs[:count], refs[count:2 * count], refs[2 * count:]
    depth, block = held.shape[:2]
    work = [
        (ins[i], outs[i], low) for i in range(count) if turned[i] for low in range(0, ins[i].shape[1], block)
    ]

    def copy_of(at):
        source, _, low = work[at]
        return pltpu.make_async_copy(source.at[group, pl.ds(low, block), :], held.at[at % depth], sems.at[at % depth])

    for at in range(min(depth - 1, len(work))):
        copy_of(at).start()
    direct = [
        pltpu.make_async_copy(ins[i].at[group], outs[i], straight.at[i]) for i in range(count) if not turned[i]
    ]
    for copy in direct:
        copy.start()
    for at, (_, out, low) in enumerate(work):
        if at + depth - 1 < len(work):
            copy_of(at + depth - 1).start()
        copy_of(at).wait()
        out[:, low:low + block] = held[at % depth].T
    for copy in direct:
        copy.wait()


def loaded(values, turned, group):
    hidden, width = values[0].shape[1:]
    block = LANES if hidden % LANES == 0 else hidden
    return pl.pallas_call(
        functools.partial(load_kernel, turned=turned, group=group),
        out_shape=[
            pltpu.VMEM((width, hidden) if flip else (hidden, width), value.dtype)
            for value, flip in zip(values, turned)
        ],
        in_specs=[pl.BlockSpec(memory_space=pltpu.HBM)] * len(values),
        out_specs=[WHOLE] * len(values),
        scratch_shapes=[
            pltpu.VMEM((4, block, width), values[0].dtype),
            pltpu.SemaphoreType.DMA((4,)),
            pltpu.SemaphoreType.DMA((len(values),)),
        ],
        compiler_params=pltpu.CompilerParams(vmem_limit_bytes=6 * 1024 * 1024),
        name="load",
    )(*[pltpu.with_memory_space_constraint(value, pltpu.HBM) for value in values])


def stack_kernel(*refs, group):
    ins, out, sems = refs[:-2], refs[-2], refs[-1]
    copies = [pltpu.make_async_copy(one.at[group], out.at[i], sems.at[i]) for i, one in enumerate(ins)]
    for copy in copies:
        copy.start()
    for copy in copies:
        copy.wait()


def stacked(values, group):
    shape = (len(values),) + values[0].shape[1:]
    return pl.pallas_call(
        functools.partial(stack_kernel, group=group),
        out_shape=pltpu.VMEM(shape, values[0].dtype),
        in_specs=[pl.BlockSpec(memory_space=pltpu.HBM)] * len(values),
        out_specs=WHOLE,
        scratch_shapes=[pltpu.SemaphoreType.DMA((len(values),))],
        compiler_params=pltpu.CompilerParams(vmem_limit_bytes=6 * 1024 * 1024),
        name="stack",
    )(*[pltpu.with_memory_space_constraint(value, pltpu.HBM) for value in values])


def both_first(outer):
    return [outer - 1, *range(1, outer - 1)]


def added(values):
    total = values[0].astype(jnp.float32)
    for value in values[1:]:
        total = total + value.astype(jnp.float32)
    return total


def on_device(
    state, routes, gates, norm_gain, w_gate, w_up, w_down, spare_gate, spare_up, spare_down
):
    segments = lax.axis_size("segment")
    segments, members = lax.axis_size("segment"), lax.axis_size("expert")
    outer = members // 2
    assert outer & (outer - 1) == 0
    tok_dev = state.shape[1]

    def spread(value):
        got = {j: moved(value, j, 0) for j in both_first(outer)}
        return [value] + [got[j] for j in range(1, outer)]

    weights = [w_gate[:, 0], w_up[:, 0], w_down[:, 0]]
    spare_all = [spare_gate[:, 0], spare_up[:, 0], spare_down[:, 0]]

    def fetched(values):
        return [moved(value, 0, -1) for value in values]

    head = filled(spare_all[:1], 0)
    head, rest, state, routes, gates = lax.optimization_barrier((head, spare_all[1:], state, routes, gates))
    spares = [fetched(head + filled(rest, 0))]
    shape = (tok_dev, state.shape[2] + LANES)
    own = small(
        prepare_kernel, jax.ShapeDtypeStruct(shape, state.dtype), state[0],
        jnp.transpose(routes[:, 0], (0, 2, 1)), jnp.transpose(gates[:, 0], (0, 2, 1)), norm_gain,
    )
    other = moved(own, outer, 0)
    pair = small(join_kernel, jax.ShapeDtypeStruct((2 * tok_dev, shape[1]), state.dtype), own, other)
    arrived = spread(pair)
    users = [later_users(tick_idx, segments) for tick_idx in range(TICKS)]
    opening = min([tick_idx for tick_idx in range(TICKS) if users[tick_idx]], default=TICKS)
    slots = [loaded(weights, (True, True, False), 0)]
    if users[0]:
        slots.append(loaded(weights, (True, True, False), 1))
    late = stacked(lax.optimization_barrier((*spare_all, arrived[both_first(outer)[-1]]))[:3], 1)
    near = [swapped(late, users[opening])] if opening < TICKS else []
    own = state[0]
    before = run_layer(arrived, arrived, own, [(slot, []) for slot in slots], tick_idx=0, tok_dev=tok_dev, ends=False)

    rows = arrived
    for tick_idx in range(TICKS):
        layers = [(slots[0], spares[0])]
        if users[tick_idx]:
            layers.append((slots[1], near if users[tick_idx] <= users[opening] else far))
        if tick_idx == 0:
            layers = [([], spare) for _, spare in layers]
        parts = run_layer(
            rows, arrived, own, layers, tick_idx=tick_idx, tok_dev=tok_dev,
            carried=before if tick_idx == 0 else None,
        )
        got = [moved(parts[j], j, 0) for j in both_first(outer)]
        if tick_idx == 0:
            far = [moved(lax.optimization_barrier((late, parts[0]))[0], 0, -1)]
        if tick_idx == 0 and not users[0]:
            tied = lax.optimization_barrier((*weights, parts[0]))[:3]
            gate = loaded(tied[:1], (True,), 1)
        if tick_idx + 1 == TICKS:
            total = added([parts[0]] + got)
            other = moved(total[tok_dev:].astype(jnp.bfloat16), outer, 0)
            return added([total[:tok_dev], other]).astype(jnp.bfloat16)[None]
        total = summed([parts[0]] + got)
        across = moved(total, outer, 1)
        along = moved(total, 0, 1)
        if tick_idx == 0:
            if not users[0]:
                tied = lax.optimization_barrier((*weights, parts[0]))[:3]
                slots.append(gate + loaded(tied[1:], (True, False), 1))
        own, normed = arriving(along, across, norm_gain, tick_idx + 1)
        rows = spread(normed)


def solution(mesh):
    return jax.shard_map(
        on_device,
        mesh=mesh,
        in_specs=(
            P("segment", "expert", None),
            P(None, "segment", "expert", None),
            P(None, "segment", "expert", None),
            P(None, "segment", None),
            P(None, "segment", "expert", None),
            P(None, "segment", "expert", None),
            P(None, "segment", "expert", None),
            P(None, "segment", "expert", None),
            P(None, "segment", "expert", None),
            P(None, "segment", "expert", None),
        ),
        out_specs=P("segment", "expert", None),
        check_vma=False,
    )
```
